32 devices in a mesh: fsdp: 8 (over z, y), tp: 4 (over x, core).
Axes of the slice: x: 2, y: 2, z: 4, core: 2. Of those that a mesh axis runs over, the one named last changes fastest.
Arguments:
- tokens: bfloat16 [32768, 768], P(('fsdp', 'tp')), may hold values from -16 to 16
- segment_ids: int32 [32, 1024], P('fsdp'), may hold values from 0 to 7, never falling along the last dimension, each value on 1 to 512 neighbouring positions
- valid: int32 [32768], P(('fsdp', 'tp')), may hold values from 0 to 1, as said below
- ln1_gain: bfloat16 [768], P('fsdp'), may hold values from 0.5 to 1.5
- ln1_bias: bfloat16 [768], P('fsdp'), may hold values from -3 to 3
- w_qkv: bfloat16 [768, 3, 768], P('fsdp', None, 'tp'), may hold values from -0.21875 to 0.21875
- w_out: bfloat16 [768, 768], P('tp', 'fsdp'), may hold values from -1.75 to 1.75
- ln2_gain: bfloat16 [768], P('fsdp'), may hold values from 0.5 to 1.5
- ln2_bias: bfloat16 [768], P('fsdp'), may hold values from -3 to 3
- w_up: bfloat16 [768, 3072], P('fsdp', 'tp'), may hold values from -0.21875 to 0.21875
- w_down: bfloat16 [3072, 768], P('tp', 'fsdp'), may hold values from -0.109375 to 0.109375
- cotangent: bfloat16 [32768, 768], P(('fsdp', 'tp')), may hold values from -6 to 6
Outputs:
- layer_output: bfloat16 [32768, 768], P(('fsdp', 'tp'))
- grad_tokens: float32 [32768, 768], P(('fsdp', 'tp'))
- grad_ln1_gain: float32 [768], P(('fsdp', 'tp'))
- grad_ln1_bias: float32 [768], P(('fsdp', 'tp'))
- grad_w_qkv: float32 [768, 3, 768], P('fsdp', None, 'tp')
- grad_w_out: float32 [768, 768], P('tp', 'fsdp')
- grad_ln2_gain: float32 [768], P(('fsdp', 'tp'))
- grad_ln2_bias: float32 [768], P(('fsdp', 'tp'))
- grad_w_up: float32 [768, 3072], P('fsdp', 'tp')
- grad_w_down: float32 [3072, 768], P('tp', 'fsdp')
- rms_values: float32 [3], replicated
The draws below stay inside these ranges and needn't reach their ends.
Inputs may be any that keep to these rules, and one draw needn't show every extreme that they name: `segment_ids`: document numbers never fall along a sequence; each document has 1 to half of 1024 tokens. The first token of every sequence is valid.
All inputs are finite; a program needn't handle non-finite values.
Results may differ from the reference program's by a relative error of at most 0.018.
Values may be sent and summed in bfloat16 or wider, within the bound.
A program may use at most 192 MiB of HBM per device.

```python
import math
import jax
import jax.numpy as jnp
import numpy as np
from jax import lax

D = 768
HEADS = 12
HD = 64
FF = 3072
SEQLEN = 1024
DOCS = 8
SEQS = 32
TOKENS = 32768
N_TP = 4


def draw_tokens(key, part):
    row = jnp.arange(TOKENS, dtype=jnp.float32)[:, None] / TOKENS
    base = jnp.clip(jax.random.normal(key, (TOKENS, D), jnp.float32), -4.0, 4.0)
    scale = 1.0 + 2.0 * row
    return (base * scale).astype(jnp.bfloat16)


def draw_valid(key, part):
    coin = jax.random.randint(jax.random.fold_in(key, 1), (TOKENS,), 0, 4)
    cutoff = jax.random.randint(jax.random.fold_in(key, 2), (), TOKENS // 4, TOKENS + 1)
    index = jnp.arange(TOKENS, dtype=jnp.int32)
    first = index % SEQLEN == 0
    return jnp.where(first | (coin > 0) & (index < cutoff), 1, 0).astype(jnp.int32)


def level_of(rng, extent, pieces, smallest, largest):
    level, own = 1.0, jax.random.fold_in(rng, 6)
    for dim, blocks in pieces:
        draws = jnp.exp(jax.random.uniform(jax.random.fold_in(own, dim), (blocks,), jnp.float32, smallest / len(pieces), largest / len(pieces)))
        level = level * jnp.repeat(draws, extent[dim] // blocks).reshape([-1 if axis == dim else 1 for axis in range(len(extent))])
    return level


def split_up(amount, total, bound, slope):
    loads = [(1 << 20) // math.isqrt(rank ** slope) + 1 for rank in range(2, amount + 1)]
    spare, given = total - bound - (amount - 1), [1] * (amount - 1)
    while spare > 0:
        free = [i for i in range(amount - 1) if given[i] < bound]
        whole, remaining = sum([loads[i] for i in free]), spare
        for i in free:
            extra = min(bound - given[i], max(1, remaining * loads[i] // whole), spare)
            given[i] = given[i] + extra
            spare = spare - extra
    return np.array([bound] + given)


def ragged_sizes(own_key, count, total, limit, lean):
    if count == 2:
        one = jax.random.randint(own_key, (), max(1, total - limit), min(limit, total - 1) + 1)
        return jnp.stack([one, total - one])
    lengths = jnp.asarray(split_up(count, total, limit, lean), jnp.int32)
    twos = (count - 1) // 2
    giver, receiver = lengths[1:1 + 2 * twos:2], lengths[2:2 + 2 * twos:2]
    slack = jnp.minimum(giver - 1, limit - receiver)
    moved = jax.random.randint(jax.random.fold_in(own_key, 1), (twos,), 0, 1 << 20) % (slack + 1)
    lengths = lengths.at[1:1 + 2 * twos:2].set(giver - moved).at[2:2 + 2 * twos:2].set(receiver + moved)
    return lengths[jax.random.permutation(jax.random.fold_in(own_key, 2), count)]


def bell_draw(own_key, shape, scale, reach, pieces=(), kind=jnp.bfloat16):
    values = jax.random.normal(own_key, shape, jnp.float32) * scale
    if len(pieces) > 0:
        values = level_of(own_key, shape, pieces, -0.22, 0.18) * values
    return jnp.clip(values, min=-reach, max=reach).astype(kind)


def setup_inputs(seed: int = 0) -> dict:
    keys = jax.random.split(jax.random.key(seed), 13)
    tokens = draw_tokens(jax.random.fold_in(keys[12], 71), 0)
    segment_ids = jax.vmap(lambda own: jnp.searchsorted(jnp.cumsum(ragged_sizes(own, DOCS, SEQLEN, SEQLEN // 2, 2)), jnp.arange(SEQLEN), side="right"))(jax.random.split(keys[1], SEQS)).reshape((SEQS, SEQLEN)).astype(jnp.int32)
    valid = draw_valid(jax.random.fold_in(keys[12], 71), 0)
    ln1_gain = jnp.clip(1.0 + 0.1 * jax.random.normal(keys[3], (D,), jnp.float32), 0.5, 1.5).astype(jnp.bfloat16)
    ln1_bias = bell_draw(keys[4], (D,), 0.5, 3.0, ((0, 8),))
    w_qkv = bell_draw(keys[5], (D, 3, D), D ** -0.5, 0.21875, ((0, 8), (2, 4)))
    w_out = bell_draw(keys[6], (D, D), (max(D // 64, D * DOCS // SEQLEN // 2)) ** -0.5, 1.75, ((0, 4), (1, 8)))
    ln2_gain = jnp.clip(1.0 + 0.1 * jax.random.normal(keys[7], (D,), jnp.float32), 0.5, 1.5).astype(jnp.bfloat16)
    ln2_bias = bell_draw(keys[8], (D,), 0.5, 3.0, ((0, 8),))
    w_up = bell_draw(keys[9], (D, FF), D ** -0.5, 0.21875, ((0, 8), (1, 4)))
    w_down = bell_draw(keys[10], (FF, D), FF ** -0.5, 0.109375, ((0, 4), (1, 8)))
    cotangent = bell_draw(keys[11], (TOKENS, D), 1.0, 6.0, ((0, 32),))
    return dict(tokens=tokens, segment_ids=segment_ids, valid=valid, ln1_gain=ln1_gain, ln1_bias=ln1_bias, w_qkv=w_qkv, w_out=w_out, ln2_gain=ln2_gain, ln2_bias=ln2_bias, w_up=w_up, w_down=w_down, cotangent=cotangent)


@jax.custom_vjp
def low(v):
    return lax.optimization_barrier(v.astype(jnp.bfloat16)).astype(jnp.float32)

@jax.custom_vjp
def low_back(v):
    return v

def low_keep(v):
    return (low(v), None)

def low_pass(kept, grad):
    return (grad,)

def back_keep(v):
    return (v, None)

def back_low(kept, grad):
    return (low(grad),)
low.defvjp(low_keep, low_pass)
low_back.defvjp(back_keep, back_low)
highest = lax.Precision.HIGHEST
epsilon = 1e-05
negative = -1e+30

def layer_norm(values, gain, shift):
    center = values - lax.optimization_barrier(jnp.mean(values, axis=-1, keepdims=True))
    variance = lax.optimization_barrier(jnp.mean(center * center, axis=-1, keepdims=True))
    return center * lax.rsqrt(variance + epsilon) * gain + shift

def attend_sequence(pair):
    triple, segment = pair
    query = triple[:, 0]
    key = triple[:, 1]
    value = triple[:, 2]
    scores = jnp.einsum('qhd,khd->hqk', query, key, precision=highest) * HD ** (-0.5)
    scores = low_back(scores)
    position = jnp.arange(SEQLEN, dtype=jnp.int32)
    allowed = (position[:, None] >= position[None, :]) & (segment[:, None] == segment[None, :])
    scores = jnp.where(allowed[None], scores, negative)
    probs = low(jax.nn.softmax(scores, axis=-1))
    return jnp.einsum('hqk,khd->qhd', probs, value, precision=highest)

def group_forward(block, segment, params):
    gain_one, shift_one, qkv_weight, out_weight, gain_two, shift_two, up_weight, down_weight = params
    count = block.shape[0] // SEQLEN
    normed_one = low(layer_norm(block, gain_one, shift_one))
    triples = jnp.dot(normed_one, qkv_weight.reshape(D, 3 * D), precision=highest)
    triples = low_back(low(triples)).reshape(count, SEQLEN, 3, HEADS, HD)
    context = lax.map(jax.checkpoint(attend_sequence), (triples, segment))
    context = low_back(low(context.reshape(count * SEQLEN, D)))
    branch_attn = low_back(jnp.dot(context, out_weight, precision=highest))
    middle = block + branch_attn
    normed_two = low(layer_norm(middle, gain_two, shift_two))
    upper = low_back(jnp.dot(normed_two, up_weight, precision=highest))
    active = low(jax.nn.gelu(upper, approximate=True))
    branch_mlp = low_back(jnp.dot(active, down_weight, precision=highest))
    return (middle + branch_mlp, (branch_attn, branch_mlp))

def reference(tokens, segment_ids, valid, ln1_gain, ln1_bias, w_qkv, w_out, ln2_gain, ln2_bias, w_up, w_down, cotangent):
    weights = tuple((item.astype(jnp.float32) for item in (ln1_gain, ln1_bias, w_qkv, w_out, ln2_gain, ln2_bias, w_up, w_down)))
    rows = N_TP * SEQLEN
    groups = tokens.shape[0] // rows
    inputs = (tokens.reshape(groups, rows, D), segment_ids.reshape(groups, N_TP, SEQLEN), valid.reshape(groups, rows), cotangent.reshape(groups, rows, D))

    def step(carry, item):
        totals, sums = carry
        block, segment, mask, grad_block = item

        def forward(block_in, *params):
            return group_forward(block_in, segment, params)
        output, back, branches = jax.vjp(forward, block.astype(jnp.float32), *weights, has_aux=True)
        pulled = back(grad_block.astype(jnp.float32))
        totals = tuple((left + right for left, right in zip(totals, pulled[1:])))
        weight_rows = mask.astype(jnp.float32)[:, None]
        sums = sums + jnp.stack([jnp.sum(weight_rows * output * output), jnp.sum(weight_rows * branches[0] * branches[0]), jnp.sum(weight_rows * branches[1] * branches[1])])
        return ((totals, sums), (output.astype(jnp.bfloat16), pulled[0]))
    start = (tuple((jnp.zeros_like(item) for item in weights)), jnp.zeros((3,), jnp.float32))
    (grads, sums), (outputs, grad_rows) = lax.scan(step, start, inputs)
    count = jnp.sum(valid).astype(jnp.float32)
    rms_values = jnp.sqrt(sums / (count * D))
    return (outputs.reshape(groups * rows, D), grad_rows.reshape(groups * rows, D), grads[0], grads[1], grads[2], grads[3], grads[4], grads[5], grads[6], grads[7], rms_values)
```

```python
from functools import partial

import jax
import jax.numpy as jnp
from jax import lax
from jax.experimental import pallas as pl
from jax.experimental.pallas import tpu as pltpu
from jax.sharding import PartitionSpec as P

HD = 64
BQ = 256
EPS = 1e-05
BIG = -1e30
F32 = jnp.float32
BF = jnp.bfloat16
NN = (((1,), (0,)), ((), ()))
NT = (((1,), (1,)), ((), ()))
TN = (((0,), (0,)), ((), ()))
MESH = pl.DeviceIdType.MESH
C0 = 0.7978845608
C1 = 0.7978845608 * 0.044715


def dot(a, b, dims=NN):
    return lax.dot_general(a, b, dims, preferred_element_type=F32)


def remote(src, dst, send, recv, device):
    return pltpu.make_async_remote_copy(
        src_ref=src, dst_ref=dst, send_sem=send, recv_sem=recv,
        device_id=device, device_id_type=MESH,
    )


class Place:
    def __init__(self, inner):
        f = lax.axis_index("fsdp")
        t = lax.axis_index("tp")
        g = f // inner
        self.low = f % inner
        self.inner = inner
        self.z, self.y, self.x, self.c = g // 2, g % 2, t // 2, t % 2

    def device(self, z, y, x, c):
        return ((z * 2 + y) * self.inner + self.low, x * 2 + c)

    def core(self):
        return self.device(self.z, self.y, self.x, 1 - self.c)

    def xn(self):
        return self.device(self.z, self.y, 1 - self.x, self.c)

    def yn(self):
        return self.device(self.z, 1 - self.y, self.x, self.c)

    def zn(self, d):
        return self.device((self.z + d) % 4, self.y, self.x, self.c)

    def zp(self, d):
        return self.device((self.z - d + 4) % 4, self.y, self.x, self.c)


def barrier(inner):
    p = Place(inner)
    sem = pltpu.get_barrier_semaphore()
    for dev in (p.core(), p.xn(), p.yn(), p.zn(1), p.zn(2), p.zn(3)):
        pl.semaphore_signal(sem, inc=1, device_id=dev, device_id_type=MESH)
    pl.semaphore_wait(sem, 6)


class Gather:
    def __init__(self, inner, buf, row0, rows, send, recv):
        self.inner, self.buf, self.row0, self.rows = inner, buf, row0, rows
        self.send, self.recv = send, recv

    def own(self, x, c, z, y):
        return self.buf.at[x, c, z, y, pl.ds(self.row0, self.rows)]

    def group(self, x, c, y, half=None):
        start, size = self.row0, self.rows
        if half is not None:
            size = self.rows // 2
            start = self.row0 + half * size
        return self.buf.at[x, c, :, y, pl.ds(start, size)]

    def parts(self, slot):
        p = Place(self.inner)
        x, c, z, y = p.x, p.c, p.z, p.y
        if slot < 3:
            d = slot + 1
            return self.own(x, c, z, y), self.own(x, c, (z - d + 4) % 4, y), p.zn(d)
        if slot == 3:
            return self.group(x, c, y), self.group(1 - x, c, y), p.xn()
        if slot == 4:
            return self.group(x, c, y), self.group(x, c, 1 - y), p.yn()
        if slot == 5:
            return self.group(1 - x, c, y, 0), self.group(1 - x, c, 1 - y, 0), p.yn()
        if slot == 6:
            return self.group(x, c, 1 - y, 1), self.group(1 - x, c, 1 - y, 1), p.xn()
        xx = x if slot in (7, 9) else 1 - x
        yy = y if slot in (7, 8) else 1 - y
        return self.group(xx, c, yy), self.group(xx, 1 - c, yy), p.core()

    def start(self, *slots):
        for slot in slots:
            mine, _, dev = self.parts(slot)
            remote(mine, mine, self.send.at[slot], self.recv.at[slot], dev).start()

    def arrive(self, *slots):
        for slot in slots:
            _, theirs, dev = self.parts(slot)
            remote(theirs, theirs, self.send.at[slot], self.recv.at[slot], dev).wait_recv()

    def left(self, *slots):
        for slot in slots:
            mine, _, dev = self.parts(slot)
            remote(mine, mine, self.send.at[slot], self.recv.at[slot], dev).wait_send()

    def s1(self):
        self.start(0, 1, 2)

    def s2(self):
        self.arrive(0, 1, 2)
        self.start(3, 4, 7)

    def s3(self):
        self.arrive(3)
        self.start(5, 8)
        self.arrive(4)
        self.start(6, 9)

    def s4(self):
        self.arrive(5, 6)
        self.start(10)

    def s5(self):
        self.arrive(7, 8, 9, 10)

    def s6(self):
        self.left(*range(11))


class Scatter:
    def __init__(self, inner, buf, rows, slots, send, recv, credit, out):
        self.inner, self.buf, self.rows = inner, buf, rows
        self.slots, self.send, self.recv = slots, send, recv
        self.credit, self.out = credit, out

    def parts(self, slot):
        p = Place(self.inner)
        x, c, z, y = p.x, p.c, p.z, p.y
        buf, half = self.buf, self.rows // 2
        r1, ra, rb, rx, ry, rz = self.slots
        whole, cut = pl.ds(0, self.rows), pl.ds(0, half)
        if slot == 0:
            return buf.at[:, 1 - c], r1.at[:, :, :, whole], p.core()
        if slot == 1:
            return buf.at[1 - x, c, :, 1 - y, pl.ds(0, half)], ra.at[:, cut], p.yn()
        if slot == 2:
            return buf.at[1 - x, c, :, 1 - y, pl.ds(half, half)], rb.at[:, cut], p.xn()
        if slot == 3:
            return buf.at[1 - x, c, :, y], rx.at[:, whole], p.xn()
        if slot == 4:
            return buf.at[x, c, :, 1 - y], ry.at[:, whole], p.yn()
        d = slot - 4
        return buf.at[x, c, (z + d) % 4, y], rz.at[d - 1, whole], p.zn(d)

    def start(self, *slots):
        for slot in slots:
            src, dst, dev = self.parts(slot)
            remote(src, dst, self.send.at[slot], self.recv.at[slot], dev).start()

    def arrive(self, *slots):
        for slot in slots:
            _, dst, dev = self.parts(slot)
            remote(dst, dst, self.send.at[slot], self.recv.at[slot], dev).wait_recv()

    def left(self):
        for slot in range(8):
            src, dst, dev = self.parts(slot)
            remote(src, dst, self.send.at[slot], self.recv.at[slot], dev).wait_send()

    def take_credit(self):
        for i in range(6):
            pl.semaphore_wait(self.credit.at[i], 1)

    def give_credit(self):
        p = Place(self.inner)
        for i, dev in enumerate((p.core(), p.xn(), p.yn(), p.zp(1), p.zp(2), p.zp(3))):
            pl.semaphore_signal(self.credit.at[i], inc=1, device_id=dev, device_id_type=MESH)

    def s1(self):
        self.start(0)

    def add_core(self, x, y):
        c = Place(self.inner).c
        r1 = self.slots[0]

        @pl.loop(0, 4)
        def _(z):
            got = r1[x, z, y, 0 : self.rows].astype(F32)
            self.buf[x, c, z, y] = (self.buf[x, c, z, y].astype(F32) + got).astype(BF)

    def s2(self):
        p = Place(self.inner)
        x, y = p.x, p.y
        self.arrive(0)
        self.add_core(1 - x, 1 - y)
        self.start(1, 2)
        self.add_core(1 - x, y)
        self.add_core(x, 1 - y)
        self.add_core(x, y)

    def s3(self):
        p = Place(self.inner)
        x, y, c = p.x, p.y, p.c
        buf, half = self.buf, self.rows // 2
        _, ra, rb, _, _, _ = self.slots
        self.arrive(1)

        @pl.loop(0, 4)
        def _(z):
            one = buf[1 - x, c, z, y, 0:half].astype(F32) + ra[z, 0:half].astype(F32)
            buf[1 - x, c, z, y, 0:half] = one.astype(BF)

        self.start(3)
        self.arrive(2)

        @pl.loop(0, 4)
        def _(z):
            two = buf[x, c, z, 1 - y, half : 2 * half].astype(F32) + rb[z, 0:half].astype(F32)
            buf[x, c, z, 1 - y, half : 2 * half] = two.astype(BF)

        self.start(4)

    def s4(self):
        p = Place(self.inner)
        x, y, c = p.x, p.y, p.c
        buf, rows = self.buf, self.rows
        _, _, _, rx, ry, _ = self.slots
        self.arrive(3, 4)

        @pl.loop(0, 4)
        def _(z):
            one = rx[z, 0:rows].astype(F32) + ry[z, 0:rows].astype(F32)
            buf[x, c, z, y] = (buf[x, c, z, y].astype(F32) + one).astype(BF)

        self.start(5, 6, 7)

    def s5(self):
        p = Place(self.inner)
        rows = self.rows
        rz = self.slots[5]
        self.arrive(5, 6, 7)
        total = self.buf[p.x, p.c, p.z, p.y].astype(F32)
        for d in range(3):
            total = total + rz[d, 0:rows].astype(F32)
        self.out[...] = total
        self.left()


class Total:
    def __init__(self, inner, ref, got, send, recv):
        self.inner, self.ref, self.got, self.send, self.recv = inner, ref, got, send, recv

    def copy(self, slot):
        p = Place(self.inner)
        dev = (p.core, p.xn, p.yn)[slot]() if slot < 3 else p.zn(slot - 2)
        stage = min(slot, 3)
        return remote(self.ref.at[stage], self.got.at[slot], self.send.at[slot], self.recv.at[slot], dev)

    def run(self, stage):
        slots = (stage,) if stage < 3 else (3, 4, 5)
        for slot in slots:
            self.copy(slot).start()

    def take(self, stage):
        slots = (stage,) if stage < 3 else (3, 4, 5)
        total = self.ref[stage]
        for slot in slots:
            self.copy(slot).wait_recv()
            total = total + self.got[slot]
        self.ref[stage + 1] = total

    def left(self):
        for slot in range(6):
            self.copy(slot).wait_send()


def head_parts(t_ref, k2_ref, t, h, qs, kr):
    if h < 2:
        return t_ref[t, qs, 0:128], t_ref[t, kr, 128:256], t_ref[t, kr, 256:384]
    return t_ref[t, qs, 384:512], k2_ref[kr, :], t_ref[t, kr, 512:640]


def lanes():
    return lax.broadcasted_iota(jnp.int32, (1, 128), 1)


def roll_key(t_ref, k2_ref, t):
    k2_ref[...] = pltpu.roll(t_ref[t, :, 384:512].astype(F32), 64, 1).astype(BF)


def below(transposed):
    r = lax.broadcasted_iota(jnp.int32, (BQ, BQ), 0)
    c = lax.broadcasted_iota(jnp.int32, (BQ, BQ), 1)
    return r <= c if transposed else r >= c


def attend(t_ref, l_ref, kx_ref, k2_ref, c_ref, t, length):
    lane = lanes()
    low = lane < 64
    roll_key(t_ref, k2_ref, t)
    for i in range(length // BQ):
        first = max(0, i * BQ - length // 2)
        width = (i + 1) * BQ - first
        qs, kr = slice(i * BQ, (i + 1) * BQ), slice(first, first + width)
        kx = kx_ref[kr, :]
        doc = kx_ref[qs, :].astype(F32)
        qx = jnp.where(lane < 8, BIG * (1.0 - doc), 0.0).astype(BF)
        marks = qx
        outs = []
        for h in range(3):
            q, k, v = head_parts(t_ref, k2_ref, t, h, qs, kr)
            keep = jnp.logical_not(low) if h == 1 else low
            q = jnp.where(keep, q * BF(HD ** -0.5), BF(0))
            s = dot(jnp.concatenate([q, qx], 1), jnp.concatenate([k, kx], 1), NT)
            edge = jnp.where(below(False), s[:, width - BQ :], BIG)
            s = edge if width == BQ else jnp.concatenate([s[:, : width - BQ], edge], 1)
            top = jnp.max(s, axis=1, keepdims=True)
            p = jnp.exp(s - top).astype(BF)
            both = dot(p, jnp.concatenate([v, jnp.ones((width, 128), BF)], 1))
            total = both[:, 128:256]
            outs.append(both[:, :128] / total)
            rest = -(top + jnp.log(total))
            for n in range(3):
                piece = rest.astype(BF)
                marks = jnp.where(lane == 8 + 16 * h + n, piece, marks)
                rest = rest - piece.astype(F32)
        l_ref[t, qs, :] = marks
        c_ref[t, qs, 0:128] = jnp.where(low, outs[0], outs[1]).astype(BF)
        c_ref[t, qs, 128:256] = jnp.where(low, outs[2], 0.0).astype(BF)


def attend_back(t_ref, l_ref, kx_ref, k2_ref, c_ref, do_ref, sums, t, length):
    lane = lanes()
    low = lane < 64
    dk_ref, dv_ref, dk2_ref, dv2_ref = sums
    roll_key(t_ref, k2_ref, t)
    for ref in sums:
        ref[...] = jnp.zeros_like(ref)
    for i in range(length // BQ):
        first = max(0, i * BQ - length // 2)
        width = (i + 1) * BQ - first
        qs, kr = slice(i * BQ, (i + 1) * BQ), slice(first, first + width)
        marks = l_ref[t, qs, :]
        kx = kx_ref[kr, :]
        minus = jnp.full((width, 128), -1.0, BF)
        grads = []
        for h in range(3):
            q, k, v = head_parts(t_ref, k2_ref, t, h, qs, kr)
            keep = jnp.logical_not(low) if h == 1 else low
            side = slice(0, 128) if h < 2 else slice(128, 256)
            q = jnp.where(keep, q * BF(HD ** -0.5), BF(0))
            do = jnp.where(keep, do_ref[t, qs, side], BF(0))
            km = jnp.where(keep, k, BF(0))
            dd = (do.astype(F32) * c_ref[t, qs, side].astype(F32)).astype(BF)
            mine = (lane < 8) | ((lane >= 8 + 16 * h) & (lane < 24 + 16 * h))
            qe = jnp.concatenate([q, jnp.where(mine, marks, BF(0))], 1)
            s = dot(jnp.concatenate([k, kx], 1), qe, NT)
            dp = dot(jnp.concatenate([v, minus], 1), jnp.concatenate([do, dd], 1), NT)
            edge = jnp.where(below(True), s[width - BQ :], BIG)
            s = edge if width == BQ else jnp.concatenate([s[: width - BQ], edge], 0)
            p = jnp.exp(s)
            ds = (p * dp).astype(BF)
            grads.append(dot(ds, km, TN))
            gv, gk = dot(p.astype(BF), do), dot(ds, q)
            if h < 2:
                dk_ref[kr, :] += gk
                dv_ref[kr, :] += gv
            else:
                dk2_ref[kr, :] += gk
                dv2_ref[kr, :] += gv
        t_ref[t, qs, 0:128] = ((grads[0] + grads[1]) * HD ** -0.5).astype(BF)
        t_ref[t, qs, 384:512] = jnp.where(low, (grads[2] * HD ** -0.5).astype(BF), t_ref[t, qs, 384:512])
    t_ref[t, :, 128:256] = dk_ref[...].astype(BF)
    t_ref[t, :, 256:384] = dv_ref[...].astype(BF)
    t_ref[t, :, 384:512] = jnp.where(low, t_ref[t, :, 384:512], pltpu.roll(dk2_ref[...], 64, 1).astype(BF))
    t_ref[t, :, 512:640] = dv2_ref[...].astype(BF)


def stats(v):
    mean = jnp.mean(v, axis=-1, keepdims=True)
    center = v - mean
    scale = lax.rsqrt(jnp.mean(center * center, axis=-1, keepdims=True) + EPS)
    return center * scale, scale


def norm_back(v, q, gain):
    n, scale = stats(v)
    e = q * gain
    back = scale * (e - jnp.mean(e, -1, keepdims=True) - n * jnp.mean(e * n, -1, keepdims=True))
    return back, jnp.sum(q * n, 0, keepdims=True), jnp.sum(q, 0, keepdims=True)


def kernel(
    inner, length,
    tok, cot, seg, valid, wq_in, wo_in, wm_in,
    lo_out, gt_out, gq_out, go_out, gm_out, ar_out,
    bq, bo, bm0, bm1, bm2,
    n1, tt, cc, ll, kx, k2, mid, n2, acc, gn, act, gu, val, par,
    dk, dv, dk2, dv2,
    m_sets, q_set, ar, ar_got,
    ag_send, ag_recv, rs_send, rs_recv, credit, ar_send, ar_recv, local_sem,
):
    width = tok.shape[1]
    bm = (bm0, bm1, bm2)
    blocks = [(bq, 0, 32), (bq, 32, 32), (bq, 64, 32), (bo, 0, 96)] + [(b, 0, 192) for b in bm]
    gathers = [Gather(inner, b, r0, rows, ag_send.at[k], ag_recv.at[k]) for k, (b, r0, rows) in enumerate(blocks)]
    here = Place(inner)

    def fills():
        at = (here.x, here.c, here.z, here.y)
        pairs = [(wq_in, bq), (wo_in, bo)] + [(wm_in.at[j], bm[j]) for j in range(3)]
        return [pltpu.make_async_copy(src, b.at[at], local_sem.at[k]) for k, (src, b) in enumerate(pairs)]

    for one in fills():
        one.start()
    barrier(inner)
    for one in fills():
        one.wait()

    for g in gathers:
        g.s1()
    for g in gathers:
        g.s2()
        g.s3()
        g.s4()
    for g in gathers:
        g.s5()
        g.s6()

    def rows_of(i, size):
        return pl.ds(pl.multiple_of(i * size, size), size)

    def weight(buf, t, r0, rows, columns):
        return buf[t // 2, t % 2, :, :, r0 : r0 + rows, columns].reshape(8 * rows, -1)

    par[...] = bq[0, 0, :, :, :, 512:640].reshape(width, 128).astype(F32).T
    me_t = lax.axis_index("tp")
    row = seg[pl.ds(me_t, 1), :].astype(F32)
    lane_id = lax.broadcasted_iota(jnp.int32, (128, length), 0)
    marks = jnp.where(row == lane_id.astype(F32), 1.0, 0.0)
    marks = jnp.where(lane_id < 8, marks, 0.0)
    low4 = lane_id % 16
    ones = (lane_id >= 8) & (lane_id < 56) & (low4 >= 8) & (low4 < 11)
    marks = jnp.where(ones, 1.0, marks)
    marks = jnp.where(lane_id == 64, valid[...].astype(F32), marks)
    columns = marks.T
    val[...] = columns[:, 64:65]
    kx[...] = jnp.where(lanes() < 64, columns, 0.0).astype(BF)
    ar[0] = jnp.zeros_like(ar.at[0])
    ar[0, 7:8, 0:128] = jnp.broadcast_to(jnp.sum(valid[...].astype(F32), axis=1, keepdims=True), (1, 128))

    @pl.loop(0, length // 256)
    def _(i):
        s = rows_of(i, 256)
        n, _ = stats(tok[s, :].astype(F32))
        n1[s, :] = (n * par[64:65, :] + par[65:66, :]).astype(BF)

    @pl.loop(0, 4)
    def _(t):
        w = weight(bq, t, 0, 96, slice(0, 640))

        @pl.loop(0, length // 512)
        def _(i):
            s = rows_of(i, 512)
            tt[t, s, :] = dot(n1[s, :], w).astype(BF)

        attend(tt, ll, kx, k2, cc, t, length)

    @pl.loop(0, length // 256)
    def _(i):
        s = rows_of(i, 256)
        branch = jnp.zeros((256, width), F32)
        for t in range(4):
            branch = branch + dot(cc[t, s, :], weight(bo, t, 0, 96, slice(0, 256)), NT)
        v = tok[s, :].astype(F32) + branch
        mid[s, :] = v
        ar[0, 5:6, :] += jnp.sum(val[s, :] * (branch * branch), 0, keepdims=True)
        n, _ = stats(v)
        n2[s, :] = (n * par[66:67, :] + par[67:68, :]).astype(BF)

    for j in range(3):
        b = bm[j]

        @pl.loop(0, 4)
        def _(t):
            up = weight(b, t, 0, 96, slice(0, 256))
            down = weight(b, t, 96, 96, slice(0, 256))

            @pl.loop(0, length // 512)
            def _(i):
                s = rows_of(i, 512)
                v = dot(n2[s, :], up)
                ga = dot(cot[s, :], down)
                v2 = v * v
                th = jnp.tanh(v * (C0 + C1 * v2))
                h = 0.5 + 0.5 * th
                act[t, s, :] = (v * h).astype(BF)
                slope = h + (0.5 * v) * (1.0 - th * th) * (C0 + (3.0 * C1) * v2)
                gu[t, s, :] = (ga * slope).astype(BF)

        def cat(ref, s):
            return jnp.concatenate([ref[t, s, :] for t in range(4)], 1)

        def wcat(r0):
            return jnp.concatenate([weight(b, t, r0, 96, slice(0, 256)) for t in range(4)], 1)

        @pl.loop(0, length // 256)
        def _(i):
            s = rows_of(i, 256)
            one = dot(cat(act, s), wcat(96), NT)
            two = dot(cat(gu, s), wcat(0), NT)
            if j == 0:
                acc[s, :] = one
                gn[s, :] = two
            else:
                acc[s, :] += one
                gn[s, :] += two

        @pl.loop(0, 4)
        def _(t):
            gup = dot(n2[...], gu[t], TN).astype(BF)
            b[t // 2, t % 2, :, :, 0:96, :] = gup.reshape(4, 2, 96, 256)
            gdown = dot(cot[...], act[t], TN).astype(BF)
            b[t // 2, t % 2, :, :, 96:192, :] = gdown.reshape(4, 2, 96, 256)

    @pl.loop(0, length // 256)
    def _(i):
        s = rows_of(i, 256)
        v = mid[s, :]
        mlp = acc[s, :]
        out = v + mlp
        weight_rows = val[s, :]
        ar[0, 4:5, :] += jnp.sum(weight_rows * (out * out), 0, keepdims=True)
        ar[0, 6:7, :] += jnp.sum(weight_rows * (mlp * mlp), 0, keepdims=True)
        low_out = out.astype(BF)
        for k in range(width // 256):
            gu[k, s, :] = low_out[:, 256 * k : 256 * k + 256]
        back, g_gain, g_bias = norm_back(v, gn[s, :], par[66:67, :])
        ar[0, 2:3, :] += g_gain
        ar[0, 3:4, :] += g_bias
        grad = cot[s, :].astype(F32) + back
        mid[s, :] = grad
        n2[s, :] = grad.astype(BF)

    def store_low():
        return [
            pltpu.make_async_copy(gu.at[k], lo_out.at[:, pl.ds(256 * k, 256)], local_sem.at[k])
            for k in range(width // 256)
        ]

    for one in store_low():
        one.start()

    @pl.loop(0, 4)
    def _(t):
        w = weight(bo, t, 0, 96, slice(0, 256))
        act[t] = dot(n2[...], w).astype(BF)
        bo[t // 2, t % 2] = dot(n2[...], cc[t], TN).astype(BF).reshape(4, 2, 96, 256)

    @pl.loop(0, 4)
    def _(t):
        attend_back(tt, ll, kx, k2, cc, act, (dk, dv, dk2, dv2), t, length)

    @pl.loop(0, length // 256)
    def _(i):
        s = rows_of(i, 256)
        total = jnp.zeros((256, width), F32)
        for t in range(4):
            total = total + dot(tt[t, s, :], weight(bq, t, 0, 96, slice(0, 640)), NT)
        back, g_gain, g_bias = norm_back(tok[s, :].astype(F32), total, par[64:65, :])
        ar[0, 0:1, :] += g_gain
        ar[0, 1:2, :] += g_bias
        acc[s, :] = mid[s, :] + back

    def store_grad():
        return pltpu.make_async_copy(acc, gt_out, local_sem.at[4])

    store_grad().start()

    @pl.loop(0, 4)
    def _(t):
        bq[t // 2, t % 2] = dot(n1[...], tt[t], TN).astype(BF).reshape(4, 2, 96, 640)

    sets = [m_sets[0:6], m_sets[6:12]]
    plan = [(bm0, 192, sets[0], gm_out.at[0]), (bm1, 192, sets[1], gm_out.at[1]),
            (bm2, 192, sets[0], gm_out.at[2]), (bo, 96, sets[1], go_out), (bq, 96, q_set, gq_out)]
    scatters = [
        Scatter(inner, b, rows, slots, rs_send.at[k], rs_recv.at[k], credit.at[k], out)
        for k, (b, rows, slots, out) in enumerate(plan)
    ]
    for k, s in enumerate(scatters):
        if k in (2, 3):
            scatters[k - 2].take_credit()
        s.s1()
        s.s2()
        s.s3()
        s.s4()
        s.s5()
        if k in (0, 1):
            s.give_credit()
    total = Total(inner, ar, ar_got, ar_send, ar_recv)
    for stage in range(4):
        total.run(stage)
        total.take(stage)
    total.left()
    ar_out[...] = ar[4]
    for one in store_low():
        one.wait()
    store_grad().wait()


def scatter_slots(rows, columns):
    return [
        pltpu.VMEM((2, 4, 2, rows, columns), BF),
        pltpu.VMEM((4, rows // 2, columns), BF),
        pltpu.VMEM((4, rows // 2, columns), BF),
        pltpu.VMEM((4, rows, columns), BF),
        pltpu.VMEM((4, rows, columns), BF),
        pltpu.VMEM((3, rows, columns), BF),
    ]


def layer(inner, tokens, cotangent, segments, valid, wq, wo, wm):
    length, width = tokens.shape
    block = lambda rows, columns: pltpu.VMEM((2, 2, 4, 2, rows, columns), BF)
    scratch = [
        block(96, 640), block(96, 256), block(192, 256), block(192, 256), block(192, 256),
        pltpu.VMEM((length, width), BF),
        pltpu.VMEM((4, length, 640), BF),
        pltpu.VMEM((4, length, 256), BF),
        pltpu.VMEM((4, length, 128), BF),
        pltpu.VMEM((length, 128), BF),
        pltpu.VMEM((length, 128), BF),
        pltpu.VMEM((length, width), F32),
        pltpu.VMEM((length, width), BF),
        pltpu.VMEM((length, width), F32),
        pltpu.VMEM((length, width), F32),
        pltpu.VMEM((4, length, 256), BF),
        pltpu.VMEM((4, length, 256), BF),
        pltpu.VMEM((length, 1), F32),
        pltpu.VMEM((128, width), F32),
    ]
    scratch += [pltpu.VMEM((length, 128), F32)] * 4
    scratch += [scatter_slots(192, 256) + scatter_slots(192, 256), scatter_slots(96, 640)]
    scratch += [
        pltpu.VMEM((5, 8, width), F32),
        pltpu.VMEM((6, 8, width), F32),
        pltpu.SemaphoreType.DMA((7, 11)),
        pltpu.SemaphoreType.DMA((7, 11)),
        pltpu.SemaphoreType.DMA((5, 8)),
        pltpu.SemaphoreType.DMA((5, 8)),
        pltpu.SemaphoreType.REGULAR((2, 6)),
        pltpu.SemaphoreType.DMA((6,)),
        pltpu.SemaphoreType.DMA((6,)),
        pltpu.SemaphoreType.DMA((5,)),
    ]
    vmem, anywhere = pl.BlockSpec(memory_space=pltpu.VMEM), pl.BlockSpec(memory_space=pl.ANY)
    return pl.pallas_call(
        partial(kernel, inner, length),
        out_shape=(
            jax.ShapeDtypeStruct((length, width), BF),
            jax.ShapeDtypeStruct((length, width), F32),
            jax.ShapeDtypeStruct((96, 640), F32),
            jax.ShapeDtypeStruct((96, 256), F32),
            jax.ShapeDtypeStruct((3, 192, 256), F32),
            jax.ShapeDtypeStruct((8, width), F32),
        ),
        in_specs=[vmem] * 4 + [anywhere] * 3,
        out_specs=(anywhere, anywhere, vmem, vmem, vmem, vmem),
        scratch_shapes=scratch,
        compiler_params=pltpu.CompilerParams(
            collective_id=0, has_side_effects=True, vmem_limit_bytes=63 * 2**20
        ),
    )(tokens, cotangent, segments, valid, wq, wo, wm)


def local(
    tokens, segment_ids, valid, ln1_gain, ln1_bias, w_qkv, w_out, ln2_gain, ln2_bias, w_up, w_down, cotangent
):
    length, width = tokens.shape
    holders = lax.axis_size("fsdp")
    inner = holders // 8
    groups = [[g * inner + i for i in range(inner)] for g in range(8)]

    def widen(block):
        if inner == 1:
            return block
        return lax.all_gather(block, "fsdp", axis_index_groups=groups, axis=0, tiled=True)

    def narrow(block):
        if inner == 1:
            return block
        return lax.psum_scatter(
            block, "fsdp", scatter_dimension=0, axis_index_groups=groups, tiled=True
        )

    rows = w_up.shape[0]
    heads = w_qkv.reshape(rows, 3, 3, HD)
    pairs = heads[:, :, 0:2].reshape(rows, 3 * 2 * HD)
    odd = heads[:, :, 2].reshape(rows, 3 * HD)
    params = jnp.stack([ln1_gain, ln1_bias, ln2_gain, ln2_bias], axis=1)
    wq = widen(jnp.concatenate([pairs, odd, params, jnp.zeros((rows, 60), BF)], axis=1))
    wo = widen(jnp.pad(w_out.T, ((0, 0), (0, 64))))
    up = widen(w_up).reshape(rows * inner, 3, 256)
    down = widen(w_down.T).reshape(rows * inner, 3, 256)
    wm = jnp.concatenate([up, down], axis=0).transpose(1, 0, 2)

    low, grad_tokens, gq, go, gm, sums = layer(
        inner, tokens, cotangent, segment_ids, valid.reshape(1, length), wq, wo, wm
    )

    gq = narrow(gq[:, : 9 * HD])
    pair = gq[:, : 6 * HD].reshape(rows, 3, 2 * HD)
    one = gq[:, 6 * HD : 9 * HD].reshape(rows, 3, HD)
    grad_qkv = jnp.concatenate([pair, one], axis=2)
    grad_out = narrow(go[:, : 3 * HD]).T
    gm = gm.transpose(1, 0, 2).reshape(192, 768)
    grad_up = narrow(gm[:96])
    grad_down = narrow(gm[96:]).T
    if inner > 1:
        sums = lax.psum(sums, "fsdp", axis_index_groups=groups)
    share = width // (holders * lax.axis_size("tp"))
    owner = lax.axis_index("fsdp") * lax.axis_size("tp") + lax.axis_index("tp")
    mine = lax.dynamic_slice_in_dim(sums[0:4], owner * share, share, 1)
    spread = jnp.sqrt(jnp.sum(sums[4:7], axis=1) / (sums[7, 0] * width))
    return (
        low, grad_tokens, mine[0], mine[1], grad_qkv, grad_out, mine[2], mine[3], grad_up, grad_down, spread
    )


def solution(mesh):
    both = ("fsdp", "tp")
    return jax.shard_map(
        local,
        mesh=mesh,
        in_specs=(
            P(both, None), P("fsdp", None), P(both), P("fsdp"), P("fsdp"), P("fsdp", None, "tp"),
            P("tp", "fsdp"), P("fsdp"), P("fsdp"), P("fsdp", "tp"), P("tp", "fsdp"), P(both, None),
        ),
        out_specs=(
            P(both, None), P(both, None), P(both), P(both), P("fsdp", None, "tp"), P("tp", "fsdp"),
            P(both), P(both), P("fsdp", "tp"), P("tp", "fsdp"), P(),
        ),
        check_vma=False,
    )
```

```python
from functools import partial

import jax
import jax.numpy as jnp
from jax import lax
from jax.experimental import pallas as pl
from jax.experimental.pallas import tpu as pltpu
from jax.sharding import PartitionSpec as P

HD = 64
BQ = 256
EPS = 1e-05
BIG = -1e30
F32 = jnp.float32
BF = jnp.bfloat16
NN = (((1,), (0,)), ((), ()))
NT = (((1,), (1,)), ((), ()))
TN = (((0,), (0,)), ((), ()))
MESH = pl.DeviceIdType.MESH
C0 = 0.7978845608
C1 = 0.7978845608 * 0.044715


def dot(a, b, dims=NN):
    return lax.dot_general(a, b, dims, preferred_element_type=F32)


def remote(src, dst, send, recv, device):
    return pltpu.make_async_remote_copy(
        src_ref=src, dst_ref=dst, send_sem=send, recv_sem=recv,
        device_id=device, device_id_type=MESH,
    )


class Place:
    def __init__(self, inner):
        f = lax.axis_index("fsdp")
        t = lax.axis_index("tp")
        g = f // inner
        self.low = f % inner
        self.inner = inner
        self.z, self.y, self.x, self.c = g // 2, g % 2, t // 2, t % 2

    def device(self, z, y, x, c):
        return ((z * 2 + y) * self.inner + self.low, x * 2 + c)

    def core(self):
        return self.device(self.z, self.y, self.x, 1 - self.c)

    def xn(self):
        return self.device(self.z, self.y, 1 - self.x, self.c)

    def yn(self):
        return self.device(self.z, 1 - self.y, self.x, self.c)

    def zn(self, d):
        return self.device((self.z + d) % 4, self.y, self.x, self.c)

    def zp(self, d):
        return self.device((self.z - d + 4) % 4, self.y, self.x, self.c)


def barrier(inner):
    p = Place(inner)
    sem = pltpu.get_barrier_semaphore()
    for dev in (p.core(), p.xn(), p.yn(), p.zn(1), p.zn(2), p.zn(3)):
        pl.semaphore_signal(sem, inc=1, device_id=dev, device_id_type=MESH)
    pl.semaphore_wait(sem, 6)


class Gather:
    def __init__(self, inner, buf, row0, rows, send, recv):
        self.inner, self.buf, self.row0, self.rows = inner, buf, row0, rows
        self.send, self.recv = send, recv

    def own(self, x, c, z, y):
        return self.buf.at[x, c, z, y, pl.ds(self.row0, self.rows)]

    def group(self, x, c, y, half=None):
        start, size = self.row0, self.rows
        if half is not None:
            size = self.rows // 2
            start = self.row0 + half * size
        return self.buf.at[x, c, :, y, pl.ds(start, size)]

    def parts(self, slot):
        p = Place(self.inner)
        x, c, z, y = p.x, p.c, p.z, p.y
        if slot < 3:
            d = slot + 1
            return self.own(x, c, z, y), self.own(x, c, (z - d + 4) % 4, y), p.zn(d)
        if slot == 3:
            return self.group(x, c, y), self.group(1 - x, c, y), p.xn()
        if slot == 4:
            return self.group(x, c, y), self.group(x, c, 1 - y), p.yn()
        if slot == 5:
            return self.group(1 - x, c, y, 0), self.group(1 - x, c, 1 - y, 0), p.yn()
        if slot == 6:
            return self.group(x, c, 1 - y, 1), self.group(1 - x, c, 1 - y, 1), p.xn()
        xx = x if slot in (7, 9) else 1 - x
        yy = y if slot in (7, 8) else 1 - y
        return self.group(xx, c, yy), self.group(xx, 1 - c, yy), p.core()

    def start(self, *slots):
        for slot in slots:
            mine, _, dev = self.parts(slot)
            remote(mine, mine, self.send.at[slot], self.recv.at[slot], dev).start()

    def arrive(self, *slots):
        for slot in slots:
            _, theirs, dev = self.parts(slot)
            remote(theirs, theirs, self.send.at[slot], self.recv.at[slot], dev).wait_recv()

    def left(self, *slots):
        for slot in slots:
            mine, _, dev = self.parts(slot)
            remote(mine, mine, self.send.at[slot], self.recv.at[slot], dev).wait_send()

    def s1(self):
        self.start(0, 1, 2)

    def s2(self):
        self.arrive(0, 1, 2)
        self.start(3, 4, 7)

    def s3(self):
        self.arrive(3)
        self.start(5, 8)
        self.arrive(4)
        self.start(6, 9)

    def s4(self):
        self.arrive(5, 6)
        self.start(10)

    def s5(self):
        self.arrive(7, 8, 9, 10)

    def s6(self):
        self.left(*range(11))


class Scatter:
    def __init__(self, inner, buf, rows, col0, cols, slots, send, recv, credit, out):
        self.inner, self.buf, self.rows = inner, buf, rows
        self.cols = slice(col0, col0 + cols)
        self.slots, self.send, self.recv = slots, send, recv
        self.credit, self.out = credit, out

    def parts(self, slot):
        p = Place(self.inner)
        x, c, z, y = p.x, p.c, p.z, p.y
        half = self.rows // 2
        cols = self.cols
        r1, ra, rb, rx, ry, rz = self.slots
        rows, cut, rest = slice(0, self.rows), slice(0, half), slice(half, self.rows)
        buf = self.buf
        if slot == 0:
            return buf.at[:, 1 - c, :, :, :, cols], r1.at[:, :, :, rows], p.core()
        if slot == 1:
            return buf.at[1 - x, c, :, 1 - y, cut, cols], ra.at[:, cut], p.yn()
        if slot == 2:
            return buf.at[1 - x, c, :, 1 - y, rest, cols], rb.at[:, cut], p.xn()
        if slot == 3:
            return buf.at[1 - x, c, :, y, rows, cols], rx.at[:, rows], p.xn()
        if slot == 4:
            return buf.at[x, c, :, 1 - y, rows, cols], ry.at[:, rows], p.yn()
        d = slot - 4
        return buf.at[x, c, (z + d) % 4, y, rows, cols], rz.at[d - 1, rows], p.zn(d)

    def start(self, *slots):
        for slot in slots:
            src, dst, dev = self.parts(slot)
            remote(src, dst, self.send.at[slot], self.recv.at[slot], dev).start()

    def arrive(self, *slots):
        for slot in slots:
            _, dst, dev = self.parts(slot)
            remote(dst, dst, self.send.at[slot], self.recv.at[slot], dev).wait_recv()

    def left(self):
        for slot in range(8):
            src, dst, dev = self.parts(slot)
            remote(src, dst, self.send.at[slot], self.recv.at[slot], dev).wait_send()

    def take_credit(self):
        for i in range(6):
            pl.semaphore_wait(self.credit.at[i], 1)

    def give_credit(self):
        p = Place(self.inner)
        for i, dev in enumerate((p.core(), p.xn(), p.yn(), p.zp(1), p.zp(2), p.zp(3))):
            pl.semaphore_signal(self.credit.at[i], inc=1, device_id=dev, device_id_type=MESH)

    def s1(self):
        self.start(0)

    def add(self, x, y, rows, *others):
        c = Place(self.inner).c

        @pl.loop(0, 4)
        def _(z):
            total = self.buf[x, c, z, y, rows, self.cols].astype(F32)
            for other in others:
                total = total + other(z).astype(F32)
            self.buf[x, c, z, y, rows, self.cols] = total.astype(BF)

    def s2(self):
        p = Place(self.inner)
        rows = slice(0, self.rows)
        r1 = self.slots[0]
        self.arrive(0)
        for x, y in ((1 - p.x, 1 - p.y), (1 - p.x, p.y), (p.x, 1 - p.y), (p.x, p.y)):
            self.add(x, y, rows, lambda z: r1[x, z, y, rows])
            if x is not p.x and y is not p.y:
                self.start(1, 2)

    def s3(self):
        p = Place(self.inner)
        half = self.rows // 2
        cut, rest = slice(0, half), slice(half, self.rows)
        ra, rb = self.slots[1:3]
        self.arrive(1)
        self.add(1 - p.x, p.y, cut, lambda z: ra[z, cut])
        self.start(3)
        self.arrive(2)
        self.add(p.x, 1 - p.y, rest, lambda z: rb[z, cut])
        self.start(4)

    def s4(self):
        p = Place(self.inner)
        rows = slice(0, self.rows)
        rx, ry = self.slots[3:5]
        self.arrive(3, 4)
        self.add(p.x, p.y, rows, lambda z: rx[z, rows], lambda z: ry[z, rows])
        self.start(5, 6, 7)

    def s5(self):
        p = Place(self.inner)
        rows = slice(0, self.rows)
        rz = self.slots[5]
        self.arrive(5, 6, 7)
        total = self.buf[p.x, p.c, p.z, p.y, rows, self.cols].astype(F32)
        for d in range(3):
            total = total + rz[d, rows].astype(F32)
        self.out[...] = total
        self.left()


class Total:
    def __init__(self, inner, ref, got, send, recv):
        self.inner, self.ref, self.got, self.send, self.recv = inner, ref, got, send, recv

    def copy(self, slot):
        p = Place(self.inner)
        dev = (p.core, p.xn, p.yn)[slot]() if slot < 3 else p.zn(slot - 2)
        stage = min(slot, 3)
        return remote(self.ref.at[stage], self.got.at[slot], self.send.at[slot], self.recv.at[slot], dev)

    def run(self, stage):
        slots = (stage,) if stage < 3 else (3, 4, 5)
        for slot in slots:
            self.copy(slot).start()

    def take(self, stage):
        slots = (stage,) if stage < 3 else (3, 4, 5)
        total = self.ref[stage]
        for slot in slots:
            self.copy(slot).wait_recv()
            total = total + self.got[slot]
        self.ref[stage + 1] = total

    def left(self):
        for slot in range(6):
            self.copy(slot).wait_send()


def head_parts(t_ref, k2_ref, t, h, qs, kr):
    if h < 2:
        return t_ref[t, qs, 0:128], t_ref[t, kr, 128:256], t_ref[t, kr, 256:384]
    return t_ref[t, qs, 384:512], k2_ref[kr, :], t_ref[t, kr, 512:640]


def lanes():
    return lax.broadcasted_iota(jnp.int32, (1, 128), 1)


def roll_key(t_ref, k2_ref, t):
    k2_ref[...] = pltpu.roll(t_ref[t, :, 384:512].astype(F32), 64, 1).astype(BF)


def below(transposed):
    r = lax.broadcasted_iota(jnp.int32, (BQ, BQ), 0)
    c = lax.broadcasted_iota(jnp.int32, (BQ, BQ), 1)
    return r <= c if transposed else r >= c


def attend(t_ref, l_ref, kx_ref, k2_ref, c_ref, t, length):
    lane = lanes()
    low = lane < 64
    roll_key(t_ref, k2_ref, t)
    for i in range(length // BQ):
        first = max(0, i * BQ - length // 2)
        width = (i + 1) * BQ - first
        qs, kr = slice(i * BQ, (i + 1) * BQ), slice(first, first + width)
        kx = kx_ref[kr, :]
        doc = kx_ref[qs, :].astype(F32)
        qx = jnp.where(lane < 8, BIG * (1.0 - doc), 0.0).astype(BF)
        marks = qx
        outs = []
        for h in range(3):
            q, k, v = head_parts(t_ref, k2_ref, t, h, qs, kr)
            keep = jnp.logical_not(low) if h == 1 else low
            q = jnp.where(keep, q * BF(HD ** -0.5), BF(0))
            s = dot(jnp.concatenate([q, qx], 1), jnp.concatenate([k, kx], 1), NT)
            edge = jnp.where(below(False), s[:, width - BQ :], BIG)
            s = edge if width == BQ else jnp.concatenate([s[:, : width - BQ], edge], 1)
            top = jnp.max(s, axis=1, keepdims=True)
            p = jnp.exp(s - top).astype(BF)
            both = dot(p, jnp.concatenate([v, jnp.ones((width, 128), BF)], 1))
            total = both[:, 128:256]
            outs.append(both[:, :128] / total)
            rest = -(top + jnp.log(total))
            for n in range(3):
                piece = rest.astype(BF)
                marks = jnp.where(lane == 8 + 16 * h + n, piece, marks)
                rest = rest - piece.astype(F32)
        l_ref[t, qs, :] = marks
        c_ref[t, qs, 0:128] = jnp.where(low, outs[0], outs[1]).astype(BF)
        c_ref[t, qs, 128:256] = jnp.where(low, outs[2], 0.0).astype(BF)


def attend_back(t_ref, l_ref, kx_ref, k2_ref, c_ref, do_ref, sums, heads, t, length):
    lane = lanes()
    low = lane < 64
    dk_ref, dv_ref = sums
    odd = heads == (2,)
    if odd:
        roll_key(t_ref, k2_ref, t)
    for ref in sums:
        ref[...] = jnp.zeros_like(ref)
    for i in range(length // BQ):
        first = max(0, i * BQ - length // 2)
        width = (i + 1) * BQ - first
        qs, kr = slice(i * BQ, (i + 1) * BQ), slice(first, first + width)
        marks = l_ref[t, qs, :]
        kx = kx_ref[kr, :]
        minus = jnp.full((width, 128), -1.0, BF)
        grad = None
        for h in heads:
            q, k, v = head_parts(t_ref, k2_ref, t, h, qs, kr)
            keep = jnp.logical_not(low) if h == 1 else low
            side = slice(128, 256) if odd else slice(0, 128)
            q = jnp.where(keep, q * BF(HD ** -0.5), BF(0))
            do = jnp.where(keep, do_ref[t, qs, side], BF(0))
            km = jnp.where(keep, k, BF(0))
            dd = (do.astype(F32) * c_ref[t, qs, side].astype(F32)).astype(BF)
            mine = (lane < 8) | ((lane >= 8 + 16 * h) & (lane < 24 + 16 * h))
            qe = jnp.concatenate([q, jnp.where(mine, marks, BF(0))], 1)
            s = dot(jnp.concatenate([k, kx], 1), qe, NT)
            dp = dot(jnp.concatenate([v, minus], 1), jnp.concatenate([do, dd], 1), NT)
            edge = jnp.where(below(True), s[width - BQ :], BIG)
            s = edge if width == BQ else jnp.concatenate([s[: width - BQ], edge], 0)
            p = jnp.exp(s)
            ds = (p * dp).astype(BF)
            gq = dot(ds, km, TN)
            grad = gq if grad is None else grad + gq
            dv_ref[kr, :] += dot(p.astype(BF), do)
            dk_ref[kr, :] += dot(ds, q)
        grad = (grad * HD ** -0.5).astype(BF)
        if odd:
            t_ref[t, qs, 384:512] = jnp.where(low, grad, t_ref[t, qs, 384:512])
        else:
            t_ref[t, qs, 0:128] = grad
    if odd:
        moved = pltpu.roll(dk_ref[...], 64, 1).astype(BF)
        t_ref[t, :, 384:512] = jnp.where(low, t_ref[t, :, 384:512], moved)
        t_ref[t, :, 512:640] = dv_ref[...].astype(BF)
    else:
        t_ref[t, :, 128:256] = dk_ref[...].astype(BF)
        t_ref[t, :, 256:384] = dv_ref[...].astype(BF)


def stats(v):
    mean = jnp.mean(v, axis=-1, keepdims=True)
    center = v - mean
    scale = lax.rsqrt(jnp.mean(center * center, axis=-1, keepdims=True) + EPS)
    return center * scale, scale


def norm_back(v, q, gain):
    n, scale = stats(v)
    e = q * gain
    back = scale * (e - jnp.mean(e, -1, keepdims=True) - n * jnp.mean(e * n, -1, keepdims=True))
    return back, jnp.sum(q * n, 0, keepdims=True), jnp.sum(q, 0, keepdims=True)


def kernel(
    inner, length,
    tok, cot, seg, valid, wq_in, wo_in, wm_in,
    lo_out, gt_out, gq_out, go_out, gm_out, ar_out,
    bq, bo, bm0, bm1, bm2,
    n1, tt, cc, ll, kx, k2, mid, n2, acc, gn, act, gu, val, par,
    dk, dv,
    m_sets, q_set, ar, ar_got,
    ag_send, ag_recv, rs_send, rs_recv, credit, ar_send, ar_recv, local_sem,
):
    width = tok.shape[1]
    bm = (bm0, bm1, bm2)
    blocks = [(bq, 0, 32), (bq, 32, 32), (bq, 64, 32), (bo, 0, 96)] + [(b, 0, 192) for b in bm]
    gathers = [Gather(inner, b, r0, rows, ag_send.at[k], ag_recv.at[k]) for k, (b, r0, rows) in enumerate(blocks)]
    here = Place(inner)

    def fills():
        at = (here.x, here.c, here.z, here.y)
        pairs = [(wq_in, bq), (wo_in, bo)] + [(wm_in.at[j], bm[j]) for j in range(3)]
        return [pltpu.make_async_copy(src, b.at[at], local_sem.at[k]) for k, (src, b) in enumerate(pairs)]

    scatters = []
    sets = [m_sets[0:6], m_sets[6:12]]
    plan = [(bm0, 192, 0, 256, sets[0], gm_out.at[0]), (bm1, 192, 0, 256, sets[1], gm_out.at[1]),
            (bm2, 192, 0, 256, sets[0], gm_out.at[2]), (bo, 96, 0, 256, sets[1], go_out),
            (bq, 96, 0, 384, q_set, gq_out.at[:, 0:384]), (bq, 96, 384, 256, sets[0], gq_out.at[:, 384:640])]
    for k, (b, rows, col0, cols, slots, out) in enumerate(plan):
        cred = credit.at[min(k, 2)]
        scatters.append(Scatter(inner, b, rows, col0, cols, slots, rs_send.at[k], rs_recv.at[k], cred, out))
    m_sum, o_sum, qa_sum, qb_sum = scatters[0:3], scatters[3], scatters[4], scatters[5]
    q_in, o_in, m_in = gathers[0:3], gathers[3], gathers[4:7]
    total = Total(inner, ar, ar_got, ar_send, ar_recv)

    def after(t, last, *steps):
        @pl.when(t == last)
        def _():
            for step in steps:
                step()

    def rows_of(i, size):
        return pl.ds(pl.multiple_of(i * size, size), size)

    def weight(buf, t, r0, rows, columns):
        return buf[t // 2, t % 2, :, :, r0 : r0 + rows, columns].reshape(8 * rows, -1)

    for one in fills():
        one.start()
    barrier(inner)
    for one in fills():
        one.wait()
    for g in q_in:
        g.s1()

    me_t = lax.axis_index("tp")
    row = seg[pl.ds(me_t, 1), :].astype(F32)
    lane_id = lax.broadcasted_iota(jnp.int32, (128, length), 0)
    marks = jnp.where(row == lane_id.astype(F32), 1.0, 0.0)
    marks = jnp.where(lane_id < 8, marks, 0.0)
    low4 = lane_id % 16
    ones = (lane_id >= 8) & (lane_id < 56) & (low4 >= 8) & (low4 < 11)
    marks = jnp.where(ones, 1.0, marks)
    marks = jnp.where(lane_id == 64, valid[...].astype(F32), marks)
    columns = marks.T
    val[...] = columns[:, 64:65]
    kx[...] = jnp.where(lanes() < 64, columns, 0.0).astype(BF)
    ar[0] = jnp.zeros_like(ar.at[0])
    ar[0, 7:8, 0:128] = jnp.broadcast_to(jnp.sum(valid[...].astype(F32), axis=1, keepdims=True), (1, 128))

    @pl.loop(0, length // 256)
    def _(i):
        s = rows_of(i, 256)
        mid[s, :] = stats(tok[s, :].astype(F32))[0]

    q_in[0].s2()
    o_in.s1()
    q_in[1].s2()
    q_in[0].s3()
    m_in[0].s1()
    q_in[2].s2()
    q_in[1].s3()
    q_in[0].s4()
    q_in[2].s3()
    q_in[1].s4()
    o_in.s2()
    m_in[1].s1()
    q_in[2].s4()
    for g in q_in:
        g.s5()
    m_in[0].s2()

    par[...] = bq[0, 0, :, :, :, 512:640].reshape(width, 128).astype(F32).T

    @pl.loop(0, length // 256)
    def _(i):
        s = rows_of(i, 256)
        n1[s, :] = (mid[s, :] * par[64:65, :] + par[65:66, :]).astype(BF)

    @pl.loop(0, 4)
    def _(t):
        w = weight(bq, t, 0, 96, slice(0, 640))

        @pl.loop(0, length // 512)
        def _(i):
            s = rows_of(i, 512)
            tt[t, s, :] = dot(n1[s, :], w).astype(BF)

        attend(tt, ll, kx, k2, cc, t, length)
        after(t, 0, o_in.s3, m_in[2].s1)
        after(t, 1, m_in[1].s2, o_in.s4)
        after(t, 2, m_in[0].s3, o_in.s5)
        after(t, 3, m_in[2].s2, m_in[0].s4)

    @pl.loop(0, length // 256)
    def _(i):
        s = rows_of(i, 256)
        branch = jnp.zeros((256, width), F32)
        for t in range(4):
            branch = branch + dot(cc[t, s, :], weight(bo, t, 0, 96, slice(0, 256)), NT)
        v = tok[s, :].astype(F32) + branch
        mid[s, :] = v
        ar[0, 5:6, :] += jnp.sum(val[s, :] * (branch * branch), 0, keepdims=True)
        n, _ = stats(v)
        n2[s, :] = (n * par[66:67, :] + par[67:68, :]).astype(BF)

    m_in[1].s3()
    m_in[0].s5()

    for j in range(3):
        b = bm[j]
        before = m_sum[j - 1] if j > 0 else None

        @pl.loop(0, 4)
        def _(t):
            up = weight(b, t, 0, 96, slice(0, 256))
            down = weight(b, t, 96, 96, slice(0, 256))

            @pl.loop(0, length // 512)
            def _(i):
                s = rows_of(i, 512)
                v = dot(n2[s, :], up)
                ga = dot(cot[s, :], down)
                v2 = v * v
                th = jnp.tanh(v * (C0 + C1 * v2))
                h = 0.5 + 0.5 * th
                act[t, s, :] = (v * h).astype(BF)
                slope = h + (0.5 * v) * (1.0 - th * th) * (C0 + (3.0 * C1) * v2)
                gu[t, s, :] = (ga * slope).astype(BF)

            if j > 0:
                after(t, 1, before.s2)

        if j == 0:
            m_in[2].s3()
            m_in[1].s4()
        else:
            before.s3()

        def cat(ref, s):
            return jnp.concatenate([ref[t, s, :] for t in range(4)], 1)

        def wcat(r0):
            return jnp.concatenate([weight(b, t, r0, 96, slice(0, 256)) for t in range(4)], 1)

        @pl.loop(0, length // 256)
        def _(i):
            s = rows_of(i, 256)
            one = dot(cat(act, s), wcat(96), NT)
            two = dot(cat(gu, s), wcat(0), NT)
            if j == 0:
                acc[s, :] = one
                gn[s, :] = two
            else:
                acc[s, :] += one
                gn[s, :] += two

        m_in[j].s6()
        if j == 0:
            m_in[2].s4()
            m_in[1].s5()
        else:
            before.s4()

        @pl.loop(0, 4)
        def _(t):
            gup = dot(n2[...], gu[t], TN).astype(BF)
            b[t // 2, t % 2, :, :, 0:96, :] = gup.reshape(4, 2, 96, 256)
            gdown = dot(cot[...], act[t], TN).astype(BF)
            b[t // 2, t % 2, :, :, 96:192, :] = gdown.reshape(4, 2, 96, 256)

        if j == 2:
            m_sum[0].take_credit()
        m_sum[j].s1()
        if j == 0:
            m_in[2].s5()
        else:
            before.s5()
            before.give_credit()

    @pl.loop(0, length // 256)
    def _(i):
        s = rows_of(i, 256)
        v = mid[s, :]
        mlp = acc[s, :]
        out = v + mlp
        weight_rows = val[s, :]
        ar[0, 4:5, :] += jnp.sum(weight_rows * (out * out), 0, keepdims=True)
        ar[0, 6:7, :] += jnp.sum(weight_rows * (mlp * mlp), 0, keepdims=True)
        low_out = out.astype(BF)
        for k in range(width // 256):
            gu[k, s, :] = low_out[:, 256 * k : 256 * k + 256]
        back, g_gain, g_bias = norm_back(v, gn[s, :], par[66:67, :])
        ar[0, 2:3, :] += g_gain
        ar[0, 3:4, :] += g_bias
        grad = cot[s, :].astype(F32) + back
        mid[s, :] = grad
        n2[s, :] = grad.astype(BF)

    def store_low():
        return [
            pltpu.make_async_copy(gu.at[k], lo_out.at[:, pl.ds(256 * k, 256)], local_sem.at[k])
            for k in range(width // 256)
        ]

    for one in store_low():
        one.start()
    m_sum[2].s2()
    o_in.s6()

    @pl.loop(0, 4)
    def _(t):
        w = weight(bo, t, 0, 96, slice(0, 256))
        act[t] = dot(n2[...], w).astype(BF)
        bo[t // 2, t % 2] = dot(n2[...], cc[t], TN).astype(BF).reshape(4, 2, 96, 256)

    m_sum[1].take_credit()
    o_sum.s1()
    m_sum[2].s3()

    @pl.loop(0, 4)
    def _(t):
        attend_back(tt, ll, kx, k2, cc, act, (dk, dv), (0, 1), t, length)
        after(t, 0, o_sum.s2, m_sum[2].s4)
        after(t, 1, o_sum.s3, m_sum[2].s5, m_sum[2].give_credit)
        after(t, 2, o_sum.s4)
        after(t, 3, o_sum.s5)

    for g in q_in:
        g.s6()

    @pl.loop(0, length // 256)
    def _(i):
        s = rows_of(i, 256)
        part = jnp.zeros((256, width), F32)
        for t in range(4):
            part = part + dot(tt[t, s, 0:384], weight(bq, t, 0, 96, slice(0, 384)), NT)
        gn[s, :] = part

    @pl.loop(0, 4)
    def _(t):
        bq[t // 2, t % 2, :, :, :, 0:384] = dot(n1[...], tt[t, :, 0:384], TN).astype(BF).reshape(4, 2, 96, 384)

    qa_sum.s1()

    @pl.loop(0, 4)
    def _(t):
        attend_back(tt, ll, kx, k2, cc, act, (dk, dv), (2,), t, length)
        after(t, 0, qa_sum.s2)
        after(t, 1, qa_sum.s3)
        after(t, 3, qa_sum.s4)

    @pl.loop(0, length // 256)
    def _(i):
        s = rows_of(i, 256)
        part = gn[s, :]
        for t in range(4):
            part = part + dot(tt[t, s, 384:640], weight(bq, t, 0, 96, slice(384, 640)), NT)
        gn[s, :] = part

    @pl.loop(0, 4)
    def _(t):
        bq[t // 2, t % 2, :, :, :, 384:640] = dot(n1[...], tt[t, :, 384:640], TN).astype(BF).reshape(4, 2, 96, 256)

    m_sum[2].take_credit()
    qb_sum.s1()
    qa_sum.s5()
    qb_sum.s2()

    @pl.loop(0, length // 256)
    def _(i):
        s = rows_of(i, 256)
        back, g_gain, g_bias = norm_back(tok[s, :].astype(F32), gn[s, :], par[64:65, :])
        ar[0, 0:1, :] += g_gain
        ar[0, 1:2, :] += g_bias
        acc[s, :] = mid[s, :] + back

    def store_grad():
        return pltpu.make_async_copy(acc, gt_out, local_sem.at[4])

    store_grad().start()
    total.run(0)
    qb_sum.s3()
    total.take(0)
    total.run(1)
    total.take(1)
    total.run(2)
    qb_sum.s4()
    total.take(2)
    total.run(3)
    qb_sum.s5()
    total.take(3)
    total.left()
    ar_out[...] = ar[4]
    for one in store_low():
        one.wait()
    store_grad().wait()


def scatter_slots(rows, columns):
    return [
        pltpu.VMEM((2, 4, 2, rows, columns), BF),
        pltpu.VMEM((4, rows // 2, columns), BF),
        pltpu.VMEM((4, rows // 2, columns), BF),
        pltpu.VMEM((4, rows, columns), BF),
        pltpu.VMEM((4, rows, columns), BF),
        pltpu.VMEM((3, rows, columns), BF),
    ]


def layer(inner, tokens, cotangent, segments, valid, wq, wo, wm):
    length, width = tokens.shape
    block = lambda rows, columns: pltpu.VMEM((2, 2, 4, 2, rows, columns), BF)
    scratch = [
        block(96, 640), block(96, 256), block(192, 256), block(192, 256), block(192, 256),
        pltpu.VMEM((length, width), BF),
        pltpu.VMEM((4, length, 640), BF),
        pltpu.VMEM((4, length, 256), BF),
        pltpu.VMEM((4, length, 128), BF),
        pltpu.VMEM((length, 128), BF),
        pltpu.VMEM((length, 128), BF),
        pltpu.VMEM((length, width), F32),
        pltpu.VMEM((length, width), BF),
        pltpu.VMEM((length, width), F32),
        pltpu.VMEM((length, width), F32),
        pltpu.VMEM((4, length, 256), BF),
        pltpu.VMEM((4, length, 256), BF),
        pltpu.VMEM((length, 1), F32),
        pltpu.VMEM((128, width), F32),
    ]
    scratch += [pltpu.VMEM((length, 128), F32)] * 2
    scratch += [scatter_slots(192, 256) + scatter_slots(192, 256), scatter_slots(96, 384)]
    scratch += [
        pltpu.VMEM((5, 8, width), F32),
        pltpu.VMEM((6, 8, width), F32),
        pltpu.SemaphoreType.DMA((7, 11)),
        pltpu.SemaphoreType.DMA((7, 11)),
        pltpu.SemaphoreType.DMA((6, 8)),
        pltpu.SemaphoreType.DMA((6, 8)),
        pltpu.SemaphoreType.REGULAR((3, 6)),
        pltpu.SemaphoreType.DMA((6,)),
        pltpu.SemaphoreType.DMA((6,)),
        pltpu.SemaphoreType.DMA((5,)),
    ]
    vmem, anywhere = pl.BlockSpec(memory_space=pltpu.VMEM), pl.BlockSpec(memory_space=pl.ANY)
    return pl.pallas_call(
        partial(kernel, inner, length),
        out_shape=(
            jax.ShapeDtypeStruct((length, width), BF),
            jax.ShapeDtypeStruct((length, width), F32),
            jax.ShapeDtypeStruct((96, 640), F32),
            jax.ShapeDtypeStruct((96, 256), F32),
            jax.ShapeDtypeStruct((3, 192, 256), F32),
            jax.ShapeDtypeStruct((8, width), F32),
        ),
        in_specs=[vmem] * 4 + [anywhere] * 3,
        out_specs=(anywhere, anywhere, vmem, vmem, vmem, vmem),
        scratch_shapes=scratch,
        compiler_params=pltpu.CompilerParams(
            collective_id=0, has_side_effects=True, vmem_limit_bytes=63 * 2**20
        ),
    )(tokens, cotangent, segments, valid, wq, wo, wm)


def local(
    tokens, segment_ids, valid, ln1_gain, ln1_bias, w_qkv, w_out, ln2_gain, ln2_bias, w_up, w_down, cotangent
):
    length, width = tokens.shape
    holders = lax.axis_size("fsdp")
    inner = holders // 8
    groups = [[g * inner + i for i in range(inner)] for g in range(8)]

    def widen(block):
        if inner == 1:
            return block
        return lax.all_gather(block, "fsdp", axis_index_groups=groups, axis=0, tiled=True)

    def narrow(block):
        if inner == 1:
            return block
        return lax.psum_scatter(
            block, "fsdp", scatter_dimension=0, axis_index_groups=groups, tiled=True
        )

    rows = w_up.shape[0]
    heads = w_qkv.reshape(rows, 3, 3, HD)
    pairs = heads[:, :, 0:2].reshape(rows, 3 * 2 * HD)
    odd = heads[:, :, 2].reshape(rows, 3 * HD)
    params = jnp.stack([ln1_gain, ln1_bias, ln2_gain, ln2_bias], axis=1)
    wq = widen(jnp.concatenate([pairs, odd, params, jnp.zeros((rows, 60), BF)], axis=1))
    wo = widen(jnp.pad(w_out.T, ((0, 0), (0, 64))))
    up = widen(w_up).reshape(rows * inner, 3, 256)
    down = widen(w_down.T).reshape(rows * inner, 3, 256)
    wm = jnp.concatenate([up, down], axis=0).transpose(1, 0, 2)

    low, grad_tokens, gq, go, gm, sums = layer(
        inner, tokens, cotangent, segment_ids, valid.reshape(1, length), wq, wo, wm
    )

    gq = narrow(gq[:, : 9 * HD])
    pair = gq[:, : 6 * HD].reshape(rows, 3, 2 * HD)
    one = gq[:, 6 * HD : 9 * HD].reshape(rows, 3, HD)
    grad_qkv = jnp.concatenate([pair, one], axis=2)
    grad_out = narrow(go[:, : 3 * HD]).T
    gm = gm.transpose(1, 0, 2).reshape(192, 768)
    grad_up = narrow(gm[:96])
    grad_down = narrow(gm[96:]).T
    if inner > 1:
        sums = lax.psum(sums, "fsdp", axis_index_groups=groups)
    share = width // (holders * lax.axis_size("tp"))
    owner = lax.axis_index("fsdp") * lax.axis_size("tp") + lax.axis_index("tp")
    mine = lax.dynamic_slice_in_dim(sums[0:4], owner * share, share, 1)
    spread = jnp.sqrt(jnp.sum(sums[4:7], axis=1) / (sums[7, 0] * width))
    return (
        low, grad_tokens, mine[0], mine[1], grad_qkv, grad_out, mine[2], mine[3], grad_up, grad_down, spread
    )


def solution(mesh):
    both = ("fsdp", "tp")
    return jax.shard_map(
        local,
        mesh=mesh,
        in_specs=(
            P(both, None), P("fsdp", None), P(both), P("fsdp"), P("fsdp"), P("fsdp", None, "tp"),
            P("tp", "fsdp"), P("fsdp"), P("fsdp"), P("fsdp", "tp"), P("tp", "fsdp"), P(both, None),
        ),
        out_specs=(
            P(both, None), P(both, None), P(both), P(both), P("fsdp", None, "tp"), P("tp", "fsdp"),
            P(both), P(both), P("fsdp", "tp"), P("tp", "fsdp"), P(),
        ),
        check_vma=False,
    )
```

```python
from functools import partial

import jax
import jax.numpy as jnp
from jax import lax
from jax.experimental import pallas as pl
from jax.experimental.pallas import tpu as pltpu
from jax.sharding import PartitionSpec as P

HD = 64
BQ = 256
EPS = 1e-05
BIG = -1e30
F32 = jnp.float32
BF = jnp.bfloat16
NN = (((1,), (0,)), ((), ()))
NT = (((1,), (1,)), ((), ()))
TN = (((0,), (0,)), ((), ()))
MESH = pl.DeviceIdType.MESH
C0 = 0.7978845608
C1 = 0.7978845608 * 0.044715


def dot(a, b, dims=NN):
    return lax.dot_general(a, b, dims, preferred_element_type=F32)


def phase(body):
    return body


def remote(src, dst, send, recv, device):
    return pltpu.make_async_remote_copy(
        src_ref=src, dst_ref=dst, send_sem=send, recv_sem=recv,
        device_id=device, device_id_type=MESH,
    )


class Place:
    def __init__(self, inner):
        f = lax.axis_index("fsdp")
        t = lax.axis_index("tp")
        g = f // inner
        self.low = f % inner
        self.inner = inner
        self.z, self.y, self.x, self.c = g // 2, g % 2, t // 2, t % 2

    def device(self, z, y, x, c):
        return ((z * 2 + y) * self.inner + self.low, x * 2 + c)

    def core(self):
        return self.device(self.z, self.y, self.x, 1 - self.c)

    def xn(self):
        return self.device(self.z, self.y, 1 - self.x, self.c)

    def yn(self):
        return self.device(self.z, 1 - self.y, self.x, self.c)

    def cube(self, n):
        y, x, c = (self.y + n // 4) % 2, (self.x + n // 2) % 2, (self.c + n) % 2
        return self.device(self.z, y, x, c)

    def zn(self, d):
        return self.device((self.z + d) % 4, self.y, self.x, self.c)

    def zp(self, d):
        return self.device((self.z - d + 4) % 4, self.y, self.x, self.c)


def greet(inner):
    p = Place(inner)
    sem = pltpu.get_barrier_semaphore()
    for dev in [p.cube(n) for n in range(1, 8)] + [p.zn(d) for d in range(1, 4)]:
        pl.semaphore_signal(sem, inc=1, device_id=dev, device_id_type=MESH)


def met(inner):
    pl.semaphore_wait(pltpu.get_barrier_semaphore(), 10)


class Gather:
    def __init__(self, name, inner, buf, row0, rows, send, recv):
        self.name = name
        self.inner, self.buf, self.row0, self.rows = inner, buf, row0, rows
        self.send, self.recv = send, recv

    def own(self, x, c, z, y):
        return self.buf.at[x, c, z, y, pl.ds(self.row0, self.rows)]

    def group(self, x, c, y, half=None):
        start, size = self.row0, self.rows
        if half is not None:
            size = self.rows // 2
            start = self.row0 + half * size
        return self.buf.at[x, c, :, y, pl.ds(start, size)]

    def parts(self, slot):
        p = Place(self.inner)
        x, c, z, y = p.x, p.c, p.z, p.y
        if slot < 3:
            d = slot + 1
            return self.own(x, c, z, y), self.own(x, c, (z - d + 4) % 4, y), p.zn(d)
        if slot == 3:
            return self.group(x, c, y), self.group(1 - x, c, y), p.xn()
        if slot == 4:
            return self.group(x, c, y), self.group(x, c, 1 - y), p.yn()
        if slot == 5:
            return self.group(1 - x, c, y, 0), self.group(1 - x, c, 1 - y, 0), p.yn()
        if slot == 6:
            return self.group(x, c, 1 - y, 1), self.group(1 - x, c, 1 - y, 1), p.xn()
        xx = x if slot in (7, 9) else 1 - x
        yy = y if slot in (7, 8) else 1 - y
        return self.group(xx, c, yy), self.group(xx, 1 - c, yy), p.core()

    def start(self, *slots):
        for slot in slots:
            mine, _, dev = self.parts(slot)
            remote(mine, mine, self.send.at[slot], self.recv.at[slot], dev).start()

    def arrive(self, *slots):
        for slot in slots:
            _, theirs, dev = self.parts(slot)
            remote(theirs, theirs, self.send.at[slot], self.recv.at[slot], dev).wait_recv()

    def left(self, *slots):
        for slot in slots:
            mine, _, dev = self.parts(slot)
            remote(mine, mine, self.send.at[slot], self.recv.at[slot], dev).wait_send()

    def s1(self):
        self.start(0, 1, 2)

    def s2(self):
        self.arrive(0, 1, 2)
        self.start(3, 4, 7)

    def s3(self):
        self.arrive(4)
        self.start(6, 9)
        self.arrive(3)
        self.start(5, 8)

    def s4(self):
        self.arrive(5, 6)
        self.start(10)

    def near(self):
        self.arrive(7, 9)

    def far(self):
        self.arrive(8, 10)

    def s5(self):
        self.near()
        self.far()

    def s6(self):
        self.left(*range(11))


class Scatter:
    def __init__(self, name, inner, buf, rows, col0, cols, slots, send, recv, credit, out):
        self.name = name
        self.inner, self.buf, self.rows = inner, buf, rows
        self.half = (rows // 2 + 15) // 16 * 16
        self.cols = slice(col0, col0 + cols)
        self.slots, self.send, self.recv = slots, send, recv
        self.credit, self.out = credit, out

    def parts(self, slot):
        p = Place(self.inner)
        x, c, z, y = p.x, p.c, p.z, p.y
        half = self.half
        cols = self.cols
        r1, ra, rb, rx, ry, rz = self.slots
        rows, cut, rest = slice(0, self.rows), slice(0, half), slice(half, self.rows)
        buf = self.buf
        if slot == 0:
            return buf.at[:, 1 - c, :, :, rows, cols], r1.at[:, :, :, rows], p.core()
        if slot == 1:
            return buf.at[1 - x, c, :, 1 - y, cut, cols], ra.at[:, cut], p.yn()
        if slot == 2:
            return buf.at[1 - x, c, :, 1 - y, rest, cols], rb.at[:, slice(0, self.rows - half)], p.xn()
        if slot == 3:
            return buf.at[1 - x, c, :, y, rows, cols], rx.at[:, rows], p.xn()
        if slot == 4:
            return buf.at[x, c, :, 1 - y, rows, cols], ry.at[:, rows], p.yn()
        d = slot - 4
        return buf.at[x, c, (z + d) % 4, y, rows, cols], rz.at[d - 1, rows], p.zn(d)

    def start(self, *slots):
        for slot in slots:
            src, dst, dev = self.parts(slot)
            remote(src, dst, self.send.at[slot], self.recv.at[slot], dev).start()

    def arrive(self, *slots):
        for slot in slots:
            _, dst, dev = self.parts(slot)
            remote(dst, dst, self.send.at[slot], self.recv.at[slot], dev).wait_recv()

    def left(self):
        for slot in range(8):
            src, dst, dev = self.parts(slot)
            remote(src, dst, self.send.at[slot], self.recv.at[slot], dev).wait_send()

    def take_credit(self):
        for i in range(6):
            pl.semaphore_wait(self.credit.at[i], 1)

    def give_credit(self):
        p = Place(self.inner)
        for i, dev in enumerate((p.core(), p.xn(), p.yn(), p.zp(1), p.zp(2), p.zp(3))):
            pl.semaphore_signal(self.credit.at[i], inc=1, device_id=dev, device_id_type=MESH)

    def s1(self):
        self.start(0)

    def add(self, x, y, rows, *others):
        c = Place(self.inner).c

        @pl.loop(0, 4)
        def _(z):
            total = self.buf[x, c, z, y, rows, self.cols].astype(F32)
            for other in others:
                total = total + other(z).astype(F32)
            self.buf[x, c, z, y, rows, self.cols] = total.astype(BF)

    def s2(self):
        p = Place(self.inner)
        rows = slice(0, self.rows)
        r1 = self.slots[0]
        self.arrive(0)
        for x, y in ((1 - p.x, 1 - p.y), (1 - p.x, p.y), (p.x, 1 - p.y), (p.x, p.y)):
            self.add(x, y, rows, lambda z: r1[x, z, y, rows])
            if x is not p.x and y is not p.y:
                self.start(1, 2)

    def s3(self):
        p = Place(self.inner)
        half = self.half
        cut, rest = slice(0, half), slice(half, self.rows)
        ra, rb = self.slots[1:3]
        self.arrive(1)
        self.add(1 - p.x, p.y, cut, lambda z: ra[z, cut])
        self.start(3)
        self.arrive(2)
        self.add(p.x, 1 - p.y, rest, lambda z: rb[z, 0 : self.rows - half])
        self.start(4)

    def s4(self):
        p = Place(self.inner)
        rows = slice(0, self.rows)
        rx, ry = self.slots[3:5]
        self.arrive(3, 4)
        self.add(p.x, p.y, rows, lambda z: rx[z, rows], lambda z: ry[z, rows])
        self.start(5, 6, 7)

    def s5(self):
        p = Place(self.inner)
        rows = slice(0, self.rows)
        rz = self.slots[5]
        self.arrive(5, 6, 7)
        total = self.buf[p.x, p.c, p.z, p.y, rows, self.cols].astype(F32)
        for d in range(3):
            total = total + rz[d, rows].astype(F32)
        self.out(total)
        self.left()


class Total:
    def __init__(self, inner, ref, got, send, recv):
        self.inner, self.ref, self.got, self.send, self.recv = inner, ref, got, send, recv

    def copy(self, slot):
        p = Place(self.inner)
        dev = p.cube(slot + 1) if slot < 7 else p.zn(slot - 6)
        stage = 0 if slot < 7 else 1
        return remote(self.ref.at[stage], self.got.at[slot], self.send.at[slot], self.recv.at[slot], dev)

    def slots(self, stage):
        return range(7) if stage == 0 else range(7, 10)

    def run(self, stage):
        for slot in self.slots(stage):
            self.copy(slot).start()

    def take(self, stage):
        total = self.ref[stage]
        for slot in self.slots(stage):
            self.copy(slot).wait_recv()
            total = total + self.got[slot]
        self.ref[stage + 1] = total

    def left(self):
        for slot in range(10):
            self.copy(slot).wait_send()


def head_parts(t_ref, k2_ref, t, h, qs, kr):
    if h < 2:
        return t_ref[t, qs, 0:128], t_ref[t, kr, 128:256], t_ref[t, kr, 256:384]
    return t_ref[t, qs, 384:512], k2_ref[kr, :], t_ref[t, kr, 512:640]


def lanes():
    return lax.broadcasted_iota(jnp.int32, (1, 128), 1)


def roll_key(t_ref, k2_ref, t):
    k2_ref[...] = pltpu.roll(t_ref[t, :, 384:512].astype(F32), 64, 1).astype(BF)


def below(transposed):
    r = lax.broadcasted_iota(jnp.int32, (BQ, BQ), 0)
    c = lax.broadcasted_iota(jnp.int32, (BQ, BQ), 1)
    return r <= c if transposed else r >= c


def attend(t_ref, l_ref, kx_ref, k2_ref, c_ref, t, length):
    lane = lanes()
    low = lane < 64
    roll_key(t_ref, k2_ref, t)
    for i in range(length // BQ):
        first = max(0, i * BQ - length // 2)
        width = (i + 1) * BQ - first
        qs, kr = slice(i * BQ, (i + 1) * BQ), slice(first, first + width)
        kx = kx_ref[kr, :]
        doc = kx_ref[qs, :].astype(F32)
        qx = jnp.where(lane < 8, BIG * (1.0 - doc), 0.0).astype(BF)
        marks = qx
        outs = []
        for h in range(3):
            q, k, v = head_parts(t_ref, k2_ref, t, h, qs, kr)
            keep = jnp.logical_not(low) if h == 1 else low
            q = jnp.where(keep, q * BF(HD ** -0.5), BF(0))
            s = dot(jnp.concatenate([q, qx], 1), jnp.concatenate([k, kx], 1), NT)
            edge = jnp.where(below(False), s[:, width - BQ :], BIG)
            s = edge if width == BQ else jnp.concatenate([s[:, : width - BQ], edge], 1)
            top = jnp.max(s, axis=1, keepdims=True)
            p = jnp.exp(s - top).astype(BF)
            both = dot(p, jnp.concatenate([v, jnp.ones((width, 128), BF)], 1))
            total = both[:, 128:256]
            outs.append(both[:, :128] / total)
            rest = -(top + jnp.log(total))
            for n in range(3):
                piece = rest.astype(BF)
                marks = jnp.where(lane == 8 + 16 * h + n, piece, marks)
                rest = rest - piece.astype(F32)
        l_ref[t, qs, :] = marks
        c_ref[t, qs, 0:128] = jnp.where(low, outs[0], outs[1]).astype(BF)
        c_ref[t, qs, 128:256] = jnp.where(low, outs[2], 0.0).astype(BF)


def attend_back(t_ref, l_ref, kx_ref, k2_ref, c_ref, do_ref, sums, heads, t, length):
    lane = lanes()
    low = lane < 64
    dk_ref, dv_ref = sums
    odd = heads == (2,)
    if odd:
        roll_key(t_ref, k2_ref, t)
    for ref in sums:
        ref[...] = jnp.zeros_like(ref)
    for i in range(length // BQ):
        first = max(0, i * BQ - length // 2)
        width = (i + 1) * BQ - first
        qs, kr = slice(i * BQ, (i + 1) * BQ), slice(first, first + width)
        marks = l_ref[t, qs, :]
        kx = kx_ref[kr, :]
        minus = jnp.full((width, 128), -1.0, BF)
        grad = None
        for h in heads:
            q, k, v = head_parts(t_ref, k2_ref, t, h, qs, kr)
            keep = jnp.logical_not(low) if h == 1 else low
            side = slice(128, 256) if odd else slice(0, 128)
            q = jnp.where(keep, q * BF(HD ** -0.5), BF(0))
            do = jnp.where(keep, do_ref[t, qs, side], BF(0))
            km = jnp.where(keep, k, BF(0))
            dd = (do.astype(F32) * c_ref[t, qs, side].astype(F32)).astype(BF)
            mine = (lane < 8) | ((lane >= 8 + 16 * h) & (lane < 24 + 16 * h))
            qe = jnp.concatenate([q, jnp.where(mine, marks, BF(0))], 1)
            s = dot(jnp.concatenate([k, kx], 1), qe, NT)
            dp = dot(jnp.concatenate([v, minus], 1), jnp.concatenate([do, dd], 1), NT)
            edge = jnp.where(below(True), s[width - BQ :], BIG)
            s = edge if width == BQ else jnp.concatenate([s[: width - BQ], edge], 0)
            p = jnp.exp(s)
            ds = (p * dp).astype(BF)
            gq = dot(ds, km, TN)
            grad = gq if grad is None else grad + gq
            dv_ref[kr, :] += dot(p.astype(BF), do)
            dk_ref[kr, :] += dot(ds, q)
        grad = (grad * HD ** -0.5).astype(BF)
        if odd:
            t_ref[t, qs, 384:512] = jnp.where(low, grad, t_ref[t, qs, 384:512])
        else:
            t_ref[t, qs, 0:128] = grad
    if odd:
        moved = pltpu.roll(dk_ref[...], 64, 1).astype(BF)
        t_ref[t, :, 384:512] = jnp.where(low, t_ref[t, :, 384:512], moved)
        t_ref[t, :, 512:640] = dv_ref[...].astype(BF)
    else:
        t_ref[t, :, 128:256] = dk_ref[...].astype(BF)
        t_ref[t, :, 256:384] = dv_ref[...].astype(BF)


def stats(v):
    mean = jnp.mean(v, axis=-1, keepdims=True)
    center = v - mean
    scale = lax.rsqrt(jnp.mean(center * center, axis=-1, keepdims=True) + EPS)
    return center * scale, scale


def norm_back(v, q, gain):
    n, scale = stats(v)
    e = q * gain
    back = scale * (e - jnp.mean(e, -1, keepdims=True) - n * jnp.mean(e * n, -1, keepdims=True))
    return back, jnp.sum(q * n, 0, keepdims=True), jnp.sum(q, 0, keepdims=True)


def kernel(
    inner, length,
    tok_in, cot_in, seg, valid, wq_in, wo_in, up_in, down_in, par_in,
    lo_out, gt_out, gq_out, go_out, gup_out, gdown_out, *rest,
):
    small_outs = rest[: 1 if inner > 1 else 5]
    (
        bq, bo, bm0, bm1, bm2,
        tok, cot, n1, tt, cc, ll, kx, k2, mid, n2, acc, gn, act, gu, val, par,
        dk, dv,
        m_sets, ar, ar_got,
        ag_send, ag_recv, rs_send, rs_recv, credit, ar_send, ar_recv, local_sem, own_sem,
    ) = rest[len(small_outs) :]
    width = tok.shape[1]
    bm = (bm0, bm1, bm2)
    blocks = [(bq, 0, 32), (bq, 32, 32), (bq, 64, 32), (bo, 0, 96)]
    blocks += [(b, r0, 96) for b in bm for r0 in (0, 96)]
    gathers = [
        Gather(f"gather{k}", inner, b, r0, rows, ag_send.at[k], ag_recv.at[k])
        for k, (b, r0, rows) in enumerate(blocks)
    ]
    here = Place(inner)
    mine = (here.x, here.c, here.z, here.y)

    def put_mlp(j):
        def put(total):
            gup_out[:, 256 * j : 256 * j + 256] = total[0:96]
            gdown_out[:, 256 * j : 256 * j + 256] = total[96:192]

        return put

    def put_out(total):
        go_out[...] = total.T[0 : 3 * HD]

    def put_pair(total):
        gq_out[0, :, 0:128] = total[0:96, 0:128]
        gq_out[1, :, 0:128] = total[0:96, 128:256]
        gq_out[2, 0:48, 0:128] = total[96:144, 0:128]
        gq_out[2, 48:96, 0:128] = total[96:144, 128:256]

    def put_odd(total):
        gq_out[0, :, 128:192] = total[:, 0:64]
        gq_out[1, :, 128:192] = total[:, 64:128]
        gq_out[2, :, 128:192] = total[:, 128:192]

    sets = [m_sets[0:6], m_sets[6:12], m_sets[12:18]]
    plan = [
        (bm0, 192, 0, 256, sets[0], put_mlp(0)), (bm1, 192, 0, 256, sets[1], put_mlp(1)),
        (bm2, 192, 0, 256, sets[2], put_mlp(2)), (bo, 96, 0, 256, sets[0], put_out),
        (bm0, 144, 0, 256, sets[1], put_pair), (bm1, 96, 0, 256, sets[2], put_odd),
    ]
    scatters = [
        Scatter(
            f"scatter{k}", inner, b, rows, col0, cols, slots,
            rs_send.at[k], rs_recv.at[k], credit.at[min(k, 2)], out,
        )
        for k, (b, rows, col0, cols, slots, out) in enumerate(plan)
    ]
    m_sum, o_sum, qa_sum, qb_sum = scatters[0:3], scatters[3], scatters[4], scatters[5]
    q_in, o_in, m_in = gathers[0:3], gathers[3], gathers[4:10]
    total = Total(inner, ar, ar_got, ar_send, ar_recv)

    def after(t, last, *steps):
        @pl.when(t == last)
        def _():
            for step in steps:
                step()

    def rows_of(i, size):
        return pl.ds(pl.multiple_of(i * size, size), size)

    def weight(buf, t, r0, rows, columns):
        return buf[t // 2, t % 2, :, :, r0 : r0 + rows, columns].reshape(8 * rows, -1)

    def cat(ref, s):
        return jnp.concatenate([ref[t, s, :] for t in range(4)], 1)

    def own_copies():
        copies = []
        for j in range(3):
            cols = pl.ds(256 * j, 256)
            copies.append((up_in.at[:, cols], bm[j].at[(*mine, pl.ds(0, 96))]))
            copies.append((down_in.at[:, cols], bm[j].at[(*mine, pl.ds(96, 96))]))
        copies += [(tok_in, tok), (cot_in, cot)]
        return [pltpu.make_async_copy(src, dst, own_sem.at[k]) for k, (src, dst) in enumerate(copies)]

    @phase
    def entry():
        for one in own_copies():
            one.start()
        greet(inner)
        q, k, v = (wq_in[n] for n in range(3))
        for n, one in enumerate((q, k, v)):
            bq[(*mine, slice(None), slice(128 * n, 128 * n + 128))] = one[:, 0:128]
        odd = [one[:, 128:192].astype(F32) for one in (q, k, v)]
        bq[(*mine, slice(None), slice(384, 512))] = jnp.concatenate(odd[0:2], 1).astype(BF)
        params = jnp.concatenate([par_in[...], jnp.zeros((124, 96), F32)], 0).T[:, 0:64]
        bq[(*mine, slice(None), slice(512, 640))] = jnp.concatenate([odd[2], params], 1).astype(BF)
        met(inner)

    @phase
    def document_marks():
        me_t = lax.axis_index("tp")
        row = seg[pl.ds(me_t, 1), :].astype(F32)
        lane_id = lax.broadcasted_iota(jnp.int32, (128, length), 0)
        marks = jnp.where(row == lane_id.astype(F32), 1.0, 0.0)
        marks = jnp.where(lane_id < 8, marks, 0.0)
        low4 = lane_id % 16
        ones = (lane_id >= 8) & (lane_id < 56) & (low4 >= 8) & (low4 < 11)
        marks = jnp.where(ones, 1.0, marks)
        marks = jnp.where(lane_id == 64, valid[...].astype(F32), marks)
        columns = marks.T
        val[...] = columns[:, 64:65]
        kx[...] = jnp.where(lanes() < 64, columns, 0.0).astype(BF)
        ar[0] = jnp.zeros_like(ar.at[0])
        count = jnp.sum(valid[...].astype(F32), axis=1, keepdims=True)
        ar[0, 7:8, 0:128] = jnp.broadcast_to(count, (1, 128))
        wide = jnp.concatenate([wo_in[...].astype(F32), jnp.zeros((64, 96), F32)], 0)
        bo[mine] = wide.T.astype(BF)

    @phase
    def first_norm_statistics():
        @pl.loop(0, length // 256)
        def _(i):
            s = rows_of(i, 256)
            mid[s, :] = stats(tok[s, :].astype(F32))[0]

    @phase
    def first_norm():
        par[...] = bq[here.x, here.c, :, :, :, 512:640].reshape(width, 128).astype(F32).T

        @pl.loop(0, length // 256)
        def _(i):
            s = rows_of(i, 256)
            n1[s, :] = (mid[s, :] * par[64:65, :] + par[65:66, :]).astype(BF)

    @phase
    def attention():
        @pl.loop(0, 4)
        def _(n):
            x, c = (here.x + n // 2) % 2, (here.c + n % 2) % 2
            t = 2 * x + c
            w = bq[x, c].reshape(width, 640)

            @pl.loop(0, length // 512)
            def _(i):
                s = rows_of(i, 512)
                tt[t, s, :] = dot(n1[s, :], w).astype(BF)

            after(n, 0, m_in[1].s1)
            after(n, 1, o_in.s3, m_in[1].s2, m_in[3].s1)
            after(n, 2, o_in.s4)
            after(n, 3, m_in[0].s4, m_in[2].s2, m_in[5].s1)
            attend(tt, ll, kx, k2, cc, t, length)
            after(n, 0, *[g.s4 for g in q_in], *[g.near for g in q_in], m_in[0].s2, m_in[2].s1)
            after(n, 1, m_in[0].s3, m_in[4].s1)
            after(n, 2, *[g.far for g in q_in], m_in[1].s3)
            after(n, 3, o_in.s5, m_in[3].s2, m_in[1].s4)

    @phase
    def out_projection():
        @pl.loop(0, length // 256)
        def _(i):
            s = rows_of(i, 256)
            branch = jnp.zeros((256, width), F32)
            for t in range(4):
                branch = branch + dot(cc[t, s, :], weight(bo, t, 0, 96, slice(0, 256)), NT)
            v = tok[s, :].astype(F32) + branch
            mid[s, :] = v
            ar[0, 5:6, :] += jnp.sum(val[s, :] * (branch * branch), 0, keepdims=True)
            n, _ = stats(v)
            n2[s, :] = (n * par[66:67, :] + par[67:68, :]).astype(BF)

    def mlp_hidden(j, *steps):
        b = bm[j]

        @phase
        def hidden():
            @pl.loop(0, 4)
            def _(t):
                up = weight(b, t, 0, 96, slice(0, 256))
                down = weight(b, t, 96, 96, slice(0, 256))

                for i in range(length // 512):
                    s = slice(512 * i, 512 * i + 512)
                    v = dot(n2[s, :], up)
                    ga = dot(cot[s, :], down)
                    v2 = v * v
                    th = jnp.tanh(v * (C0 + C1 * v2))
                    h = 0.5 + 0.5 * th
                    act[t, s, :] = (v * h).astype(BF)
                    slope = h + (0.5 * v) * (1.0 - th * th) * (C0 + (3.0 * C1) * v2)
                    gu[t, s, :] = (ga * slope).astype(BF)

                for k, step in enumerate(steps):
                    after(t, k, *step)

        hidden()

    def mlp_sums(j, *steps):
        b = bm[j]

        def wcat(r0):
            return jnp.concatenate([weight(b, t, r0, 96, slice(0, 256)) for t in range(4)], 1)

        @phase
        def sums():
            @pl.loop(0, length // 256)
            def _(i):
                s = rows_of(i, 256)
                one = dot(cat(act, s), wcat(96), NT)
                two = dot(cat(gu, s), wcat(0), NT)
                if j == 0:
                    acc[s, :] = one
                    gn[s, :] = two
                else:
                    acc[s, :] += one
                    gn[s, :] += two
                for k, step in enumerate(steps):
                    after(i, k, *step)

        sums()

    def mlp_weight_grads(j):
        b = bm[j]

        @phase
        def weight_grads():
            @pl.loop(0, 4)
            def _(t):
                gup = dot(n2[...], gu[t], TN).astype(BF)
                b[t // 2, t % 2, :, :, 0:96, :] = gup.reshape(4, 2, 96, 256)
                gdown = dot(cot[...], act[t], TN).astype(BF)
                b[t // 2, t % 2, :, :, 96:192, :] = gdown.reshape(4, 2, 96, 256)

        weight_grads()

    def store_low():
        return [
            pltpu.make_async_copy(gu.at[k], lo_out.at[:, pl.ds(256 * k, 256)], local_sem.at[k])
            for k in range(width // 256)
        ]

    @phase
    def second_norm_back():
        @pl.loop(0, length // 256)
        def _(i):
            s = rows_of(i, 256)
            v = mid[s, :]
            mlp = acc[s, :]
            out = v + mlp
            weight_rows = val[s, :]
            ar[0, 4:5, :] += jnp.sum(weight_rows * (out * out), 0, keepdims=True)
            ar[0, 6:7, :] += jnp.sum(weight_rows * (mlp * mlp), 0, keepdims=True)
            low_out = out.astype(BF)
            for k in range(width // 256):
                gu[k, s, :] = low_out[:, 256 * k : 256 * k + 256]
            back, g_gain, g_bias = norm_back(v, gn[s, :], par[66:67, :])
            ar[0, 2:3, :] += g_gain
            ar[0, 3:4, :] += g_bias
            grad = cot[s, :].astype(F32) + back
            mid[s, :] = grad
            n2[s, :] = grad.astype(BF)

        for one in store_low():
            one.start()

    @phase
    def out_projection_back():
        @pl.loop(0, 4)
        def _(t):
            w = weight(bo, t, 0, 96, slice(0, 256))
            act[t] = dot(n2[...], w).astype(BF)
            bo[t // 2, t % 2] = dot(n2[...], cc[t], TN).astype(BF).reshape(4, 2, 96, 256)

    @phase
    def pair_attention_back():
        @pl.loop(0, 4)
        def _(t):
            attend_back(tt, ll, kx, k2, cc, act, (dk, dv), (0, 1), t, length)
            after(t, 0, o_sum.s2, m_sum[2].s3)
            after(t, 1, m_sum[1].s5, m_sum[1].give_credit, o_sum.s3)
            after(t, 2, m_sum[2].s4)
            after(t, 3, o_sum.s4)

    @phase
    def pair_weight_grads():
        @pl.loop(0, 4)
        def _(t):
            grad = dot(n1[...], tt[t, :, 0:384], TN).astype(BF)
            x, c = t // 2, t % 2
            bm0[x, c, :, :, 0:96, :] = grad[:, 0:256].reshape(4, 2, 96, 256)
            third = grad[:, 256:384].reshape(4, 2, 96, 128)
            bm0[x, c, :, :, 96:144, 0:128] = third[:, :, 0:48]
            bm0[x, c, :, :, 96:144, 128:256] = third[:, :, 48:96]

    @phase
    def odd_weight_grads():
        @pl.loop(0, 4)
        def _(t):
            grad = dot(n1[...], tt[t, :, 384:640], TN).astype(BF)
            bm1[t // 2, t % 2, :, :, 0:96, :] = grad.reshape(4, 2, 96, 256)

    @phase
    def odd_attention_back():
        @pl.loop(0, 4)
        def _(t):
            attend_back(tt, ll, kx, k2, cc, act, (dk, dv), (2,), t, length)
            after(t, 0, qa_sum.s2, o_sum.s5)
            after(t, 1, m_sum[2].s5, m_sum[2].give_credit)
            after(t, 2, qa_sum.s3)

    def store_grad():
        return pltpu.make_async_copy(acc, gt_out, local_sem.at[4])

    @phase
    def first_norm_back():
        @pl.loop(0, length // 256)
        def _(i):
            s = rows_of(i, 256)
            grad = jnp.zeros((256, width), F32)
            for t in range(4):
                grad = grad + dot(tt[t, s, :], weight(bq, t, 0, 96, slice(0, 640)), NT)
            back, g_gain, g_bias = norm_back(tok[s, :].astype(F32), grad, par[64:65, :])
            ar[0, 0:1, :] += g_gain
            ar[0, 1:2, :] += g_bias
            acc[s, :] = mid[s, :] + back
            after(i, 0, qb_sum.s2)
            after(i, 1, qa_sum.s4)
            after(i, 2, qb_sum.s3)

        store_grad().start()

    @phase
    def small_results():
        sums = ar[2]
        if inner > 1:
            small_outs[0][...] = sums
            return
        share = width // 32
        owner = lax.axis_index("fsdp") * 4 + lax.axis_index("tp")
        moved = pltpu.roll(sums, width - owner * share, 1)
        for k in range(4):
            small_outs[k][...] = moved[k, 0:share]
        square = jnp.sum(sums[4:7], axis=1, keepdims=True) / (sums[7:8, 0:1] * width)
        rms = jnp.sqrt(jnp.broadcast_to(square, (3, 128)))
        lane = lanes()
        row = jnp.where(lane == 0, rms[0:1], jnp.where(lane == 1, rms[1:2], rms[2:3]))
        small_outs[4][...] = row[0, 0:3]

    entry()
    for g in q_in:
        g.s1()
    document_marks()
    own = own_copies()
    for one in own:
        one.wait()
    first_norm_statistics()
    q_in[0].s2()
    q_in[1].s2()
    q_in[0].s3()
    q_in[2].s2()
    o_in.s1()
    q_in[1].s3()
    m_in[0].s1()
    q_in[2].s3()
    first_norm()
    o_in.s2()
    attention()
    out_projection()
    m_in[0].s5()
    m_in[1].s5()

    mlp_hidden(0, (m_in[2].s3,), (m_in[4].s2,), (m_in[3].s3,))
    mlp_sums(0, (m_in[2].s4, m_in[5].s2), (m_in[4].s3,), (m_in[3].s4,))
    m_in[0].s6()
    m_in[1].s6()
    mlp_weight_grads(0)
    m_in[5].s3()
    m_sum[0].s1()
    m_in[2].s5()
    m_in[3].s5()

    mlp_hidden(1, (m_in[4].s4,), (), (m_sum[0].s2,))
    m_in[5].s4()
    mlp_sums(1)
    m_sum[0].s3()
    m_in[2].s6()
    m_in[3].s6()
    m_in[4].s5()
    m_in[5].s5()
    mlp_weight_grads(1)
    m_sum[1].s1()

    mlp_hidden(2, (), (), (m_sum[1].s2,))
    m_sum[0].s4()
    mlp_sums(2)
    m_sum[1].s3()
    m_in[4].s6()
    m_in[5].s6()
    mlp_weight_grads(2)
    m_sum[2].s1()

    second_norm_back()
    m_sum[2].s2()
    m_sum[0].s5()
    m_sum[0].give_credit()
    o_in.s6()
    out_projection_back()
    m_sum[1].s4()
    m_sum[0].take_credit()
    o_sum.s1()
    pair_attention_back()
    pair_weight_grads()
    m_sum[1].take_credit()
    qa_sum.s1()
    odd_attention_back()
    odd_weight_grads()
    m_sum[2].take_credit()
    qb_sum.s1()
    for g in q_in:
        g.s6()
    first_norm_back()
    total.run(0)
    total.take(0)
    total.run(1)
    qb_sum.s4()
    qa_sum.s5()
    total.take(1)
    total.left()
    small_results()
    for one in store_low():
        one.wait()
    store_grad().wait()
    qb_sum.s5()


def scatter_slots(rows, columns):
    return [
        pltpu.VMEM((2, 4, 2, rows, columns), BF),
        pltpu.VMEM((4, (rows // 2 + 15) // 16 * 16, columns), BF),
        pltpu.VMEM((4, rows // 2, columns), BF),
        pltpu.VMEM((4, rows, columns), BF),
        pltpu.VMEM((4, rows, columns), BF),
        pltpu.VMEM((3, rows, columns), BF),
    ]


def layer(inner, tokens, cotangent, segments, valid, wq, wo, up, down, params):
    length, width = tokens.shape
    block = lambda rows, columns: pltpu.VMEM((2, 2, 4, 2, rows, columns), BF)
    scratch = [
        block(96, 640), block(96, 256), block(192, 256), block(192, 256), block(192, 256),
        pltpu.VMEM((length, width), BF),
        pltpu.VMEM((length, width), BF),
        pltpu.VMEM((length, width), BF),
        pltpu.VMEM((4, length, 640), BF),
        pltpu.VMEM((4, length, 256), BF),
        pltpu.VMEM((4, length, 128), BF),
        pltpu.VMEM((length, 128), BF),
        pltpu.VMEM((length, 128), BF),
        pltpu.VMEM((length, width), F32),
        pltpu.VMEM((length, width), BF),
        pltpu.VMEM((length, width), F32),
        pltpu.VMEM((length, width), F32),
        pltpu.VMEM((4, length, 256), BF),
        pltpu.VMEM((4, length, 256), BF),
        pltpu.VMEM((length, 1), F32),
        pltpu.VMEM((128, width), F32),
    ]
    scratch += [pltpu.VMEM((length, 128), F32)] * 2
    scratch += [scatter_slots(192, 256) * 3]
    scratch += [
        pltpu.VMEM((3, 8, width), F32),
        pltpu.VMEM((10, 8, width), F32),
        pltpu.SemaphoreType.DMA((10, 11)),
        pltpu.SemaphoreType.DMA((10, 11)),
        pltpu.SemaphoreType.DMA((6, 8)),
        pltpu.SemaphoreType.DMA((6, 8)),
        pltpu.SemaphoreType.REGULAR((3, 6)),
        pltpu.SemaphoreType.DMA((10,)),
        pltpu.SemaphoreType.DMA((10,)),
        pltpu.SemaphoreType.DMA((5,)),
        pltpu.SemaphoreType.DMA((8,)),
    ]
    vmem, anywhere = pl.BlockSpec(memory_space=pltpu.VMEM), pl.BlockSpec(memory_space=pl.ANY)
    small = [(8, width)] if inner > 1 else [(width // 32,)] * 4 + [(3,)]
    shapes = [(3, 96, 3 * HD), (3 * HD, 96), (96, width), (96, width)] + small
    return pl.pallas_call(
        partial(kernel, inner, length),
        out_shape=[
            jax.ShapeDtypeStruct((length, width), BF),
            jax.ShapeDtypeStruct((length, width), F32),
        ]
        + [jax.ShapeDtypeStruct(shape, F32) for shape in shapes],
        in_specs=[anywhere, anywhere, vmem, vmem, vmem, vmem, anywhere, anywhere, vmem],
        out_specs=[anywhere, anywhere] + [vmem] * len(shapes),
        scratch_shapes=scratch,
        compiler_params=pltpu.CompilerParams(
            collective_id=0, has_side_effects=True, vmem_limit_bytes=63 * 2**20
        ),
    )(tokens, cotangent, segments, valid, wq, wo, up, down, params)


def hand_over(arrays):
    count = len(arrays)
    pieces = []
    for k, a in enumerate(arrays):
        step = 256 if a.ndim == 2 and a.shape[0] % 256 == 0 else a.shape[0]
        pieces += [(k, start, step) for start in range(0, a.shape[0], step)]

    def body(*refs):
        came, went, held = refs[:count], refs[count : 2 * count], refs[2 * count : 3 * count]
        sems = refs[-1]

        def copy(n, into):
            k, start, step = pieces[n]
            part = (lambda ref: ref.at[pl.ds(start, step)]) if step < came[k].shape[0] else (lambda ref: ref)
            if into:
                return pltpu.make_async_copy(part(came[k]), part(held[k]), sems.at[0, n])
            return pltpu.make_async_copy(part(held[k]), part(went[k]), sems.at[1, n])

        for n in range(len(pieces)):
            copy(n, True).start()
        for n in range(len(pieces)):
            copy(n, True).wait()
            copy(n, False).start()
        for n in range(len(pieces)):
            copy(n, False).wait()

    anywhere = pl.BlockSpec(memory_space=pltpu.HBM)
    return pl.pallas_call(
        body,
        out_shape=[jax.ShapeDtypeStruct(a.shape, a.dtype) for a in arrays],
        in_specs=[anywhere] * count,
        out_specs=[anywhere] * count,
        scratch_shapes=[pltpu.VMEM(a.shape, a.dtype) for a in arrays]
        + [pltpu.SemaphoreType.DMA((2, len(pieces)))],
        compiler_params=pltpu.CompilerParams(vmem_limit_bytes=63 * 2**20),
    )(*arrays)


def local(
    tokens, segment_ids, valid, ln1_gain, ln1_bias, w_qkv, w_out, ln2_gain, ln2_bias, w_up, w_down, cotangent
):
    length, width = tokens.shape
    holders = lax.axis_size("fsdp")
    inner = holders // 8
    groups = [[g * inner + i for i in range(inner)] for g in range(8)]

    def widen(block, axis=0):
        if inner == 1:
            return block
        return lax.all_gather(block, "fsdp", axis_index_groups=groups, axis=axis, tiled=True)

    def narrow(block, axis=0):
        if inner == 1:
            return block
        return lax.psum_scatter(
            block, "fsdp", scatter_dimension=axis, axis_index_groups=groups, tiled=True
        )

    params = widen(jnp.stack([ln1_gain, ln1_bias, ln2_gain, ln2_bias]), 1).astype(F32)
    results = layer(
        inner, tokens, cotangent, segment_ids, valid.reshape(1, length),
        widen(w_qkv.transpose(1, 0, 2), 1), widen(w_out, 1), widen(w_up), widen(w_down.T), params,
    )
    low, grad_tokens, gq, go, gup, gdown, *small = hand_over(results)
    if inner > 1:
        sums = lax.psum(small[0], "fsdp", axis_index_groups=groups)
        share = width // (holders * lax.axis_size("tp"))
        owner = lax.axis_index("fsdp") * lax.axis_size("tp") + lax.axis_index("tp")
        mine = lax.dynamic_slice_in_dim(sums[0:4], owner * share, share, 1)
        spread = jnp.sqrt(jnp.sum(sums[4:7], axis=1) / (sums[7, 0] * width))
        small = (mine[0], mine[1], mine[2], mine[3], spread)
    return (
        low, grad_tokens, small[0], small[1], narrow(gq, 1).transpose(1, 0, 2), narrow(go, 1),
        small[2], small[3], narrow(gup), narrow(gdown).T, small[4],
    )


def solution(mesh):
    both = ("fsdp", "tp")
    return jax.shard_map(
        local,
        mesh=mesh,
        in_specs=(
            P(both, None), P("fsdp", None), P(both), P("fsdp"), P("fsdp"), P("fsdp", None, "tp"),
            P("tp", "fsdp"), P("fsdp"), P("fsdp"), P("fsdp", "tp"), P("tp", "fsdp"), P(both, None),
        ),
        out_specs=(
            P(both, None), P(both, None), P(both), P(both), P("fsdp", None, "tp"), P("tp", "fsdp"),
            P(both), P(both), P("fsdp", "tp"), P("tp", "fsdp"), P(),
        ),
        check_vma=False,
    )
```

```python
from functools import partial

import jax
import jax.numpy as jnp
from jax import lax
from jax.experimental import pallas as pl
from jax.experimental.pallas import tpu as pltpu
from jax.sharding import PartitionSpec as P

HD = 64
BQ = 256
EPS = 1e-05
BIG = -1e30
F32 = jnp.float32
BF = jnp.bfloat16
NN = (((1,), (0,)), ((), ()))
NT = (((1,), (1,)), ((), ()))
TN = (((0,), (0,)), ((), ()))
MESH = pl.DeviceIdType.MESH
C0 = 0.7978845608
C1 = 0.7978845608 * 0.044715


def dot(a, b, dims=NN):
    return lax.dot_general(a, b, dims, preferred_element_type=F32)


def phase(body):
    return body


def remote(src, dst, send, recv, device):
    return pltpu.make_async_remote_copy(
        src_ref=src, dst_ref=dst, send_sem=send, recv_sem=recv,
        device_id=device, device_id_type=MESH,
    )


class Place:
    def __init__(self, inner):
        f = lax.axis_index("fsdp")
        t = lax.axis_index("tp")
        g = f // inner
        self.low = f % inner
        self.inner = inner
        self.z, self.y, self.x, self.c = g // 2, g % 2, t // 2, t % 2

    def device(self, z, y, x, c):
        return ((z * 2 + y) * self.inner + self.low, x * 2 + c)

    def core(self):
        return self.device(self.z, self.y, self.x, 1 - self.c)

    def xn(self):
        return self.device(self.z, self.y, 1 - self.x, self.c)

    def yn(self):
        return self.device(self.z, 1 - self.y, self.x, self.c)

    def cube(self, n):
        y, x, c = (self.y + n // 4) % 2, (self.x + n // 2) % 2, (self.c + n) % 2
        return self.device(self.z, y, x, c)

    def zn(self, d):
        return self.device((self.z + d) % 4, self.y, self.x, self.c)

    def zp(self, d):
        return self.device((self.z - d + 4) % 4, self.y, self.x, self.c)


def greet(inner):
    p = Place(inner)
    sem = pltpu.get_barrier_semaphore()
    for dev in [p.cube(n) for n in range(1, 8)] + [p.zn(d) for d in range(1, 4)]:
        pl.semaphore_signal(sem, inc=1, device_id=dev, device_id_type=MESH)


def met(inner):
    pl.semaphore_wait(pltpu.get_barrier_semaphore(), 10)


class Gather:
    def __init__(self, name, inner, buf, row0, rows, send, recv):
        self.name = name
        self.inner, self.buf, self.row0, self.rows = inner, buf, row0, rows
        self.send, self.recv = send, recv

    def own(self, x, c, z, y):
        return self.buf.at[x, c, z, y, pl.ds(self.row0, self.rows)]

    def group(self, x, c, y, half=None):
        start, size = self.row0, self.rows
        if half is not None:
            size = self.rows // 2
            start = self.row0 + half * size
        return self.buf.at[x, c, :, y, pl.ds(start, size)]

    def parts(self, slot):
        p = Place(self.inner)
        x, c, z, y = p.x, p.c, p.z, p.y
        if slot < 3:
            d = slot + 1
            return self.own(x, c, z, y), self.own(x, c, (z - d + 4) % 4, y), p.zn(d)
        if slot == 3:
            return self.group(x, c, y), self.group(1 - x, c, y), p.xn()
        if slot == 4:
            return self.group(x, c, y), self.group(x, c, 1 - y), p.yn()
        if slot == 5:
            return self.group(1 - x, c, y, 0), self.group(1 - x, c, 1 - y, 0), p.yn()
        if slot == 6:
            return self.group(x, c, 1 - y, 1), self.group(1 - x, c, 1 - y, 1), p.xn()
        xx = x if slot in (7, 9) else 1 - x
        yy = y if slot in (7, 8) else 1 - y
        return self.group(xx, c, yy), self.group(xx, 1 - c, yy), p.core()

    def start(self, *slots):
        for slot in slots:
            mine, _, dev = self.parts(slot)
            remote(mine, mine, self.send.at[slot], self.recv.at[slot], dev).start()

    def arrive(self, *slots):
        for slot in slots:
            _, theirs, dev = self.parts(slot)
            remote(theirs, theirs, self.send.at[slot], self.recv.at[slot], dev).wait_recv()

    def left(self, *slots):
        for slot in slots:
            mine, _, dev = self.parts(slot)
            remote(mine, mine, self.send.at[slot], self.recv.at[slot], dev).wait_send()

    def s1(self):
        self.start(0, 1, 2)

    def s2(self):
        self.arrive(0, 1, 2)
        self.start(3, 4, 7)

    def s3(self):
        self.arrive(4)
        self.start(6, 9)
        self.arrive(3)
        self.start(5, 8)

    def s4(self):
        self.arrive(5, 6)
        self.start(10)

    def near(self):
        self.arrive(7, 9)

    def far(self):
        self.arrive(8, 10)

    def s5(self):
        self.near()
        self.far()

    def s6(self):
        self.left(*range(11))


class Scatter:
    def __init__(self, name, inner, buf, block, slots, place, send, recv, credit, out):
        self.name = name
        self.inner, self.buf, self.slots = inner, buf, slots
        self.row0, self.rows, self.col0, columns = block
        self.half = (self.rows // 2 + 15) // 16 * 16
        row, upper, lower, col = place
        self.land = (
            slice(row, row + self.rows), slice(upper, upper + self.half),
            slice(lower, lower + self.rows - self.half), slice(col, col + columns),
        )
        self.cols = slice(self.col0, self.col0 + columns)
        self.send, self.recv = send, recv
        self.credit, self.out = credit, out

    def parts(self, slot):
        p = Place(self.inner)
        x, c, z, y = p.x, p.c, p.z, p.y
        buf, cols = self.buf, self.cols
        r1, ra, rb, rx, ry, rz = self.slots
        rows, upper, lower = self.spans()
        land, land_a, land_b, land_cols = self.land
        if slot == 0:
            return buf.at[:, 1 - c, :, :, rows, cols], r1.at[:, :, :, land, land_cols], p.core()
        if slot == 1:
            return buf.at[1 - x, c, :, 1 - y, upper, cols], ra.at[:, land_a, land_cols], p.yn()
        if slot == 2:
            return buf.at[1 - x, c, :, 1 - y, lower, cols], rb.at[:, land_b, land_cols], p.xn()
        if slot == 3:
            return buf.at[1 - x, c, :, y, rows, cols], rx.at[:, land, land_cols], p.xn()
        if slot == 4:
            return buf.at[x, c, :, 1 - y, rows, cols], ry.at[:, land, land_cols], p.yn()
        d = slot - 4
        return buf.at[x, c, (z + d) % 4, y, rows, cols], rz.at[d - 1, land, land_cols], p.zn(d)

    def spans(self):
        start, end = self.row0, self.row0 + self.rows
        return slice(start, end), slice(start, start + self.half), slice(start + self.half, end)

    def start(self, *slots):
        for slot in slots:
            src, dst, dev = self.parts(slot)
            remote(src, dst, self.send.at[slot], self.recv.at[slot], dev).start()

    def arrive(self, *slots):
        for slot in slots:
            _, dst, dev = self.parts(slot)
            remote(dst, dst, self.send.at[slot], self.recv.at[slot], dev).wait_recv()

    def left(self):
        for slot in range(8):
            src, dst, dev = self.parts(slot)
            remote(src, dst, self.send.at[slot], self.recv.at[slot], dev).wait_send()

    def take_credit(self):
        for i in range(6):
            pl.semaphore_wait(self.credit.at[i], 1)

    def give_credit(self):
        p = Place(self.inner)
        for i, dev in enumerate((p.core(), p.xn(), p.yn(), p.zp(1), p.zp(2), p.zp(3))):
            pl.semaphore_signal(self.credit.at[i], inc=1, device_id=dev, device_id_type=MESH)

    def s1(self):
        self.start(0)

    def add(self, x, y, rows, *others):
        c = Place(self.inner).c

        @pl.loop(0, 4)
        def _(z):
            total = self.buf[x, c, z, y, rows, self.cols].astype(F32)
            for other in others:
                total = total + other(z).astype(F32)
            self.buf[x, c, z, y, rows, self.cols] = total.astype(BF)

    def s2(self):
        p = Place(self.inner)
        r1, (land, _, _, cols) = self.slots[0], self.land
        self.arrive(0)
        for x, y in ((1 - p.x, 1 - p.y), (1 - p.x, p.y), (p.x, 1 - p.y), (p.x, p.y)):
            self.add(x, y, self.spans()[0], lambda z: r1[x, z, y, land, cols])
            if x is not p.x and y is not p.y:
                self.start(1, 2)

    def s3(self):
        p = Place(self.inner)
        _, upper, lower = self.spans()
        _, land_a, land_b, cols = self.land
        ra, rb = self.slots[1:3]
        self.arrive(1)
        self.add(1 - p.x, p.y, upper, lambda z: ra[z, land_a, cols])
        self.start(3)
        self.arrive(2)
        self.add(p.x, 1 - p.y, lower, lambda z: rb[z, land_b, cols])
        self.start(4)

    def s4(self):
        p = Place(self.inner)
        land, _, _, cols = self.land
        rx, ry = self.slots[3:5]
        self.arrive(3, 4)
        self.add(p.x, p.y, self.spans()[0], lambda z: rx[z, land, cols], lambda z: ry[z, land, cols])
        self.start(5, 6, 7)

    def s5(self):
        p = Place(self.inner)
        land, _, _, cols = self.land
        rz = self.slots[5]
        self.arrive(5, 6, 7)
        total = self.buf[p.x, p.c, p.z, p.y, self.spans()[0], self.cols].astype(F32)
        for d in range(3):
            total = total + rz[d, land, cols].astype(F32)
        self.out(total)
        self.left()


class Total:
    def __init__(self, name, inner, ref, got, send, recv):
        self.name = name
        self.inner, self.ref, self.got, self.send, self.recv = inner, ref, got, send, recv

    def copy(self, slot):
        p = Place(self.inner)
        dev = p.cube(slot + 1) if slot < 7 else p.zn(slot - 6)
        stage = 0 if slot < 7 else 1
        return remote(self.ref.at[stage], self.got.at[slot], self.send.at[slot], self.recv.at[slot], dev)

    def slots(self, stage):
        return range(7) if stage == 0 else range(7, 10)

    def run(self, stage):
        for slot in self.slots(stage):
            self.copy(slot).start()

    def take(self, stage):
        total = self.ref[stage]
        for slot in self.slots(stage):
            self.copy(slot).wait_recv()
            total = total + self.got[slot]
        self.ref[stage + 1] = total

    def left(self):
        for slot in range(10):
            self.copy(slot).wait_send()


def head_parts(t_ref, k2_ref, t, h, qs, kr):
    if h < 2:
        return t_ref[t, qs, 0:128], t_ref[t, kr, 128:256], t_ref[t, kr, 256:384]
    return t_ref[t, qs, 384:512], k2_ref[kr, :], t_ref[t, kr, 512:640]


def lanes():
    return lax.broadcasted_iota(jnp.int32, (1, 128), 1)


def roll_key(t_ref, k2_ref, t):
    k2_ref[...] = pltpu.roll(t_ref[t, :, 384:512].astype(F32), 64, 1).astype(BF)


def below(transposed):
    r = lax.broadcasted_iota(jnp.int32, (BQ, BQ), 0)
    c = lax.broadcasted_iota(jnp.int32, (BQ, BQ), 1)
    return r <= c if transposed else r >= c


def attend(t_ref, l_ref, kx_ref, k2_ref, c_ref, t, length):
    lane = lanes()
    low = lane < 64
    roll_key(t_ref, k2_ref, t)
    for i in range(length // BQ):
        first = max(0, i * BQ - length // 2)
        width = (i + 1) * BQ - first
        qs, kr = slice(i * BQ, (i + 1) * BQ), slice(first, first + width)
        kx = kx_ref[kr, :]
        doc = kx_ref[qs, :].astype(F32)
        qx = jnp.where(lane < 8, BIG * (1.0 - doc), 0.0).astype(BF)
        marks = qx
        outs = []
        for h in range(3):
            q, k, v = head_parts(t_ref, k2_ref, t, h, qs, kr)
            keep = jnp.logical_not(low) if h == 1 else low
            q = jnp.where(keep, q * BF(HD ** -0.5), BF(0))
            s = dot(jnp.concatenate([q, qx], 1), jnp.concatenate([k, kx], 1), NT)
            edge = jnp.where(below(False), s[:, width - BQ :], BIG)
            s = edge if width == BQ else jnp.concatenate([s[:, : width - BQ], edge], 1)
            top = jnp.max(s, axis=1, keepdims=True)
            p = jnp.exp(s - top).astype(BF)
            both = dot(p, jnp.concatenate([v, jnp.ones((width, 128), BF)], 1))
            total = both[:, 128:256]
            outs.append(both[:, :128] / total)
            rest = -(top + jnp.log(total))
            for n in range(3):
                piece = rest.astype(BF)
                marks = jnp.where(lane == 8 + 16 * h + n, piece, marks)
                rest = rest - piece.astype(F32)
        l_ref[t, qs, :] = marks
        c_ref[t, qs, 0:128] = jnp.where(low, outs[0], outs[1]).astype(BF)
        c_ref[t, qs, 128:256] = jnp.where(low, outs[2], 0.0).astype(BF)


def attend_back(t_ref, l_ref, kx_ref, k2_ref, kt_ref, c_ref, do_ref, sums, heads, t, length):
    lane = lanes()
    low = lane < 64
    dk_ref, dv_ref = sums
    odd = heads == (2,)
    if odd:
        roll_key(t_ref, k2_ref, t)
        kt_ref[...] = k2_ref[...].T
    else:
        kt_ref[...] = t_ref[t, :, 128:256].T
    for ref in sums:
        ref[...] = jnp.zeros_like(ref)
    for i in range(length // BQ):
        first = max(0, i * BQ - length // 2)
        width = (i + 1) * BQ - first
        qs, kr = slice(i * BQ, (i + 1) * BQ), slice(first, first + width)
        marks = l_ref[t, qs, :]
        side = slice(128, 256) if odd else slice(0, 128)
        qs_all, dos, left, right = [], [], [], []
        for h in heads:
            q, k, v = head_parts(t_ref, k2_ref, t, h, qs, kr)
            keep = jnp.logical_not(low) if h == 1 else low
            q = jnp.where(keep, q * BF(HD ** -0.5), BF(0))
            do = jnp.where(keep, do_ref[t, qs, side], BF(0))
            dd = (do.astype(F32) * c_ref[t, qs, side].astype(F32)).astype(BF)
            mine = (lane < 8) | ((lane >= 8 + 16 * h) & (lane < 24 + 16 * h))
            qs_all.append(q)
            dos.append(do)
            left.append(jnp.concatenate([q, jnp.where(mine, marks, BF(0))], 1))
            right.append(jnp.concatenate([do, dd], 1))
        s_all = dot(jnp.concatenate([k, kx_ref[kr, :]], 1), jnp.concatenate(left, 0), NT)
        minus = jnp.full((width, 128), -1.0, BF)
        dp_all = dot(jnp.concatenate([v, minus], 1), jnp.concatenate(right, 0), NT)
        ps, dss, grads = [], [], []
        for n in range(len(heads)):
            s = s_all[:, n * BQ : (n + 1) * BQ]
            edge = jnp.where(below(True), s[width - BQ :], BIG)
            s = edge if width == BQ else jnp.concatenate([s[: width - BQ], edge], 0)
            p = jnp.exp(s)
            ds = (p * dp_all[:, n * BQ : (n + 1) * BQ]).astype(BF)
            ps.append(p.astype(BF))
            dss.append(ds)
            grads.append(dot(kt_ref[64 * n : 64 * n + 64, kr], ds))
        if odd:
            grads.append(jnp.zeros((64, BQ), F32))
        grad = (jnp.concatenate(grads, 0).T * HD ** -0.5).astype(BF)
        dv_ref[kr, :] += dot(jnp.concatenate(ps, 1), jnp.concatenate(dos, 0))
        dk_ref[kr, :] += dot(jnp.concatenate(dss, 1), jnp.concatenate(qs_all, 0))
        if odd:
            t_ref[t, qs, 384:512] = jnp.where(low, grad, t_ref[t, qs, 384:512])
        else:
            t_ref[t, qs, 0:128] = grad
    if odd:
        moved = pltpu.roll(dk_ref[...], 64, 1).astype(BF)
        t_ref[t, :, 384:512] = jnp.where(low, t_ref[t, :, 384:512], moved)
        t_ref[t, :, 512:640] = dv_ref[...].astype(BF)
    else:
        t_ref[t, :, 128:256] = dk_ref[...].astype(BF)
        t_ref[t, :, 256:384] = dv_ref[...].astype(BF)


def stats(v):
    mean = jnp.mean(v, axis=-1, keepdims=True)
    center = v - mean
    scale = lax.rsqrt(jnp.mean(center * center, axis=-1, keepdims=True) + EPS)
    return center * scale, scale


def norm_back(v, q, gain):
    n, scale = stats(v)
    e = q * gain
    back = scale * (e - jnp.mean(e, -1, keepdims=True) - n * jnp.mean(e * n, -1, keepdims=True))
    return back, jnp.sum(q * n, 0, keepdims=True), jnp.sum(q, 0, keepdims=True)


def kernel(
    inner, length,
    tok_in, cot_in, seg, valid, wq_in, wo_in, up_in, down_in, par_in,
    lo_out, gt_out, *rest,
):
    big_outs = rest[0:5]
    (
        gq_out, go_out, gup_out, gdown_out, small_out,
        bq, bo, bm0, bm1, bm2, gb,
        tok, cot, n1, tt, cc, ll, kx, k2, kt, mid, n2, acc, gn, act, gu, val, par,
        dk, dv,
        m_sets, ar, ar_got, br, br_got, g1,
        ag_send, ag_recv, rs_send, rs_recv, credit, ar_send, ar_recv, local_sem, own_sem, give_sem,
    ) = rest[5:]
    width = tok.shape[1]
    bm = (bm0, bm1, bm2)
    blocks = [(bq, 0, 32), (bq, 32, 32), (bq, 64, 32), (bo, 0, 96)]
    blocks += [(b, r0, 96) for b in bm for r0 in (0, 96)]
    gathers = [
        Gather(f"gather{k}", inner, b, r0, rows, ag_send.at[k], ag_recv.at[k])
        for k, (b, r0, rows) in enumerate(blocks)
    ]
    here = Place(inner)
    mine = (here.x, here.c, here.z, here.y)

    def put_mlp(j):
        def put(total):
            gup_out[:, 256 * j : 256 * j + 256] = total[0:96]
            gdown_out[:, 256 * j : 256 * j + 256] = total[96:192]

        return put

    def put_out(total):
        go_out[0 : 2 * HD] = total[0:96].T
        third = total[96:144].T
        go_out[2 * HD : 3 * HD] = jnp.concatenate([third[0:64], third[64:128]], 1)

    def put_pair(total):
        gq_out[0, :, 0:128] = total[0:96, 0:128]
        gq_out[1, :, 0:128] = total[0:96, 128:256]
        gq_out[2, 0:48, 0:128] = total[96:144, 0:128]
        gq_out[2, 48:96, 0:128] = total[96:144, 128:256]

    def put_odd(total):
        gq_out[0, 0:80, 128:192] = total[:, 0:64]
        gq_out[1, 0:80, 128:192] = total[:, 64:128]

    def put_rest(total):
        gq_out[0, 80:96, 128:192] = total[0:16, 0:64]
        gq_out[1, 80:96, 128:192] = total[0:16, 64:128]
        gq_out[2, 0:48, 128:192] = total[16:64, 0:64]
        gq_out[2, 48:96, 128:192] = total[16:64, 64:128]

    grads = (gb, bm0, bm1)
    sets = [m_sets[0:6], m_sets[6:12], m_sets[12:18]]
    start = (0, 0, 0, 0)
    plan = [
        (gb, (0, 192, 0, 256), sets[0], start, put_mlp(0)),
        (bm0, (0, 192, 0, 256), sets[1], start, put_mlp(1)),
        (bm1, (0, 192, 0, 256), sets[2], start, put_mlp(2)),
        (bm2, (0, 144, 0, 128), sets[0], start, put_out),
        (gb, (0, 144, 0, 256), sets[1], start, put_pair),
        (bm2, (0, 80, 128, 128), sets[0], (0, 0, 0, 128), put_odd),
        (bm2, (80, 64, 128, 128), sets[0], (80, 48, 32, 128), put_rest),
    ]
    scatters = [
        Scatter(
            f"scatter{k}", inner, b, block, slots, place,
            rs_send.at[k], rs_recv.at[k], credit.at[min(k, 1)], out,
        )
        for k, (b, block, slots, place, out) in enumerate(plan)
    ]
    m_sum, o_sum, qa_sum, qb_sum, qc_sum = scatters[0:3], *scatters[3:7]
    q_in, o_in, m_in = gathers[0:3], gathers[3], gathers[4:10]
    early = Total("early", inner, ar, ar_got, ar_send.at[0], ar_recv.at[0])
    late = Total("late", inner, br, br_got, ar_send.at[1], ar_recv.at[1])

    def after(t, last, *steps):
        @pl.when(t == last)
        def _():
            for step in steps:
                step()

    def rows_of(i, size):
        return pl.ds(pl.multiple_of(i * size, size), size)

    def weight(buf, t, r0, rows, columns):
        return buf[t // 2, t % 2, :, :, r0 : r0 + rows, columns].reshape(8 * rows, -1)

    def fold(columns):
        parts = columns.reshape(8, 96, 64)
        halves = [parts[:, 48 * n : 48 * n + 48].reshape(8 * 48, 64) for n in range(2)]
        return jnp.concatenate(halves, 1).astype(BF).reshape(4, 2, 48, 128)

    def cat(ref, s):
        return jnp.concatenate([ref[t, s, :] for t in range(4)], 1)

    def own_copies():
        copies = []
        for j in range(3):
            cols = pl.ds(256 * j, 256)
            copies.append((up_in.at[:, cols], bm[j].at[(*mine, pl.ds(0, 96))]))
            copies.append((down_in.at[:, cols], bm[j].at[(*mine, pl.ds(96, 96))]))
        copies += [(tok_in, tok), (cot_in, cot)]
        return [pltpu.make_async_copy(src, dst, own_sem.at[k]) for k, (src, dst) in enumerate(copies)]

    @phase
    def entry():
        for one in own_copies():
            one.start()
        greet(inner)
        q, k, v = (wq_in[n] for n in range(3))
        for n, one in enumerate((q, k, v)):
            bq[(*mine, slice(None), slice(128 * n, 128 * n + 128))] = one[:, 0:128]
        odd = [one[:, 128:192].astype(F32) for one in (q, k, v)]
        bq[(*mine, slice(None), slice(384, 512))] = jnp.concatenate(odd[0:2], 1).astype(BF)
        params = jnp.concatenate([par_in[...], jnp.zeros((124, 96), F32)], 0).T[:, 0:64]
        bq[(*mine, slice(None), slice(512, 640))] = jnp.concatenate([odd[2], params], 1).astype(BF)
        met(inner)

    @phase
    def document_marks():
        me_t = lax.axis_index("tp")
        row = seg[pl.ds(me_t, 1), :].astype(F32)
        lane_id = lax.broadcasted_iota(jnp.int32, (128, length), 0)
        marks = jnp.where(row == lane_id.astype(F32), 1.0, 0.0)
        marks = jnp.where(lane_id < 8, marks, 0.0)
        low4 = lane_id % 16
        ones = (lane_id >= 8) & (lane_id < 56) & (low4 >= 8) & (low4 < 11)
        marks = jnp.where(ones, 1.0, marks)
        marks = jnp.where(lane_id == 64, valid[...].astype(F32), marks)
        columns = marks.T
        val[...] = columns[:, 64:65]
        kx[...] = jnp.where(lanes() < 64, columns, 0.0).astype(BF)
        ar[0] = jnp.zeros_like(ar.at[0])
        br[0] = jnp.zeros_like(br.at[0])
        g1[...] = jnp.zeros_like(g1)
        count = jnp.sum(valid[...].astype(F32), axis=1, keepdims=True)
        ar[0, 7:8, 0:128] = jnp.broadcast_to(count, (1, 128))
        wide = jnp.concatenate([wo_in[...].astype(F32), jnp.zeros((64, 96), F32)], 0)
        bo[mine] = wide.T.astype(BF)

    @phase
    def first_norm_statistics():
        @pl.loop(0, length // 256)
        def _(i):
            s = rows_of(i, 256)
            mid[s, :] = stats(tok[s, :].astype(F32))[0]

    @phase
    def first_norm():
        par[...] = bq[here.x, here.c, :, :, :, 512:640].reshape(width, 128).astype(F32).T

        @pl.loop(0, length // 256)
        def _(i):
            s = rows_of(i, 256)
            n1[s, :] = (mid[s, :] * par[64:65, :] + par[65:66, :]).astype(BF)

    @phase
    def attention():
        @pl.loop(0, 4)
        def _(n):
            x, c = (here.x + n // 2) % 2, (here.c + n % 2) % 2
            t = 2 * x + c
            w = bq[x, c].reshape(width, 640)

            @pl.loop(0, length // 512)
            def _(i):
                s = rows_of(i, 512)
                tt[t, s, :] = dot(n1[s, :], w).astype(BF)

            after(n, 1, m_in[1].s2, m_in[2].s1)
            after(n, 2, m_in[0].s3)
            after(n, 3, o_in.s4, m_in[2].s2, m_in[5].s1)
            attend(tt, ll, kx, k2, cc, t, length)
            after(n, 0, *[g.s4 for g in q_in], *[g.near for g in q_in], m_in[0].s2)
            after(n, 1, o_in.s3, m_in[3].s1)
            after(n, 2, *[g.far for g in q_in], m_in[1].s3, m_in[4].s1)
            after(n, 3, m_in[0].s4, m_in[3].s2, m_in[1].s4, o_in.s5)

    @phase
    def out_projection():
        @pl.loop(0, length // 256)
        def _(i):
            s = rows_of(i, 256)
            branch = jnp.zeros((256, width), F32)
            for t in range(4):
                branch = branch + dot(cc[t, s, :], weight(bo, t, 0, 96, slice(0, 256)), NT)
            v = tok[s, :].astype(F32) + branch
            mid[s, :] = v
            ar[0, 5:6, :] += jnp.sum(val[s, :] * (branch * branch), 0, keepdims=True)
            n, _ = stats(v)
            n2[s, :] = (n * par[66:67, :] + par[67:68, :]).astype(BF)

    def mlp_hidden(j, *steps):
        b = bm[j]

        @phase
        def hidden():
            @pl.loop(0, 4)
            def _(t):
                up = weight(b, t, 0, 96, slice(0, 256))
                down = weight(b, t, 96, 96, slice(0, 256))

                def finish(s, v, ga):
                    v2 = v * v
                    th = jnp.tanh(v * (C0 + C1 * v2))
                    h = 0.5 + 0.5 * th
                    act[t, s, :] = (v * h).astype(BF)
                    slope = h + (0.5 * v) * (1.0 - th * th) * (C0 + (3.0 * C1) * v2)
                    gu[t, s, :] = (ga * slope).astype(BF)

                waiting = None
                for i in range(length // 128):
                    s = slice(128 * i, 128 * i + 128)
                    now = (s, dot(n2[s, :], up), dot(cot[s, :], down))
                    if waiting is not None:
                        finish(*waiting)
                    waiting = now
                finish(*waiting)

                for k, step in enumerate(steps):
                    after(t, k, *step)

        hidden()

    def mlp_sums(j, *steps):
        b = bm[j]

        def wcat(r0):
            return jnp.concatenate([weight(b, t, r0, 96, slice(0, 256)) for t in range(4)], 1)

        @phase
        def sums():
            @pl.loop(0, length // 256)
            def _(i):
                s = rows_of(i, 256)
                one = dot(cat(act, s), wcat(96), NT)
                two = dot(cat(gu, s), wcat(0), NT)
                if j == 0:
                    acc[s, :] = one
                    gn[s, :] = two
                else:
                    acc[s, :] += one
                    gn[s, :] += two
                for k, step in enumerate(steps):
                    after(i, k, *step)

        sums()

    def mlp_weight_grads(j):
        b = grads[j]

        @phase
        def weight_grads():
            for t in range(4):
                gup = dot(n2[...], gu[t], TN).astype(BF)
                b[t // 2, t % 2, :, :, 0:96, :] = gup.reshape(4, 2, 96, 256)
                gdown = dot(cot[...], act[t], TN).astype(BF)
                b[t // 2, t % 2, :, :, 96:192, :] = gdown.reshape(4, 2, 96, 256)

        weight_grads()

    def store_low():
        return [
            pltpu.make_async_copy(gu.at[k], lo_out.at[:, pl.ds(256 * k, 256)], local_sem.at[k])
            for k in range(width // 256)
        ]

    @phase
    def second_norm_back():
        @pl.loop(0, length // 256)
        def _(i):
            s = rows_of(i, 256)
            v = mid[s, :]
            mlp = acc[s, :]
            out = v + mlp
            weight_rows = val[s, :]
            ar[0, 4:5, :] += jnp.sum(weight_rows * (out * out), 0, keepdims=True)
            ar[0, 6:7, :] += jnp.sum(weight_rows * (mlp * mlp), 0, keepdims=True)
            low_out = out.astype(BF)
            for k in range(width // 256):
                gu[k, s, :] = low_out[:, 256 * k : 256 * k + 256]
            back, g_gain, g_bias = norm_back(v, gn[s, :], par[66:67, :])
            ar[0, 2:3, :] += g_gain
            ar[0, 3:4, :] += g_bias
            grad = cot[s, :].astype(F32) + back
            mid[s, :] = grad
            n2[s, :] = grad.astype(BF)

        for one in store_low():
            one.start()

    @phase
    def out_projection_back():
        @pl.loop(0, 4)
        def _(t):
            w = weight(bo, t, 0, 96, slice(0, 256))
            act[t] = dot(n2[...], w).astype(BF)
            grad = dot(n2[...], cc[t], TN)
            bm2[t // 2, t % 2, :, :, 0:96, 0:128] = grad[:, 0:128].astype(BF).reshape(4, 2, 96, 128)
            bm2[t // 2, t % 2, :, :, 96:144, 0:128] = fold(grad[:, 128:192])

    @phase
    def pair_attention_back():
        @pl.loop(0, 4)
        def _(t):
            attend_back(tt, ll, kx, k2, kt, cc, act, (dk, dv), (0, 1), t, length)
            after(t, 0, o_sum.s2, m_sum[2].s3, early_take_0)
            after(t, 1, o_sum.s3)
            after(t, 2, m_sum[1].s5, m_sum[1].give_credit, early_take_1)
            after(t, 3, m_sum[2].s4)

    def early_take_0():
        early.take(0)
        early.run(1)

    def early_take_1():
        early.take(1)
        early.left()

    @phase
    def pair_weight_grads():
        @pl.loop(0, 2)
        def _(x):
            both = jnp.concatenate([tt[2 * x, :, 0:384], tt[2 * x + 1, :, 0:384]], 1)
            grads = dot(n1[...], both, TN).astype(BF)
            for c in range(2):
                grad = grads[:, 384 * c : 384 * c + 384]
                gb[x, c, :, :, 0:96, :] = grad[:, 0:256].reshape(4, 2, 96, 256)
                third = grad[:, 256:384].reshape(4, 2, 96, 128)
                gb[x, c, :, :, 96:144, 0:128] = third[:, :, 0:48]
                gb[x, c, :, :, 96:144, 128:256] = third[:, :, 48:96]

    @phase
    def odd_weight_grads():
        @pl.loop(0, 4)
        def _(t):
            grad = dot(n1[...], tt[t, :, 384:640], TN)
            bm2[t // 2, t % 2, :, :, 0:96, 128:256] = grad[:, 0:128].astype(BF).reshape(4, 2, 96, 128)
            bm2[t // 2, t % 2, :, :, 96:144, 128:256] = fold(grad[:, 128:192])

    @phase
    def odd_attention_back():
        @pl.loop(0, 4)
        def _(t):
            attend_back(tt, ll, kx, k2, kt, cc, act, (dk, dv), (2,), t, length)
            after(t, 0, qa_sum.s2)
            after(t, 2, qa_sum.s3)
            after(t, 3, m_sum[2].s5)

    def store_grad():
        return pltpu.make_async_copy(acc, gt_out, local_sem.at[4])

    @phase
    def first_norm_back():
        @pl.loop(0, length // 256)
        def _(i):
            s = rows_of(i, 256)
            w = jnp.concatenate([weight(bq, t, 0, 96, slice(0, 640)) for t in range(4)], 1)
            grad = dot(cat(tt, s), w, NT)
            back, g_gain, g_bias = norm_back(tok[s, :].astype(F32), grad, par[64:65, :])
            g1[0:1, :] += g_gain
            g1[1:2, :] += g_bias
            acc[s, :] = mid[s, :] + back
            after(i, 0, qa_sum.s4, qb_sum.s2, qc_sum.s2)
            after(i, 2, qb_sum.s3, qc_sum.s3)

        store_grad().start()
        for k in range(width // 128):
            for n in range(2):
                br[0, 6 * n + k : 6 * n + k + 1, :] = g1[n : n + 1, 128 * k : 128 * k + 128]

    @phase
    def small_results():
        rows = [jnp.concatenate([br[2, 6 * n + k : 6 * n + k + 1, :] for k in range(6)], 1) for n in range(2)]
        sums = jnp.concatenate(rows + [ar[2, 2:8, :]], 0)
        if inner > 1:
            small_out[...] = sums
            return
        share = width // 32
        owner = lax.axis_index("fsdp") * 4 + lax.axis_index("tp")
        moved = pltpu.roll(sums, width - owner * share, 1)
        square = jnp.sum(sums[4:7], axis=1, keepdims=True) / (sums[7:8, 0:1] * width)
        rms = jnp.sqrt(jnp.broadcast_to(square, (3, 128)))
        lane = lanes()
        row = jnp.where(lane == 0, rms[0:1], jnp.where(lane == 1, rms[1:2], rms[2:3]))
        small_out[0:4, :] = moved[0:4, 0:128]
        small_out[4:8, :] = jnp.broadcast_to(row, (4, 128))

    def give(k):
        held = (gq_out, go_out, gup_out, gdown_out, small_out)[k]
        return pltpu.make_async_copy(held, big_outs[k], give_sem.at[k])

    entry()
    q_in[0].s1()
    document_marks()
    for one in own_copies():
        one.wait()
    q_in[1].s1()
    first_norm_statistics()
    q_in[0].s2()
    q_in[2].s1()
    q_in[1].s2()
    q_in[0].s3()
    q_in[2].s2()
    o_in.s1()
    q_in[1].s3()
    m_in[0].s1()
    q_in[2].s3()
    first_norm()
    o_in.s2()
    m_in[1].s1()
    attention()
    out_projection()
    m_in[0].s5()
    m_in[1].s5()

    mlp_hidden(0, (m_in[2].s3,), (), (m_in[3].s3,))
    m_in[4].s2()
    mlp_weight_grads(0)
    m_sum[0].s1()
    m_in[2].s4()
    m_in[5].s2()
    mlp_sums(0, (), (m_in[3].s4,), (m_sum[0].s2,))
    m_in[4].s3()
    m_in[2].s5()
    m_in[3].s5()

    mlp_hidden(1, (), (m_in[5].s3,), (m_sum[0].s3,))
    m_in[0].s6()
    m_in[1].s6()
    m_in[4].s4()
    mlp_weight_grads(1)
    m_sum[1].s1()
    m_in[5].s4()
    mlp_sums(1, (), (), (m_sum[1].s2,))
    m_sum[0].s4()
    m_in[4].s5()
    m_in[5].s5()

    mlp_hidden(2)
    m_sum[1].s3()
    m_in[2].s6()
    m_in[3].s6()
    mlp_weight_grads(2)
    m_sum[2].s1()
    mlp_sums(2, (), (), (m_sum[2].s2, m_sum[0].s5, m_sum[0].give_credit))
    m_in[4].s6()
    m_in[5].s6()

    second_norm_back()
    m_sum[1].s4()
    early.run(0)
    o_in.s6()
    out_projection_back()
    m_sum[0].take_credit()
    o_sum.s1()
    pair_attention_back()
    pair_weight_grads()
    m_sum[1].take_credit()
    qa_sum.s1()
    o_sum.s4()
    odd_attention_back()
    odd_weight_grads()
    qb_sum.s1()
    qc_sum.s1()
    for g in q_in:
        g.s6()
    give(2).start()
    give(3).start()
    first_norm_back()
    late.run(0)
    o_sum.s5()
    give(1).start()
    qb_sum.s4()
    qc_sum.s4()
    late.take(0)
    late.run(1)
    qa_sum.s5()
    late.take(1)
    late.left()
    small_results()
    give(4).start()
    qb_sum.s5()
    for one in store_low():
        one.wait()
    store_grad().wait()
    qc_sum.s5()
    give(0).start()
    for k in range(5):
        give(k).wait()


def scatter_slots(rows, columns):
    return [
        pltpu.VMEM((2, 4, 2, rows, columns), BF),
        pltpu.VMEM((4, (rows // 2 + 15) // 16 * 16, columns), BF),
        pltpu.VMEM((4, rows // 2, columns), BF),
        pltpu.VMEM((4, rows, columns), BF),
        pltpu.VMEM((4, rows, columns), BF),
        pltpu.VMEM((3, rows, columns), BF),
    ]


def layer(inner, tokens, cotangent, segments, valid, wq, wo, up, down, params):
    length, width = tokens.shape
    block = lambda rows, columns: pltpu.VMEM((2, 2, 4, 2, rows, columns), BF)
    small = (8, width) if inner > 1 else (8, 128)
    shapes = [(3, 96, 3 * HD), (3 * HD, 96), (96, width), (96, width), small]
    scratch = [pltpu.VMEM(shape, F32) for shape in shapes]
    scratch += [
        block(96, 640), block(96, 256), block(192, 256), block(192, 256), block(192, 256), block(192, 256),
        pltpu.VMEM((length, width), BF),
        pltpu.VMEM((length, width), BF),
        pltpu.VMEM((length, width), BF),
        pltpu.VMEM((4, length, 640), BF),
        pltpu.VMEM((4, length, 256), BF),
        pltpu.VMEM((4, length, 128), BF),
        pltpu.VMEM((length, 128), BF),
        pltpu.VMEM((length, 128), BF),
        pltpu.VMEM((128, length), BF),
        pltpu.VMEM((length, width), F32),
        pltpu.VMEM((length, width), BF),
        pltpu.VMEM((length, width), F32),
        pltpu.VMEM((length, width), F32),
        pltpu.VMEM((4, length, 256), BF),
        pltpu.VMEM((4, length, 256), BF),
        pltpu.VMEM((length, 1), F32),
        pltpu.VMEM((128, width), F32),
    ]
    scratch += [pltpu.VMEM((length, 128), F32)] * 2
    scratch += [scatter_slots(192, 256) * 3]
    scratch += [
        pltpu.VMEM((3, 8, width), F32),
        pltpu.VMEM((10, 8, width), F32),
        pltpu.VMEM((3, 16, 128), F32),
        pltpu.VMEM((10, 16, 128), F32),
        pltpu.VMEM((8, width), F32),
        pltpu.SemaphoreType.DMA((10, 11)),
        pltpu.SemaphoreType.DMA((10, 11)),
        pltpu.SemaphoreType.DMA((7, 8)),
        pltpu.SemaphoreType.DMA((7, 8)),
        pltpu.SemaphoreType.REGULAR((2, 6)),
        pltpu.SemaphoreType.DMA((2, 10)),
        pltpu.SemaphoreType.DMA((2, 10)),
        pltpu.SemaphoreType.DMA((5,)),
        pltpu.SemaphoreType.DMA((8,)),
        pltpu.SemaphoreType.DMA((5,)),
    ]
    vmem, anywhere = pl.BlockSpec(memory_space=pltpu.VMEM), pl.BlockSpec(memory_space=pl.ANY)
    return pl.pallas_call(
        partial(kernel, inner, length),
        out_shape=[
            jax.ShapeDtypeStruct((length, width), BF),
            jax.ShapeDtypeStruct((length, width), F32),
        ]
        + [jax.ShapeDtypeStruct(shape, F32) for shape in shapes],
        in_specs=[anywhere, anywhere, vmem, vmem, vmem, vmem, anywhere, anywhere, vmem],
        out_specs=[anywhere] * (2 + len(shapes)),
        scratch_shapes=scratch,
        compiler_params=pltpu.CompilerParams(
            collective_id=0, has_side_effects=True, vmem_limit_bytes=63 * 2**20
        ),
    )(tokens, cotangent, segments, valid, wq, wo, up, down, params)


def hand_over(arrays, share):
    count = len(arrays)
    pieces = []
    for k, a in enumerate(arrays):
        step = 256 if a.ndim == 2 and a.shape[0] % 256 == 0 else a.shape[0]
        pieces += [(k, start, step) for start in range(0, a.shape[0], step)]
    small = [(share,)] * 4 + [(3,)] if share else []
    shapes = [(a.shape, a.dtype) for a in arrays[: count - 1 if small else count]] + [(cut, F32) for cut in small]
    whole = len(shapes) - len(small)

    def body(*refs):
        came, went = refs[:count], refs[count : count + len(shapes)]
        held = refs[count + len(shapes) : 2 * count + len(shapes)]
        cuts, sems = refs[2 * count + len(shapes) : -1], refs[-1]

        def part(ref, n):
            _, start, step = pieces[n]
            return ref.at[pl.ds(start, step)] if step < ref.shape[0] else ref

        def fetch(n):
            k = pieces[n][0]
            return pltpu.make_async_copy(part(came[k], n), part(held[k], n), sems.at[0, n])

        def put(n):
            k = pieces[n][0]
            return pltpu.make_async_copy(part(held[k], n), part(went[k], n), sems.at[1, n])

        def put_cut(k):
            return pltpu.make_async_copy(cuts[k], went[whole + k], sems.at[1, len(pieces) + k])

        for n in reversed(range(len(pieces))):
            fetch(n).start()
        for n in reversed(range(len(pieces))):
            fetch(n).wait()
            if pieces[n][0] < whole:
                put(n).start()
                continue
            for k, cut in enumerate(small):
                cuts[k][...] = held[whole][k, 0 : cut[0]]
                put_cut(k).start()
        for n in range(len(pieces)):
            if pieces[n][0] < whole:
                put(n).wait()
        for k in range(len(small)):
            put_cut(k).wait()

    anywhere = pl.BlockSpec(memory_space=pltpu.HBM)
    return pl.pallas_call(
        body,
        out_shape=[jax.ShapeDtypeStruct(shape, dtype) for shape, dtype in shapes],
        in_specs=[anywhere] * count,
        out_specs=[anywhere] * len(shapes),
        scratch_shapes=[pltpu.VMEM(a.shape, a.dtype) for a in arrays]
        + [pltpu.VMEM(cut, F32) for cut in small]
        + [pltpu.SemaphoreType.DMA((2, len(pieces) + 5))],
        compiler_params=pltpu.CompilerParams(vmem_limit_bytes=63 * 2**20),
    )(*arrays)


def local(
    tokens, segment_ids, valid, ln1_gain, ln1_bias, w_qkv, w_out, ln2_gain, ln2_bias, w_up, w_down, cotangent
):
    length, width = tokens.shape
    holders = lax.axis_size("fsdp")
    inner = holders // 8
    groups = [[g * inner + i for i in range(inner)] for g in range(8)]

    def widen(block, axis=0):
        if inner == 1:
            return block
        return lax.all_gather(block, "fsdp", axis_index_groups=groups, axis=axis, tiled=True)

    def narrow(block, axis=0):
        if inner == 1:
            return block
        return lax.psum_scatter(
            block, "fsdp", scatter_dimension=axis, axis_index_groups=groups, tiled=True
        )

    params = widen(jnp.stack([ln1_gain, ln1_bias, ln2_gain, ln2_bias]), 1).astype(F32)
    results = layer(
        inner, tokens, cotangent, segment_ids, valid.reshape(1, length),
        widen(w_qkv.transpose(1, 0, 2), 1), widen(w_out, 1), widen(w_up), widen(w_down.T), params,
    )
    low, grad_tokens, gq, go, gup, gdown, *small = hand_over(results, width // 32 if inner == 1 else 0)
    if inner > 1:
        sums = lax.psum(small[0], "fsdp", axis_index_groups=groups)
        share = width // (holders * lax.axis_size("tp"))
        owner = lax.axis_index("fsdp") * lax.axis_size("tp") + lax.axis_index("tp")
        mine = lax.dynamic_slice_in_dim(sums[0:4], owner * share, share, 1)
        spread = jnp.sqrt(jnp.sum(sums[4:7], axis=1) / (sums[7, 0] * width))
        small = (mine[0], mine[1], mine[2], mine[3], spread)
    return (
        low, grad_tokens, small[0], small[1], narrow(gq, 1).transpose(1, 0, 2), narrow(go, 1),
        small[2], small[3], narrow(gup), narrow(gdown).T, small[4],
    )


def solution(mesh):
    both = ("fsdp", "tp")
    return jax.shard_map(
        local,
        mesh=mesh,
        in_specs=(
            P(both, None), P("fsdp", None), P(both), P("fsdp"), P("fsdp"), P("fsdp", None, "tp"),
            P("tp", "fsdp"), P("fsdp"), P("fsdp"), P("fsdp", "tp"), P("tp", "fsdp"), P(both, None),
        ),
        out_specs=(
            P(both, None), P(both, None), P(both), P(both), P("fsdp", None, "tp"), P("tp", "fsdp"),
            P(both), P(both), P("fsdp", "tp"), P("tp", "fsdp"), P(),
        ),
        check_vma=False,
    )
```

```python
from functools import partial

import jax
import jax.numpy as jnp
from jax import lax
from jax.experimental import pallas as pl
from jax.experimental.pallas import tpu as pltpu
from jax.sharding import PartitionSpec as P

HD = 64
BQ = 256
EPS = 1e-05
BIG = -1e30
F32 = jnp.float32
BF = jnp.bfloat16
NN = (((1,), (0,)), ((), ()))
NT = (((1,), (1,)), ((), ()))
TN = (((0,), (0,)), ((), ()))
MESH = pl.DeviceIdType.MESH
C0 = 0.7978845608
C1 = 0.7978845608 * 0.044715


def dot(a, b, dims=NN):
    return lax.dot_general(a, b, dims, preferred_element_type=F32)


def phase(body):
    return body


def remote(src, dst, send, recv, device):
    return pltpu.make_async_remote_copy(
        src_ref=src, dst_ref=dst, send_sem=send, recv_sem=recv,
        device_id=device, device_id_type=MESH,
    )


class Place:
    def __init__(self, inner):
        f = lax.axis_index("fsdp")
        t = lax.axis_index("tp")
        g = f // inner
        self.low = f % inner
        self.inner = inner
        self.z, self.y, self.x, self.c = g // 2, g % 2, t // 2, t % 2

    def device(self, z, y, x, c):
        return ((z * 2 + y) * self.inner + self.low, x * 2 + c)

    def core(self):
        return self.device(self.z, self.y, self.x, 1 - self.c)

    def xn(self):
        return self.device(self.z, self.y, 1 - self.x, self.c)

    def yn(self):
        return self.device(self.z, 1 - self.y, self.x, self.c)

    def cube(self, n):
        y, x, c = (self.y + n // 4) % 2, (self.x + n // 2) % 2, (self.c + n) % 2
        return self.device(self.z, y, x, c)

    def zn(self, d):
        return self.device((self.z + d) % 4, self.y, self.x, self.c)

    def zp(self, d):
        return self.device((self.z - d + 4) % 4, self.y, self.x, self.c)


def greet(inner):
    p = Place(inner)
    sem = pltpu.get_barrier_semaphore()
    for dev in [p.cube(n) for n in range(1, 8)] + [p.zn(d) for d in range(1, 4)]:
        pl.semaphore_signal(sem, inc=1, device_id=dev, device_id_type=MESH)


def met(inner):
    pl.semaphore_wait(pltpu.get_barrier_semaphore(), 10)


class Gather:
    def __init__(self, name, inner, buf, row0, rows, send, recv):
        self.name = name
        self.inner, self.buf, self.row0, self.rows = inner, buf, row0, rows
        self.send, self.recv = send, recv

    def own(self, x, c, z, y):
        return self.buf.at[x, c, z, y, pl.ds(self.row0, self.rows)]

    def group(self, x, c, y, half=None):
        start, size = self.row0, self.rows
        if half is not None:
            size = self.rows // 2
            start = self.row0 + half * size
        return self.buf.at[x, c, :, y, pl.ds(start, size)]

    def parts(self, slot):
        p = Place(self.inner)
        x, c, z, y = p.x, p.c, p.z, p.y
        if slot < 3:
            d = slot + 1
            return self.own(x, c, z, y), self.own(x, c, (z - d + 4) % 4, y), p.zn(d)
        if slot == 3:
            return self.group(x, c, y), self.group(1 - x, c, y), p.xn()
        if slot == 4:
            return self.group(x, c, y), self.group(x, c, 1 - y), p.yn()
        if slot == 5:
            return self.group(1 - x, c, y, 0), self.group(1 - x, c, 1 - y, 0), p.yn()
        if slot == 6:
            return self.group(x, c, 1 - y, 1), self.group(1 - x, c, 1 - y, 1), p.xn()
        xx = x if slot in (7, 9) else 1 - x
        yy = y if slot in (7, 8) else 1 - y
        return self.group(xx, c, yy), self.group(xx, 1 - c, yy), p.core()

    SENT = (0, 0, 0, 1, 1, 2, 2, 1, 2, 2, 2)
    CAME = (0, 0, 0, 1, 2, 3, 3, 4, 5, 4, 5)

    def start(self, *slots):
        for slot in slots:
            mine, _, dev = self.parts(slot)
            remote(mine, mine, self.send.at[self.SENT[slot]], self.recv.at[self.CAME[slot]], dev).start()

    def bytes_of(self, blocks):
        rows = pl.ds(self.row0, self.rows)
        if blocks == 3:
            return self.buf.at[0, 0, 0:3, 0, rows]
        if blocks == 4:
            return self.buf.at[0, 0, :, 0, rows]
        if blocks == 8:
            return self.buf.at[0, 0, :, :, rows]
        if blocks == 12:
            return self.buf.at[:, :, 0:3, 0, rows]
        return self.buf.at[0, :, :, :, rows]

    def arrive(self, group):
        ref = self.bytes_of((3, 4, 4, 4, 8, 8)[group])
        dev = Place(self.inner).core()
        remote(ref, ref, self.send.at[0], self.recv.at[group], dev).wait_recv()

    def left(self):
        for group, blocks in enumerate((3, 12, 16)):
            ref = self.bytes_of(blocks)
            dev = Place(self.inner).core()
            remote(ref, ref, self.send.at[group], self.recv.at[0], dev).wait_send()

    def s1(self):
        self.start(0, 1, 2)

    def s2(self):
        self.arrive(0)
        self.start(3, 4, 7)

    def s3(self):
        self.arrive(2)
        self.start(6, 9)
        self.arrive(1)
        self.start(5, 8)

    def s4(self):
        self.arrive(3)
        self.start(10)

    def near(self):
        self.arrive(4)

    def far(self):
        self.arrive(5)

    def s5(self):
        self.near()
        self.far()

    def s6(self):
        self.left()


class Scatter:
    def __init__(self, name, inner, buf, block, slots, place, send, recv, credit, out):
        self.name = name
        self.inner, self.buf, self.slots = inner, buf, slots
        self.row0, self.rows, self.col0, columns = block
        self.half = (self.rows // 2 + 15) // 16 * 16
        row, upper, lower, col = place
        self.land = (
            slice(row, row + self.rows), slice(upper, upper + self.half),
            slice(lower, lower + self.rows - self.half), slice(col, col + columns),
        )
        self.cols = slice(self.col0, self.col0 + columns)
        self.send, self.recv = send, recv
        self.credit, self.out = credit, out

    def parts(self, slot):
        p = Place(self.inner)
        x, c, z, y = p.x, p.c, p.z, p.y
        buf, cols = self.buf, self.cols
        r1, ra, rb, rx, ry, rz = self.slots
        rows, upper, lower = self.spans()
        land, land_a, land_b, land_cols = self.land
        if slot == 0:
            return buf.at[:, 1 - c, :, :, rows, cols], r1.at[:, :, :, land, land_cols], p.core()
        if slot == 1:
            return buf.at[1 - x, c, :, 1 - y, upper, cols], ra.at[:, land_a, land_cols], p.yn()
        if slot == 2:
            return buf.at[1 - x, c, :, 1 - y, lower, cols], rb.at[:, land_b, land_cols], p.xn()
        if slot == 3:
            return buf.at[1 - x, c, :, y, rows, cols], rx.at[:, land, land_cols], p.xn()
        if slot == 4:
            return buf.at[x, c, :, 1 - y, rows, cols], ry.at[:, land, land_cols], p.yn()
        d = slot - 4
        return buf.at[x, c, (z + d) % 4, y, rows, cols], rz.at[d - 1, land, land_cols], p.zn(d)

    def spans(self):
        start, end = self.row0, self.row0 + self.rows
        return slice(start, end), slice(start, start + self.half), slice(start + self.half, end)

    SENT = (0, 1, 1, 1, 1, 2, 2, 2)
    CAME = (0, 1, 2, 3, 3, 4, 4, 4)

    def start(self, *slots):
        for slot in slots:
            src, dst, dev = self.parts(slot)
            remote(src, dst, self.send.at[self.SENT[slot]], self.recv.at[self.CAME[slot]], dev).start()

    def arrive(self, group):
        land, _, _, cols = self.land
        if group < 3:
            ref = self.parts(group)[1]
        elif group == 3:
            ref = self.slots[0].at[0, :, :, land, cols]
        else:
            ref = self.slots[5].at[:, land, cols]
        remote(ref, ref, self.send.at[0], self.recv.at[group], Place(self.inner).core()).wait_recv()

    def left(self):
        rows, cols = self.spans()[0], self.cols
        refs = (
            self.buf.at[:, 0, :, :, rows, cols], self.buf.at[:, :, 0:3, 0, rows, cols],
            self.buf.at[0, 0, 0:3, 0, rows, cols],
        )
        for group, ref in enumerate(refs):
            dev = Place(self.inner).core()
            remote(ref, ref, self.send.at[group], self.recv.at[0], dev).wait_send()

    def take_credit(self):
        for i in range(6):
            pl.semaphore_wait(self.credit.at[i], 1)

    def give_credit(self):
        p = Place(self.inner)
        for i, dev in enumerate((p.core(), p.xn(), p.yn(), p.zp(1), p.zp(2), p.zp(3))):
            pl.semaphore_signal(self.credit.at[i], inc=1, device_id=dev, device_id_type=MESH)

    def s1(self):
        self.start(0)

    def add(self, x, y, rows, *others):
        c = Place(self.inner).c

        @pl.loop(0, 4)
        def _(z):
            total = self.buf[x, c, z, y, rows, self.cols].astype(F32)
            for other in others:
                total = total + other(z).astype(F32)
            self.buf[x, c, z, y, rows, self.cols] = total.astype(BF)

    def s2(self):
        p = Place(self.inner)
        r1, (land, _, _, cols) = self.slots[0], self.land
        self.arrive(0)
        for x, y in ((1 - p.x, 1 - p.y), (1 - p.x, p.y), (p.x, 1 - p.y), (p.x, p.y)):
            self.add(x, y, self.spans()[0], lambda z: r1[x, z, y, land, cols])
            if x is not p.x and y is not p.y:
                self.start(1, 2)

    def s3(self):
        p = Place(self.inner)
        _, upper, lower = self.spans()
        _, land_a, land_b, cols = self.land
        ra, rb = self.slots[1:3]
        self.arrive(1)
        self.add(1 - p.x, p.y, upper, lambda z: ra[z, land_a, cols])
        self.start(3)
        self.arrive(2)
        self.add(p.x, 1 - p.y, lower, lambda z: rb[z, land_b, cols])
        self.start(4)

    def s4(self):
        p = Place(self.inner)
        land, _, _, cols = self.land
        rx, ry = self.slots[3:5]
        self.arrive(3)
        self.add(p.x, p.y, self.spans()[0], lambda z: rx[z, land, cols], lambda z: ry[z, land, cols])
        self.start(5, 6, 7)

    def s5(self):
        p = Place(self.inner)
        land, _, _, cols = self.land
        rz = self.slots[5]
        self.arrive(4)
        total = self.buf[p.x, p.c, p.z, p.y, self.spans()[0], self.cols].astype(F32)
        for d in range(3):
            total = total + rz[d, land, cols].astype(F32)
        self.out(total)
        self.left()


class Total:
    def __init__(self, name, inner, ref, got, send, recv):
        self.name = name
        self.inner, self.ref, self.got, self.send, self.recv = inner, ref, got, send, recv

    def copy(self, slot):
        p = Place(self.inner)
        dev = p.cube(slot + 1) if slot < 7 else p.zn(slot - 6)
        stage = 0 if slot < 7 else 1
        return remote(self.ref.at[stage], self.got.at[slot], self.send.at[stage], self.recv.at[stage], dev)

    def slots(self, stage):
        return range(7) if stage == 0 else range(7, 10)

    def all_of(self, stage):
        span = self.slots(stage)
        ref = self.got.at[span.start : span.stop]
        return remote(ref, ref, self.send.at[stage], self.recv.at[stage], Place(self.inner).core())

    def run(self, stage):
        for slot in self.slots(stage):
            self.copy(slot).start()

    def take(self, stage):
        self.all_of(stage).wait_recv()
        total = self.ref[stage]
        for slot in self.slots(stage):
            total = total + self.got[slot]
        self.ref[stage + 1] = total

    def left(self):
        for stage in range(2):
            self.all_of(stage).wait_send()


def head_parts(t_ref, k2_ref, t, h, qs, kr):
    if h < 2:
        return t_ref[t, qs, 0:128], t_ref[t, kr, 128:256], t_ref[t, kr, 256:384]
    return t_ref[t, qs, 384:512], k2_ref[kr, :], t_ref[t, kr, 512:640]


def lanes():
    return lax.broadcasted_iota(jnp.int32, (1, 128), 1)


def roll_key(t_ref, k2_ref, t):
    k2_ref[...] = pltpu.roll(t_ref[t, :, 384:512].astype(F32), 64, 1).astype(BF)


def below(transposed):
    r = lax.broadcasted_iota(jnp.int32, (BQ, BQ), 0)
    c = lax.broadcasted_iota(jnp.int32, (BQ, BQ), 1)
    return r <= c if transposed else r >= c


def attend(t_ref, l_ref, kx_ref, k2_ref, c_ref, t, length):
    lane = lanes()
    low = lane < 64
    roll_key(t_ref, k2_ref, t)
    for i in range(length // BQ):
        first = max(0, i * BQ - length // 2)
        width = (i + 1) * BQ - first
        qs, kr = slice(i * BQ, (i + 1) * BQ), slice(first, first + width)
        kx = kx_ref[kr, :]
        doc = kx_ref[qs, :].astype(F32)
        qx = jnp.where(lane < 8, BIG * (1.0 - doc), 0.0).astype(BF)
        marks = qx
        outs = []
        for h in range(3):
            q, k, v = head_parts(t_ref, k2_ref, t, h, qs, kr)
            keep = jnp.logical_not(low) if h == 1 else low
            q = jnp.where(keep, q * BF(HD ** -0.5), BF(0))
            s = dot(jnp.concatenate([q, qx], 1), jnp.concatenate([k, kx], 1), NT)
            edge = jnp.where(below(False), s[:, width - BQ :], BIG)
            s = edge if width == BQ else jnp.concatenate([s[:, : width - BQ], edge], 1)
            top = jnp.max(s, axis=1, keepdims=True)
            p = jnp.exp(s - top).astype(BF)
            both = dot(p, jnp.concatenate([v, jnp.ones((width, 128), BF)], 1))
            total = both[:, 128:256]
            outs.append(both[:, :128] / total)
            rest = -(top + jnp.log(total))
            for n in range(3):
                piece = rest.astype(BF)
                marks = jnp.where(lane == 8 + 16 * h + n, piece, marks)
                rest = rest - piece.astype(F32)
        l_ref[t, qs, :] = marks
        c_ref[t, qs, 0:128] = jnp.where(low, outs[0], outs[1]).astype(BF)
        c_ref[t, qs, 128:256] = jnp.where(low, outs[2], 0.0).astype(BF)


def attend_back(t_ref, l_ref, kx_ref, k2_ref, kt_ref, c_ref, do_ref, sums, heads, t, length):
    lane = lanes()
    low = lane < 64
    dk_ref, dv_ref = sums
    odd = heads == (2,)
    if odd:
        roll_key(t_ref, k2_ref, t)
        kt_ref[...] = k2_ref[...].T
    else:
        kt_ref[...] = t_ref[t, :, 128:256].T
    for ref in sums:
        ref[...] = jnp.zeros_like(ref)
    for i in range(length // BQ):
        first = max(0, i * BQ - length // 2)
        width = (i + 1) * BQ - first
        qs, kr = slice(i * BQ, (i + 1) * BQ), slice(first, first + width)
        marks = l_ref[t, qs, :]
        side = slice(128, 256) if odd else slice(0, 128)
        qs_all, dos, left, right = [], [], [], []
        for h in heads:
            q, k, v = head_parts(t_ref, k2_ref, t, h, qs, kr)
            keep = jnp.logical_not(low) if h == 1 else low
            q = jnp.where(keep, q * BF(HD ** -0.5), BF(0))
            do = jnp.where(keep, do_ref[t, qs, side], BF(0))
            dd = (do.astype(F32) * c_ref[t, qs, side].astype(F32)).astype(BF)
            mine = (lane < 8) | ((lane >= 8 + 16 * h) & (lane < 24 + 16 * h))
            qs_all.append(q)
            dos.append(do)
            left.append(jnp.concatenate([q, jnp.where(mine, marks, BF(0))], 1))
            right.append(jnp.concatenate([do, dd], 1))
        s_all = dot(jnp.concatenate([k, kx_ref[kr, :]], 1), jnp.concatenate(left, 0), NT)
        minus = jnp.full((width, 128), -1.0, BF)
        dp_all = dot(jnp.concatenate([v, minus], 1), jnp.concatenate(right, 0), NT)
        ps, dss, grads = [], [], []
        for n in range(len(heads)):
            s = s_all[:, n * BQ : (n + 1) * BQ]
            edge = jnp.where(below(True), s[width - BQ :], BIG)
            s = edge if width == BQ else jnp.concatenate([s[: width - BQ], edge], 0)
            p = jnp.exp(s)
            ds = (p * dp_all[:, n * BQ : (n + 1) * BQ]).astype(BF)
            ps.append(p.astype(BF))
            dss.append(ds)
            grads.append(dot(kt_ref[64 * n : 64 * n + 64, kr], ds))
        if odd:
            grads.append(jnp.zeros((64, BQ), F32))
        grad = (jnp.concatenate(grads, 0).T * HD ** -0.5).astype(BF)
        dv_ref[kr, :] += dot(jnp.concatenate(ps, 1), jnp.concatenate(dos, 0))
        dk_ref[kr, :] += dot(jnp.concatenate(dss, 1), jnp.concatenate(qs_all, 0))
        if odd:
            t_ref[t, qs, 384:512] = jnp.where(low, grad, t_ref[t, qs, 384:512])
        else:
            t_ref[t, qs, 0:128] = grad
    if odd:
        moved = pltpu.roll(dk_ref[...], 64, 1).astype(BF)
        t_ref[t, :, 384:512] = jnp.where(low, t_ref[t, :, 384:512], moved)
        t_ref[t, :, 512:640] = dv_ref[...].astype(BF)
    else:
        t_ref[t, :, 128:256] = dk_ref[...].astype(BF)
        t_ref[t, :, 256:384] = dv_ref[...].astype(BF)


def stats(v):
    mean = jnp.mean(v, axis=-1, keepdims=True)
    center = v - mean
    scale = lax.rsqrt(jnp.mean(center * center, axis=-1, keepdims=True) + EPS)
    return center * scale, scale


def norm_back(v, q, gain):
    n, scale = stats(v)
    e = q * gain
    back = scale * (e - jnp.mean(e, -1, keepdims=True) - n * jnp.mean(e * n, -1, keepdims=True))
    return back, jnp.sum(q * n, 0, keepdims=True), jnp.sum(q, 0, keepdims=True)


def kernel(
    inner, length,
    tok_in, cot_in, seg, valid, wq_in, wo_in, up_in, down_in, par_a, par_b, par_c, par_d,
    lo_out, gt_out, *rest,
):
    big_outs = rest[0:5]
    (
        gq_out, go_out, gup_out, gdown_out, small_out,
        bq, bo, bm0, bm1, bm2, gb,
        tok, cot, n1, tt, cc, ll, kx, k2, kt, mid, n2, acc, gn, act, gu, val, par,
        dk, dv,
        m_sets, o_set, ar, ar_got, br, br_got, g1,
        ag_send, ag_recv, rs_send, rs_recv, credit, ar_send, ar_recv, local_sem, own_sem, give_sem,
    ) = rest[5:]
    width = tok.shape[1]
    bm = (bm0, bm1, bm2)
    blocks = [(bq, 0, 32), (bq, 32, 32), (bq, 64, 32), (bo, 0, 96)]
    blocks += [(b, r0, 96) for b in bm for r0 in (0, 96)]
    gathers = [
        Gather(f"gather{k}", inner, b, r0, rows, ag_send.at[k], ag_recv.at[k])
        for k, (b, r0, rows) in enumerate(blocks)
    ]
    here = Place(inner)
    mine = (here.x, here.c, here.z, here.y)

    def put_mlp(j):
        def put(total):
            gup_out[:, 256 * j : 256 * j + 256] = total[0:96]
            gdown_out[:, 256 * j : 256 * j + 256] = total[96:192]

        return put

    def put_out(total):
        go_out[0 : 2 * HD] = total[0:96].T
        third = total[96:144].T
        go_out[2 * HD : 3 * HD] = jnp.concatenate([third[0:64], third[64:128]], 1)

    def put_pair(total):
        gq_out[0, :, 0:128] = total[0:96, 0:128]
        gq_out[1, :, 0:128] = total[0:96, 128:256]
        gq_out[2, 0:48, 0:128] = total[96:144, 0:128]
        gq_out[2, 48:96, 0:128] = total[96:144, 128:256]

    def put_odd(total):
        gq_out[0, 0:80, 128:192] = total[:, 0:64]
        gq_out[1, 0:80, 128:192] = total[:, 64:128]

    def put_rest(total):
        gq_out[0, 80:96, 128:192] = total[0:16, 0:64]
        gq_out[1, 80:96, 128:192] = total[0:16, 64:128]
        gq_out[2, 0:48, 128:192] = total[16:64, 0:64]
        gq_out[2, 48:96, 128:192] = total[16:64, 64:128]

    grads = (gb, bm0, bm1)
    sets = [m_sets[0:6], m_sets[6:12], m_sets[12:18]]
    start = (0, 0, 0, 0)
    plan = [
        (gb, (0, 192, 0, 256), sets[0], start, put_mlp(0)),
        (bm0, (0, 192, 0, 256), sets[1], start, put_mlp(1)),
        (bm1, (0, 192, 0, 256), sets[2], start, put_mlp(2)),
        (bm2, (0, 144, 0, 128), o_set, start, put_out),
        (gb, (0, 144, 0, 256), sets[0], start, put_pair),
        (bm2, (0, 80, 128, 128), o_set, (0, 0, 0, 128), put_odd),
        (bm2, (80, 64, 128, 128), o_set, (80, 48, 32, 128), put_rest),
    ]
    scatters = [
        Scatter(
            f"scatter{k}", inner, b, block, slots, place,
            rs_send.at[k], rs_recv.at[k], credit.at[0], out,
        )
        for k, (b, block, slots, place, out) in enumerate(plan)
    ]
    m_sum, o_sum, qa_sum, qb_sum, qc_sum = scatters[0:3], *scatters[3:7]
    q_in, o_in, m_in = gathers[0:3], gathers[3], gathers[4:10]
    early = Total("early", inner, ar, ar_got, ar_send.at[0], ar_recv.at[0])
    late = Total("late", inner, br, br_got, ar_send.at[1], ar_recv.at[1])

    def after(t, last, *steps):
        @pl.when(t == last)
        def _():
            for step in steps:
                step()

    def rows_of(i, size):
        return pl.ds(pl.multiple_of(i * size, size), size)

    def weight(buf, t, r0, rows, columns):
        return buf[t // 2, t % 2, :, :, r0 : r0 + rows, columns].reshape(8 * rows, -1)

    def fold(columns):
        parts = columns.reshape(8, 96, 64)
        halves = [parts[:, 48 * n : 48 * n + 48].reshape(8 * 48, 64) for n in range(2)]
        return jnp.concatenate(halves, 1).astype(BF).reshape(4, 2, 48, 128)

    def cat(ref, s):
        return jnp.concatenate([ref[t, s, :] for t in range(4)], 1)

    def own_copies():
        copies = []
        for j in range(3):
            cols = pl.ds(256 * j, 256)
            copies.append((up_in.at[:, cols], bm[j].at[(*mine, pl.ds(0, 96))]))
            copies.append((down_in.at[:, cols], bm[j].at[(*mine, pl.ds(96, 96))]))
        copies += [(tok_in, tok), (cot_in, cot)]
        return [pltpu.make_async_copy(src, dst, own_sem.at[k]) for k, (src, dst) in enumerate(copies)]

    @phase
    def entry():
        for one in own_copies():
            one.start()
        greet(inner)
        q, k, v = (wq_in[n] for n in range(3))
        for n, one in enumerate((q, k, v)):
            bq[(*mine, slice(None), slice(128 * n, 128 * n + 128))] = one[:, 0:128]
        odd = [one[:, 128:192].astype(F32) for one in (q, k, v)]
        bq[(*mine, slice(None), slice(384, 512))] = jnp.concatenate(odd[0:2], 1).astype(BF)
        params = jnp.concatenate([one[...].astype(F32) for one in (par_a, par_b, par_c, par_d)] + [jnp.zeros((124, 96), F32)], 0).T[:, 0:64]
        bq[(*mine, slice(None), slice(512, 640))] = jnp.concatenate([odd[2], params], 1).astype(BF)
        met(inner)

    @phase
    def document_marks():
        me_t = lax.axis_index("tp")
        row = seg[pl.ds(me_t, 1), :].astype(F32)
        lane_id = lax.broadcasted_iota(jnp.int32, (128, length), 0)
        marks = jnp.where(row == lane_id.astype(F32), 1.0, 0.0)
        marks = jnp.where(lane_id < 8, marks, 0.0)
        low4 = lane_id % 16
        ones = (lane_id >= 8) & (lane_id < 56) & (low4 >= 8) & (low4 < 11)
        marks = jnp.where(ones, 1.0, marks)
        marks = jnp.where(lane_id == 64, valid[...].astype(F32), marks)
        columns = marks.T
        val[...] = columns[:, 64:65]
        kx[...] = jnp.where(lanes() < 64, columns, 0.0).astype(BF)
        ar[0] = jnp.zeros_like(ar.at[0])
        br[0] = jnp.zeros_like(br.at[0])
        g1[...] = jnp.zeros_like(g1)
        count = jnp.sum(valid[...].astype(F32), axis=1, keepdims=True)
        ar[0, 7:8, 0:128] = jnp.broadcast_to(count, (1, 128))
        wide = jnp.concatenate([wo_in[...].astype(F32), jnp.zeros((64, 96), F32)], 0)
        bo[mine] = wide.T.astype(BF)

    @phase
    def first_norm_statistics():
        @pl.loop(0, length // 256)
        def _(i):
            s = rows_of(i, 256)
            mid[s, :] = stats(tok[s, :].astype(F32))[0]

    @phase
    def first_norm():
        par[...] = bq[here.x, here.c, :, :, :, 512:640].reshape(width, 128).astype(F32).T

        @pl.loop(0, length // 256)
        def _(i):
            s = rows_of(i, 256)
            n1[s, :] = (mid[s, :] * par[64:65, :] + par[65:66, :]).astype(BF)

    @phase
    def attention():
        @pl.loop(0, 4)
        def _(n):
            x, c = (here.x + n // 2) % 2, (here.c + n % 2) % 2
            t = 2 * x + c
            w = bq[x, c].reshape(width, 640)

            @pl.loop(0, length // 512)
            def _(i):
                s = rows_of(i, 512)
                tt[t, s, :] = dot(n1[s, :], w).astype(BF)

            after(n, 1, m_in[1].s2, m_in[2].s1)
            after(n, 3, m_in[1].s3, m_in[2].s2, m_in[5].s1)
            attend(tt, ll, kx, k2, cc, t, length)
            after(n, 0, *[g.s4 for g in q_in], *[g.near for g in q_in], m_in[0].s2)
            after(n, 1, o_in.s3, m_in[3].s1)
            after(n, 2, m_in[0].s3, *[g.far for g in q_in], m_in[4].s1)
            after(n, 3, o_in.s4, m_in[3].s2, m_in[0].s4, o_in.s5)

    @phase
    def out_projection():
        @pl.loop(0, length // 256)
        def _(i):
            s = rows_of(i, 256)
            branch = jnp.zeros((256, width), F32)
            for t in range(4):
                branch = branch + dot(cc[t, s, :], weight(bo, t, 0, 96, slice(0, 256)), NT)
            v = tok[s, :].astype(F32) + branch
            mid[s, :] = v
            ar[0, 5:6, :] += jnp.sum(val[s, :] * (branch * branch), 0, keepdims=True)
            n, _ = stats(v)
            n2[s, :] = (n * par[66:67, :] + par[67:68, :]).astype(BF)

    def mlp_hidden(j, *steps):
        b = bm[j]

        @phase
        def hidden():
            @pl.loop(0, 4)
            def _(t):
                up = weight(b, t, 0, 96, slice(0, 256))
                down = weight(b, t, 96, 96, slice(0, 256))

                def finish(s, v, ga):
                    v2 = v * v
                    th = jnp.tanh(v * (C0 + C1 * v2))
                    h = 0.5 + 0.5 * th
                    act[t, s, :] = (v * h).astype(BF)
                    slope = h + (0.5 * v) * (1.0 - th * th) * (C0 + (3.0 * C1) * v2)
                    gu[t, s, :] = (ga * slope).astype(BF)

                waiting = None
                for i in range(length // 128):
                    s = slice(128 * i, 128 * i + 128)
                    now = (s, dot(n2[s, :], up), dot(cot[s, :], down))
                    if waiting is not None:
                        finish(*waiting)
                    waiting = now
                finish(*waiting)

                for k, step in enumerate(steps):
                    after(t, k, *step)

        hidden()

    def mlp_sums(j, *steps):
        b = bm[j]

        def wcat(r0):
            return jnp.concatenate([weight(b, t, r0, 96, slice(0, 256)) for t in range(4)], 1)

        @phase
        def sums():
            @pl.loop(0, length // 256)
            def _(i):
                s = rows_of(i, 256)
                one = dot(cat(act, s), wcat(96), NT)
                two = dot(cat(gu, s), wcat(0), NT)
                if j == 0:
                    acc[s, :] = one
                    gn[s, :] = two
                else:
                    acc[s, :] += one
                    gn[s, :] += two
                for k, step in enumerate(steps):
                    after(i, k, *step)

        sums()

    def mlp_weight_grads(j):
        b = grads[j]

        @phase
        def weight_grads():
            for t in range(4):
                gup = dot(n2[...], gu[t], TN).astype(BF)
                b[t // 2, t % 2, :, :, 0:96, :] = gup.reshape(4, 2, 96, 256)
                gdown = dot(cot[...], act[t], TN).astype(BF)
                b[t // 2, t % 2, :, :, 96:192, :] = gdown.reshape(4, 2, 96, 256)

        weight_grads()

    def store_low():
        return [
            pltpu.make_async_copy(gu.at[k], lo_out.at[:, pl.ds(256 * k, 256)], local_sem.at[k])
            for k in range(width // 256)
        ]

    @phase
    def second_norm_back():
        @pl.loop(0, length // 256)
        def _(i):
            s = rows_of(i, 256)
            v = mid[s, :]
            mlp = acc[s, :]
            out = v + mlp
            weight_rows = val[s, :]
            ar[0, 4:5, :] += jnp.sum(weight_rows * (out * out), 0, keepdims=True)
            ar[0, 6:7, :] += jnp.sum(weight_rows * (mlp * mlp), 0, keepdims=True)
            low_out = out.astype(BF)
            for k in range(width // 256):
                gu[k, s, :] = low_out[:, 256 * k : 256 * k + 256]
            back, g_gain, g_bias = norm_back(v, gn[s, :], par[66:67, :])
            ar[0, 2:3, :] += g_gain
            ar[0, 3:4, :] += g_bias
            grad = cot[s, :].astype(F32) + back
            mid[s, :] = grad
            n2[s, :] = grad.astype(BF)

        for one in store_low():
            one.start()

    @phase
    def out_projection_back():
        @pl.loop(0, 4)
        def _(t):
            w = weight(bo, t, 0, 96, slice(0, 256))
            act[t] = dot(n2[...], w).astype(BF)
            grad = dot(n2[...], cc[t], TN)
            bm2[t // 2, t % 2, :, :, 0:96, 0:128] = grad[:, 0:128].astype(BF).reshape(4, 2, 96, 128)
            bm2[t // 2, t % 2, :, :, 96:144, 0:128] = fold(grad[:, 128:192])

    @phase
    def pair_attention_back():
        @pl.loop(0, 4)
        def _(t):
            attend_back(tt, ll, kx, k2, kt, cc, act, (dk, dv), (0, 1), t, length)
            after(t, 0, m_sum[2].s3, m_sum[1].s4)
            after(t, 1, o_sum.s2, early_take_0)
            after(t, 3, m_sum[2].s4)

    def early_take_0():
        early.take(0)
        early.run(1)

    def early_take_1():
        early.take(1)
        early.left()

    @phase
    def pair_weight_grads():
        @pl.loop(0, 2)
        def _(x):
            both = jnp.concatenate([tt[2 * x, :, 0:384], tt[2 * x + 1, :, 0:384]], 1)
            grads = dot(n1[...], both, TN).astype(BF)
            for c in range(2):
                grad = grads[:, 384 * c : 384 * c + 384]
                gb[x, c, :, :, 0:96, :] = grad[:, 0:256].reshape(4, 2, 96, 256)
                third = grad[:, 256:384].reshape(4, 2, 96, 128)
                gb[x, c, :, :, 96:144, 0:128] = third[:, :, 0:48]
                gb[x, c, :, :, 96:144, 128:256] = third[:, :, 48:96]

    @phase
    def odd_weight_grads():
        @pl.loop(0, 4)
        def _(t):
            grad = dot(n1[...], tt[t, :, 384:640], TN)
            bm2[t // 2, t % 2, :, :, 0:96, 128:256] = grad[:, 0:128].astype(BF).reshape(4, 2, 96, 128)
            bm2[t // 2, t % 2, :, :, 96:144, 128:256] = fold(grad[:, 128:192])

    @phase
    def odd_attention_back():
        @pl.loop(0, 4)
        def _(t):
            attend_back(tt, ll, kx, k2, kt, cc, act, (dk, dv), (2,), t, length)
            after(t, 0, qa_sum.s2, early_take_1)
            after(t, 1, m_sum[1].s5)
            after(t, 2, qa_sum.s3)
            after(t, 3, o_sum.s4)

    def store_grad():
        return pltpu.make_async_copy(acc, gt_out, local_sem.at[4])

    @phase
    def first_norm_back():
        @pl.loop(0, length // 256)
        def _(i):
            s = rows_of(i, 256)
            w = jnp.concatenate([weight(bq, t, 0, 96, slice(0, 640)) for t in range(4)], 1)
            grad = dot(cat(tt, s), w, NT)
            after(i, 2, qb_sum.s3, qc_sum.s3)
            back, g_gain, g_bias = norm_back(tok[s, :].astype(F32), grad, par[64:65, :])
            g1[0:1, :] += g_gain
            g1[1:2, :] += g_bias
            acc[s, :] = mid[s, :] + back
            after(i, 0, qb_sum.s2, qc_sum.s2)
            after(i, 1, qa_sum.s4)

        store_grad().start()
        for k in range(width // 128):
            for n in range(2):
                br[0, 6 * n + k : 6 * n + k + 1, :] = g1[n : n + 1, 128 * k : 128 * k + 128]

    @phase
    def small_results():
        rows = [jnp.concatenate([br[2, 6 * n + k : 6 * n + k + 1, :] for k in range(6)], 1) for n in range(2)]
        sums = jnp.concatenate(rows + [ar[2, 2:8, :]], 0)
        if inner > 1:
            small_out[...] = sums
            return
        share = width // 32
        owner = lax.axis_index("fsdp") * 4 + lax.axis_index("tp")
        moved = pltpu.roll(sums, width - owner * share, 1)
        square = jnp.sum(sums[4:7], axis=1, keepdims=True) / (sums[7:8, 0:1] * width)
        rms = jnp.sqrt(jnp.broadcast_to(square, (3, 128)))
        lane = lanes()
        row = jnp.where(lane == 0, rms[0:1], jnp.where(lane == 1, rms[1:2], rms[2:3]))
        small_out[0:4, :] = moved[0:4, 0:128]
        small_out[4:8, :] = jnp.broadcast_to(row, (4, 128))

    def give(k):
        held = (gq_out, go_out, gup_out, gdown_out, small_out)[k]
        return pltpu.make_async_copy(held, big_outs[k], give_sem.at[k])

    entry()
    q_in[0].s1()
    document_marks()
    for one in own_copies():
        one.wait()
    q_in[1].s1()
    first_norm_statistics()
    q_in[0].s2()
    q_in[2].s1()
    q_in[1].s2()
    q_in[0].s3()
    q_in[2].s2()
    o_in.s1()
    q_in[1].s3()
    m_in[0].s1()
    q_in[2].s3()
    first_norm()
    o_in.s2()
    m_in[1].s1()
    attention()
    out_projection()
    m_in[1].s4()
    m_in[0].s5()
    m_in[1].s5()

    mlp_hidden(0, (), (m_in[2].s3,), (), (m_in[3].s3,))
    m_in[4].s2()
    mlp_weight_grads(0)
    m_sum[0].s1()
    m_in[2].s4()
    m_in[5].s2()
    mlp_sums(0, (), (), (m_in[3].s4,))
    m_sum[0].s2()
    m_in[2].s5()
    m_in[3].s5()

    mlp_hidden(1, (), (m_in[4].s3,), (), (m_in[5].s3,))
    m_in[0].s6()
    m_in[1].s6()
    mlp_weight_grads(1)
    m_sum[1].s1()
    mlp_sums(1, (m_sum[0].s3,), (m_in[4].s4,), (), (m_in[5].s4,))
    m_sum[1].s2()
    m_in[4].s5()
    m_in[5].s5()

    mlp_hidden(2)
    m_in[2].s6()
    m_in[3].s6()
    mlp_weight_grads(2)
    m_sum[2].s1()
    m_sum[0].s4()
    mlp_sums(2, (), (m_sum[1].s3,))
    m_sum[2].s2()
    m_in[4].s6()
    m_in[5].s6()

    second_norm_back()
    early.run(0)
    o_in.s6()
    out_projection_back()
    o_sum.s1()
    m_sum[0].s5()
    m_sum[0].give_credit()
    pair_attention_back()
    pair_weight_grads()
    o_sum.s3()
    m_sum[0].take_credit()
    qa_sum.s1()
    odd_attention_back()
    odd_weight_grads()
    qb_sum.s1()
    qc_sum.s1()
    m_sum[2].s5()
    for g in q_in:
        g.s6()
    give(2).start()
    give(3).start()
    first_norm_back()
    late.run(0)
    o_sum.s5()
    give(1).start()
    qb_sum.s4()
    qc_sum.s4()
    late.take(0)
    late.run(1)
    qa_sum.s5()
    late.take(1)
    late.left()
    small_results()
    give(4).start()
    qb_sum.s5()
    for one in store_low():
        one.wait()
    store_grad().wait()
    qc_sum.s5()
    give(0).start()
    for k in range(5):
        give(k).wait()


def scatter_slots(rows, columns):
    return [
        pltpu.VMEM((2, 4, 2, rows, columns), BF),
        pltpu.VMEM((4, (rows // 2 + 15) // 16 * 16, columns), BF),
        pltpu.VMEM((4, rows // 2, columns), BF),
        pltpu.VMEM((4, rows, columns), BF),
        pltpu.VMEM((4, rows, columns), BF),
        pltpu.VMEM((3, rows, columns), BF),
    ]


def layer(inner, tokens, cotangent, segments, valid, wq, wo, up, down, *params):
    length, width = tokens.shape
    block = lambda rows, columns: pltpu.VMEM((2, 2, 4, 2, rows, columns), BF)
    small = (8, width) if inner > 1 else (8, 128)
    shapes = [(3, 96, 3 * HD), (3 * HD, 96), (96, width), (96, width), small]
    scratch = [pltpu.VMEM(shape, F32) for shape in shapes]
    scratch += [
        block(96, 640), block(96, 256), block(192, 256), block(192, 256), block(192, 256), block(192, 256),
        pltpu.VMEM((length, width), BF),
        pltpu.VMEM((length, width), BF),
        pltpu.VMEM((length, width), BF),
        pltpu.VMEM((4, length, 640), BF),
        pltpu.VMEM((4, length, 256), BF),
        pltpu.VMEM((4, length, 128), BF),
        pltpu.VMEM((length, 128), BF),
        pltpu.VMEM((length, 128), BF),
        pltpu.VMEM((128, length), BF),
        pltpu.VMEM((length, width), F32),
        pltpu.VMEM((length, width), BF),
        pltpu.VMEM((length, width), F32),
        pltpu.VMEM((length, width), F32),
        pltpu.VMEM((4, length, 256), BF),
        pltpu.VMEM((4, length, 256), BF),
        pltpu.VMEM((length, 1), F32),
        pltpu.VMEM((128, width), F32),
    ]
    scratch += [pltpu.VMEM((length, 128), F32)] * 2
    scratch += [scatter_slots(192, 256) * 3, scatter_slots(144, 256)]
    scratch += [
        pltpu.VMEM((3, 8, width), F32),
        pltpu.VMEM((10, 8, width), F32),
        pltpu.VMEM((3, 16, 128), F32),
        pltpu.VMEM((10, 16, 128), F32),
        pltpu.VMEM((8, width), F32),
        pltpu.SemaphoreType.DMA((10, 3)),
        pltpu.SemaphoreType.DMA((10, 6)),
        pltpu.SemaphoreType.DMA((7, 3)),
        pltpu.SemaphoreType.DMA((7, 5)),
        pltpu.SemaphoreType.REGULAR((1, 6)),
        pltpu.SemaphoreType.DMA((2, 2)),
        pltpu.SemaphoreType.DMA((2, 2)),
        pltpu.SemaphoreType.DMA((5,)),
        pltpu.SemaphoreType.DMA((8,)),
        pltpu.SemaphoreType.DMA((5,)),
    ]
    vmem, anywhere = pl.BlockSpec(memory_space=pltpu.VMEM), pl.BlockSpec(memory_space=pl.ANY)
    return pl.pallas_call(
        partial(kernel, inner, length),
        out_shape=[
            jax.ShapeDtypeStruct((length, width), BF),
            jax.ShapeDtypeStruct((length, width), F32),
        ]
        + [jax.ShapeDtypeStruct(shape, F32) for shape in shapes],
        in_specs=[anywhere, anywhere, vmem, vmem, vmem, vmem, anywhere, anywhere] + [vmem] * 4,
        out_specs=[anywhere] * (2 + len(shapes)),
        scratch_shapes=scratch,
        compiler_params=pltpu.CompilerParams(
            collective_id=0, has_side_effects=True, vmem_limit_bytes=63 * 2**20
        ),
    )(tokens, cotangent, segments, valid, wq, wo, up, down, *params)


def hand_over(arrays, share):
    count = len(arrays)
    pieces = []
    for k, a in enumerate(arrays):
        step = 256 if a.ndim == 2 and a.shape[0] % 256 == 0 else a.shape[0]
        pieces += [(k, start, step) for start in range(0, a.shape[0], step)]
    small = [(share,)] * 4 + [(3,)] if share else []
    shapes = [(a.shape, a.dtype) for a in arrays[: count - 1 if small else count]] + [(cut, F32) for cut in small]
    whole = len(shapes) - len(small)

    def body(*refs):
        came, went = refs[:count], refs[count : count + len(shapes)]
        held = refs[count + len(shapes) : 2 * count + len(shapes)]
        cuts, sems = refs[2 * count + len(shapes) : -1], refs[-1]

        def part(ref, n):
            _, start, step = pieces[n]
            return ref.at[pl.ds(start, step)] if step < ref.shape[0] else ref

        def fetch(n):
            k = pieces[n][0]
            return pltpu.make_async_copy(part(came[k], n), part(held[k], n), sems.at[0, n])

        def put(n):
            k = pieces[n][0]
            return pltpu.make_async_copy(part(held[k], n), part(went[k], n), sems.at[1, n])

        def put_cut(k):
            return pltpu.make_async_copy(cuts[k], went[whole + k], sems.at[1, len(pieces) + k])

        for n in reversed(range(len(pieces))):
            fetch(n).start()
        for n in reversed(range(len(pieces))):
            fetch(n).wait()
            if pieces[n][0] < whole:
                put(n).start()
                continue
            for k, cut in enumerate(small):
                cuts[k][...] = held[whole][k, 0 : cut[0]]
                put_cut(k).start()
        for n in range(len(pieces)):
            if pieces[n][0] < whole:
                put(n).wait()
        for k in range(len(small)):
            put_cut(k).wait()

    anywhere = pl.BlockSpec(memory_space=pltpu.HBM)
    return pl.pallas_call(
        body,
        out_shape=[jax.ShapeDtypeStruct(shape, dtype) for shape, dtype in shapes],
        in_specs=[anywhere] * count,
        out_specs=[anywhere] * len(shapes),
        scratch_shapes=[pltpu.VMEM(a.shape, a.dtype) for a in arrays]
        + [pltpu.VMEM(cut, F32) for cut in small]
        + [pltpu.SemaphoreType.DMA((2, len(pieces) + 5))],
        compiler_params=pltpu.CompilerParams(vmem_limit_bytes=63 * 2**20),
    )(*arrays)


def local(
    tokens, segment_ids, valid, ln1_gain, ln1_bias, w_qkv, w_out, ln2_gain, ln2_bias, w_up, w_down, cotangent
):
    length, width = tokens.shape
    holders = lax.axis_size("fsdp")
    inner = holders // 8
    groups = [[g * inner + i for i in range(inner)] for g in range(8)]

    def widen(block, axis=0):
        if inner == 1:
            return block
        return lax.all_gather(block, "fsdp", axis_index_groups=groups, axis=axis, tiled=True)

    def narrow(block, axis=0):
        if inner == 1:
            return block
        return lax.psum_scatter(
            block, "fsdp", scatter_dimension=axis, axis_index_groups=groups, tiled=True
        )

    params = [widen(one.reshape(1, -1), 1) for one in (ln1_gain, ln1_bias, ln2_gain, ln2_bias)]
    results = layer(
        inner, tokens, cotangent, segment_ids, valid.reshape(1, length),
        widen(w_qkv.transpose(1, 0, 2), 1), widen(w_out, 1), widen(w_up), widen(w_down.T), *params,
    )
    low, grad_tokens, gq, go, gup, gdown, *small = hand_over(results, width // 32 if inner == 1 else 0)
    if inner > 1:
        sums = lax.psum(small[0], "fsdp", axis_index_groups=groups)
        share = width // (holders * lax.axis_size("tp"))
        owner = lax.axis_index("fsdp") * lax.axis_size("tp") + lax.axis_index("tp")
        mine = lax.dynamic_slice_in_dim(sums[0:4], owner * share, share, 1)
        spread = jnp.sqrt(jnp.sum(sums[4:7], axis=1) / (sums[7, 0] * width))
        small = (mine[0], mine[1], mine[2], mine[3], spread)
    return (
        low, grad_tokens, small[0], small[1], narrow(gq, 1).transpose(1, 0, 2), narrow(go, 1),
        small[2], small[3], narrow(gup), narrow(gdown).T, small[4],
    )


def solution(mesh):
    both = ("fsdp", "tp")
    return jax.shard_map(
        local,
        mesh=mesh,
        in_specs=(
            P(both, None), P("fsdp", None), P(both), P("fsdp"), P("fsdp"), P("fsdp", None, "tp"),
            P("tp", "fsdp"), P("fsdp"), P("fsdp"), P("fsdp", "tp"), P("tp", "fsdp"), P(both, None),
        ),
        out_specs=(
            P(both, None), P(both, None), P(both), P(both), P("fsdp", None, "tp"), P("tp", "fsdp"),
            P(both), P(both), P("fsdp", "tp"), P("tp", "fsdp"), P(),
        ),
        check_vma=False,
    )
```

```python
from functools import partial

import jax
import jax.numpy as jnp
from jax import lax
from jax.experimental import pallas as pl
from jax.experimental.pallas import tpu as pltpu
from jax.sharding import PartitionSpec as P

HD = 64
BQ = 256
EPS = 1e-05
BIG = -1e30
F32 = jnp.float32
BF = jnp.bfloat16
NN = (((1,), (0,)), ((), ()))
NT = (((1,), (1,)), ((), ()))
TN = (((0,), (0,)), ((), ()))
MESH = pl.DeviceIdType.MESH
C0 = 0.7978845608
C1 = 0.7978845608 * 0.044715


def dot(a, b, dims=NN):
    return lax.dot_general(a, b, dims, preferred_element_type=F32)


def phase(body):
    return body


def remote(src, dst, send, recv, device):
    return pltpu.make_async_remote_copy(
        src_ref=src, dst_ref=dst, send_sem=send, recv_sem=recv,
        device_id=device, device_id_type=MESH,
    )


class Place:
    def __init__(self, inner):
        f = lax.axis_index("fsdp")
        t = lax.axis_index("tp")
        g = f // inner
        self.low = f % inner
        self.inner = inner
        self.z, self.y, self.x, self.c = g // 2, g % 2, t // 2, t % 2

    def device(self, z, y, x, c):
        return ((z * 2 + y) * self.inner + self.low, x * 2 + c)

    def core(self):
        return self.device(self.z, self.y, self.x, 1 - self.c)

    def xn(self):
        return self.device(self.z, self.y, 1 - self.x, self.c)

    def yn(self):
        return self.device(self.z, 1 - self.y, self.x, self.c)

    def cube(self, n):
        y, x, c = (self.y + n // 4) % 2, (self.x + n // 2) % 2, (self.c + n) % 2
        return self.device(self.z, y, x, c)

    def zn(self, d):
        return self.device((self.z + d) % 4, self.y, self.x, self.c)

    def reach(self, k):
        upper = self.z // 2
        return (3 - k) * (1 - upper) + (1 + k) * upper

    def zp(self, d):
        return self.device((self.z - d + 4) % 4, self.y, self.x, self.c)


def greet(inner):
    p = Place(inner)
    sem = pltpu.get_barrier_semaphore()
    for dev in [p.cube(n) for n in range(1, 8)] + [p.zn(d) for d in range(1, 4)]:
        pl.semaphore_signal(sem, inc=1, device_id=dev, device_id_type=MESH)


def met(inner):
    pl.semaphore_wait(pltpu.get_barrier_semaphore(), 10)


class Gather:
    def __init__(self, name, inner, buf, row0, rows, send, recv):
        self.name = name
        self.inner, self.buf, self.row0, self.rows = inner, buf, row0, rows
        self.send, self.recv = send, recv

    def own(self, x, c, z, y):
        return self.buf.at[x, c, z, y, pl.ds(self.row0, self.rows)]

    def group(self, x, c, y, half=None):
        start, size = self.row0, self.rows
        if half is not None:
            cut = (size // 2 + 15) // 16 * 16
            start, size = (start + cut, size - cut) if half else (start, cut)
        return self.buf.at[x, c, :, y, pl.ds(start, size)]

    def parts(self, slot):
        p = Place(self.inner)
        x, c, z, y = p.x, p.c, p.z, p.y
        if slot < 3:
            mine = self.own(x, c, z, y)
            return mine, mine, p.zn(p.reach(slot))
        if slot == 3:
            return self.group(x, c, y), self.group(1 - x, c, y), p.xn()
        if slot == 4:
            return self.group(x, c, y), self.group(x, c, 1 - y), p.yn()
        if slot == 5:
            return self.group(1 - x, c, y, 0), self.group(1 - x, c, 1 - y, 0), p.yn()
        if slot == 6:
            return self.group(x, c, 1 - y, 1), self.group(1 - x, c, 1 - y, 1), p.xn()
        xx = x if slot in (7, 9) else 1 - x
        yy = y if slot in (7, 8) else 1 - y
        return self.group(xx, c, yy), self.group(xx, 1 - c, yy), p.core()

    SENT = (0, 0, 0, 1, 1, 2, 2, 1, 2, 2, 2)
    CAME = (0, 0, 0, 1, 2, 3, 3, 4, 5, 4, 5)

    def start(self, *slots):
        for slot in slots:
            mine, _, dev = self.parts(slot)
            remote(mine, mine, self.send.at[self.SENT[slot]], self.recv.at[self.CAME[slot]], dev).start()

    def bytes_of(self, blocks):
        rows = pl.ds(self.row0, self.rows)
        if blocks == 3:
            return self.buf.at[0, 0, 0:3, 0, rows]
        if blocks == 4:
            return self.buf.at[0, 0, :, 0, rows]
        if blocks == 8:
            return self.buf.at[0, 0, :, :, rows]
        if blocks == 12:
            return self.buf.at[:, :, 0:3, 0, rows]
        return self.buf.at[0, :, :, :, rows]

    def arrive(self, group):
        ref = self.bytes_of((3, 4, 4, 4, 8, 8)[group])
        dev = Place(self.inner).core()
        remote(ref, ref, self.send.at[0], self.recv.at[group], dev).wait_recv()

    def left(self):
        for group, blocks in enumerate((3, 12, 16)):
            ref = self.bytes_of(blocks)
            dev = Place(self.inner).core()
            remote(ref, ref, self.send.at[group], self.recv.at[0], dev).wait_send()

    def s1(self):
        self.start(0, 1, 2)

    def s2(self):
        self.arrive(0)
        self.start(3, 4, 7)

    def s3(self):
        self.arrive(2)
        self.start(6, 9)
        self.arrive(1)
        self.start(5, 8)

    def s4(self):
        self.arrive(3)
        self.start(10)

    def near(self):
        self.arrive(4)

    def far(self):
        self.arrive(5)

    def s5(self):
        self.near()
        self.far()

    def s6(self):
        self.left()


class Scatter:
    def __init__(self, name, inner, buf, block, slots, place, send, recv, credit, out):
        self.name = name
        self.inner, self.buf, self.slots = inner, buf, slots
        self.row0, self.rows, self.col0, columns = block
        self.half = (self.rows // 2 + 15) // 16 * 16
        row, upper, lower, col = place
        self.land = (
            slice(row, row + self.rows), slice(upper, upper + self.half),
            slice(lower, lower + self.rows - self.half), slice(col, col + columns),
        )
        self.cols = slice(self.col0, self.col0 + columns)
        self.send, self.recv = send, recv
        self.credit, self.out = credit, out

    def parts(self, slot):
        p = Place(self.inner)
        x, c, z, y = p.x, p.c, p.z, p.y
        buf, cols = self.buf, self.cols
        r1, ra, rb, rx, ry, rz = self.slots
        rows, upper, lower = self.spans()
        land, land_a, land_b, land_cols = self.land
        if slot == 0:
            return buf.at[:, 1 - c, :, :, rows, cols], r1.at[:, :, :, land, land_cols], p.core()
        if slot == 1:
            return buf.at[1 - x, c, :, 1 - y, upper, cols], ra.at[:, land_a, land_cols], p.yn()
        if slot == 2:
            return buf.at[1 - x, c, :, 1 - y, lower, cols], rb.at[:, land_b, land_cols], p.xn()
        if slot == 3:
            return buf.at[1 - x, c, :, y, rows, cols], rx.at[:, land, land_cols], p.xn()
        if slot == 4:
            return buf.at[x, c, :, 1 - y, rows, cols], ry.at[:, land, land_cols], p.yn()
        d = p.reach(slot - 5)
        return buf.at[x, c, (z + d) % 4, y, rows, cols], rz.at[d - 1, land, land_cols], p.zn(d)

    def spans(self):
        start, end = self.row0, self.row0 + self.rows
        return slice(start, end), slice(start, start + self.half), slice(start + self.half, end)

    SENT = (0, 1, 1, 1, 1, 2, 2, 2)
    CAME = (0, 1, 2, 3, 3, 4, 4, 4)

    def start(self, *slots):
        for slot in slots:
            src, dst, dev = self.parts(slot)
            remote(src, dst, self.send.at[self.SENT[slot]], self.recv.at[self.CAME[slot]], dev).start()

    def arrive(self, group):
        land, _, _, cols = self.land
        if group < 3:
            ref = self.parts(group)[1]
        elif group == 3:
            ref = self.slots[0].at[0, :, :, land, cols]
        else:
            ref = self.slots[5].at[:, land, cols]
        remote(ref, ref, self.send.at[0], self.recv.at[group], Place(self.inner).core()).wait_recv()

    def left(self):
        rows, cols = self.spans()[0], self.cols
        refs = (
            self.buf.at[:, 0, :, :, rows, cols], self.buf.at[:, :, 0:3, 0, rows, cols],
            self.buf.at[0, 0, 0:3, 0, rows, cols],
        )
        for group, ref in enumerate(refs):
            dev = Place(self.inner).core()
            remote(ref, ref, self.send.at[group], self.recv.at[0], dev).wait_send()

    def take_credit(self):
        for i in range(6):
            pl.semaphore_wait(self.credit.at[i], 1)

    def give_credit(self):
        p = Place(self.inner)
        for i, dev in enumerate((p.core(), p.xn(), p.yn(), p.zp(1), p.zp(2), p.zp(3))):
            pl.semaphore_signal(self.credit.at[i], inc=1, device_id=dev, device_id_type=MESH)

    def s1(self):
        self.start(0)

    def add(self, x, y, rows, *others):
        c = Place(self.inner).c

        @pl.loop(0, 4)
        def _(z):
            total = self.buf[x, c, z, y, rows, self.cols]
            if len(others) > 1:
                total = total.astype(F32)
            for other in others:
                total = total + other(z).astype(total.dtype)
            self.buf[x, c, z, y, rows, self.cols] = total.astype(BF)

    def s2(self):
        p = Place(self.inner)
        r1, (land, _, _, cols) = self.slots[0], self.land
        self.arrive(0)
        for x, y in ((1 - p.x, 1 - p.y), (1 - p.x, p.y), (p.x, 1 - p.y), (p.x, p.y)):
            self.add(x, y, self.spans()[0], lambda z: r1[x, z, y, land, cols])
            if x is not p.x and y is not p.y:
                self.start(1, 2)

    def s3(self):
        p = Place(self.inner)
        _, upper, lower = self.spans()
        _, land_a, land_b, cols = self.land
        ra, rb = self.slots[1:3]
        self.arrive(1)
        self.add(1 - p.x, p.y, upper, lambda z: ra[z, land_a, cols])
        self.start(3)
        self.arrive(2)
        self.add(p.x, 1 - p.y, lower, lambda z: rb[z, land_b, cols])
        self.start(4)

    def s4(self):
        p = Place(self.inner)
        land, _, _, cols = self.land
        rx, ry = self.slots[3:5]
        self.arrive(3)
        self.add(p.x, p.y, self.spans()[0], lambda z: rx[z, land, cols], lambda z: ry[z, land, cols])
        self.start(5, 6, 7)

    def s5(self):
        p = Place(self.inner)
        land, _, _, cols = self.land
        rz = self.slots[5]
        self.arrive(4)
        total = self.buf[p.x, p.c, p.z, p.y, self.spans()[0], self.cols].astype(F32)
        for d in range(3):
            total = total + rz[d, land, cols].astype(F32)
        self.out(total)
        self.left()


class Total:
    def __init__(self, name, inner, ref, got, send, recv):
        self.name = name
        self.inner, self.ref, self.got, self.send, self.recv = inner, ref, got, send, recv

    def copy(self, slot):
        p = Place(self.inner)
        dev = p.cube(slot + 1) if slot < 7 else p.zn(slot - 6)
        stage = 0 if slot < 7 else 1
        return remote(self.ref.at[stage], self.got.at[slot], self.send.at[stage], self.recv.at[stage], dev)

    def slots(self, stage):
        return range(7) if stage == 0 else range(7, 10)

    def all_of(self, stage):
        span = self.slots(stage)
        ref = self.got.at[span.start : span.stop]
        return remote(ref, ref, self.send.at[stage], self.recv.at[stage], Place(self.inner).core())

    def run(self, stage):
        for slot in self.slots(stage):
            self.copy(slot).start()

    def take(self, stage):
        self.all_of(stage).wait_recv()
        total = self.ref[stage]
        for slot in self.slots(stage):
            total = total + self.got[slot]
        self.ref[stage + 1] = total

    def left(self):
        for stage in range(2):
            self.all_of(stage).wait_send()


def head_parts(t_ref, k2_ref, t, h, qs, kr):
    if h < 2:
        return t_ref[t, qs, 0:128], t_ref[t, kr, 128:256], t_ref[t, kr, 256:384]
    return t_ref[t, qs, 384:512], k2_ref[kr, :], t_ref[t, kr, 512:640]


def lanes():
    return lax.broadcasted_iota(jnp.int32, (1, 128), 1)


def roll_key(t_ref, k2_ref, t):
    k2_ref[...] = pltpu.roll(t_ref[t, :, 384:512].astype(F32), 64, 1).astype(BF)


def below(transposed, size=BQ):
    r = lax.broadcasted_iota(jnp.int32, (size, size), 0)
    c = lax.broadcasted_iota(jnp.int32, (size, size), 1)
    return r <= c if transposed else r >= c


def attend(t_ref, l_ref, kx_ref, k2_ref, c_ref, t, length):
    lane = lanes()
    low = lane < 64
    roll_key(t_ref, k2_ref, t)
    for i in range(length // BQ):
        first = max(0, i * BQ - length // 2)
        width = (i + 1) * BQ - first
        qs, kr = slice(i * BQ, (i + 1) * BQ), slice(first, first + width)
        kx = kx_ref[kr, :]
        doc = kx_ref[qs, :].astype(F32)
        qx = jnp.where(lane < 8, BIG * (1.0 - doc), 0.0).astype(BF)
        marks = qx
        outs = []
        for h in range(3):
            q, k, v = head_parts(t_ref, k2_ref, t, h, qs, kr)
            keep = jnp.logical_not(low) if h == 1 else low
            q = jnp.where(keep, q * BF(HD ** -0.5), BF(0))
            s = dot(jnp.concatenate([q, qx], 1), jnp.concatenate([k, kx], 1), NT)
            edge = jnp.where(below(False), s[:, width - BQ :], BIG)
            s = edge if width == BQ else jnp.concatenate([s[:, : width - BQ], edge], 1)
            top = jnp.max(s, axis=1, keepdims=True)
            p = jnp.exp(s - top).astype(BF)
            both = dot(p, jnp.concatenate([v, jnp.ones((width, 128), BF)], 1))
            total = both[:, 128:256]
            outs.append(both[:, :128] / total)
            rest = -(top + jnp.log(total))
            for n in range(3):
                piece = rest.astype(BF)
                marks = jnp.where(lane == 8 + 16 * h + n, piece, marks)
                rest = rest - piece.astype(F32)
        l_ref[t, qs, :] = marks
        c_ref[t, qs, 0:128] = jnp.where(low, outs[0], outs[1]).astype(BF)
        c_ref[t, qs, 128:256] = jnp.where(low, outs[2], 0.0).astype(BF)


def attend_back(t_ref, l_ref, kx_ref, k2_ref, kt_ref, c_ref, do_ref, sums, heads, t, length):
    lane = lanes()
    low = lane < 64
    dk_ref, dv_ref = sums
    odd = heads == (2,)
    size = BQ
    if odd:
        roll_key(t_ref, k2_ref, t)
        kt_ref[...] = k2_ref[...].T
    else:
        kt_ref[...] = t_ref[t, :, 128:256].T
    for ref in sums:
        ref[...] = jnp.zeros_like(ref)
    for i in range(length // size):
        first = max(0, i * size - length // 2)
        width = (i + 1) * size - first
        qs, kr = slice(i * size, (i + 1) * size), slice(first, first + width)
        marks = l_ref[t, qs, :]
        side = slice(128, 256) if odd else slice(0, 128)
        qs_all, dos, left, right = [], [], [], []
        for h in heads:
            q, k, v = head_parts(t_ref, k2_ref, t, h, qs, kr)
            keep = jnp.logical_not(low) if h == 1 else low
            q = jnp.where(keep, q * BF(HD ** -0.5), BF(0))
            do = jnp.where(keep, do_ref[t, qs, side], BF(0))
            dd = (do.astype(F32) * c_ref[t, qs, side].astype(F32)).astype(BF)
            mine = (lane < 8) | ((lane >= 8 + 16 * h) & (lane < 24 + 16 * h))
            qs_all.append(q)
            dos.append(do)
            left.append(jnp.concatenate([q, jnp.where(mine, marks, BF(0))], 1))
            right.append(jnp.concatenate([do, dd], 1))
        s_all = dot(jnp.concatenate([k, kx_ref[kr, :]], 1), jnp.concatenate(left, 0), NT)
        minus = jnp.full((width, 128), -1.0, BF)
        dp_all = dot(jnp.concatenate([v, minus], 1), jnp.concatenate(right, 0), NT)
        ps, dss, grads = [], [], []
        for n in range(len(heads)):
            s = s_all[:, n * size : (n + 1) * size]
            edge = jnp.where(below(True, size), s[width - size :], BIG)
            s = edge if width == size else jnp.concatenate([s[: width - size], edge], 0)
            p = jnp.exp(s)
            ds = (p * dp_all[:, n * size : (n + 1) * size]).astype(BF)
            ps.append(p.astype(BF))
            dss.append(ds)
            grads.append(dot(kt_ref[64 * n : 64 * n + 64, kr], ds))
        if odd:
            grads.append(jnp.zeros((64, size), F32))
        grad = (jnp.concatenate(grads, 0).T * HD ** -0.5).astype(BF)
        dv_ref[kr, :] += dot(jnp.concatenate(ps, 1), jnp.concatenate(dos, 0))
        dk_ref[kr, :] += dot(jnp.concatenate(dss, 1), jnp.concatenate(qs_all, 0))
        if odd:
            t_ref[t, qs, 384:512] = jnp.where(low, grad, t_ref[t, qs, 384:512])
        else:
            t_ref[t, qs, 0:128] = grad
    if odd:
        moved = pltpu.roll(dk_ref[...], 64, 1).astype(BF)
        t_ref[t, :, 384:512] = jnp.where(low, t_ref[t, :, 384:512], moved)
        t_ref[t, :, 512:640] = dv_ref[...].astype(BF)
    else:
        t_ref[t, :, 128:256] = dk_ref[...].astype(BF)
        t_ref[t, :, 256:384] = dv_ref[...].astype(BF)


def stats(v):
    mean = jnp.mean(v, axis=-1, keepdims=True)
    center = v - mean
    scale = lax.rsqrt(jnp.mean(center * center, axis=-1, keepdims=True) + EPS)
    return center * scale, scale


def norm_back(v, q, gain):
    n, scale = stats(v)
    e = q * gain
    back = scale * (e - jnp.mean(e, -1, keepdims=True) - n * jnp.mean(e * n, -1, keepdims=True))
    return back, jnp.sum(q * n, 0, keepdims=True), jnp.sum(q, 0, keepdims=True)


def kernel(
    inner, length,
    tok_in, cot_in, seg, valid, wq_in, wo_in, up_in, down_in, par_a, par_b, par_c, par_d,
    lo_out, gt_out, *rest,
):
    big_outs = rest[0:5]
    (
        gq_out, go_out, gup_out, gdown_out, small_out,
        bq, bo, bm0, bm1, bm2, gb,
        tok, cot, n1, tt, cc, ll, kx, k2, kt, wo, mid, n2, acc, gn, act, gu, val, par,
        dk, dv,
        m_sets, o_set, ar, ar_got, br, br_got, g1,
        ag_send, ag_recv, rs_send, rs_recv, credit, ar_send, ar_recv, local_sem, own_sem, give_sem,
    ) = rest[5:]
    width = tok.shape[1]
    bm = (bm0, bm1, bm2)
    blocks = [(bq, 0, 32), (bq, 32, 32), (bq, 64, 32), (bo, 0, 144)]
    blocks += [(b, r0, 96) for b in bm for r0 in (0, 96)]
    gathers = [
        Gather(f"gather{k}", inner, b, r0, rows, ag_send.at[k], ag_recv.at[k])
        for k, (b, r0, rows) in enumerate(blocks)
    ]
    here = Place(inner)
    mine = (here.x, here.c, here.z, here.y)

    def put_mlp(j):
        def put(total):
            gup_out[:, 256 * j : 256 * j + 256] = total[0:96]
            gdown_out[:, 256 * j : 256 * j + 256] = total[96:192]

        return put

    def put_out(total):
        go_out[0 : 2 * HD] = total[0:96].T
        third = total[96:144].T
        go_out[2 * HD : 3 * HD] = jnp.concatenate([third[0:64], third[64:128]], 1)

    def put_pair(total):
        gq_out[0, 0:80, 0:128] = total[:, 0:128]
        gq_out[1, 0:80, 0:128] = total[:, 128:256]

    def put_pair_rest(total):
        gq_out[0, 80:96, 0:128] = total[0:16, 0:128]
        gq_out[1, 80:96, 0:128] = total[0:16, 128:256]
        gq_out[2, 0:48, 0:128] = total[16:64, 0:128]
        gq_out[2, 48:96, 0:128] = total[16:64, 128:256]

    def put_odd(total):
        gq_out[0, 0:80, 128:192] = total[:, 0:64]
        gq_out[1, 0:80, 128:192] = total[:, 64:128]

    def put_rest(total):
        gq_out[0, 80:96, 128:192] = total[0:16, 0:64]
        gq_out[1, 80:96, 128:192] = total[0:16, 64:128]
        gq_out[2, 0:48, 128:192] = total[16:64, 0:64]
        gq_out[2, 48:96, 128:192] = total[16:64, 64:128]

    grads = (gb, bm0, bm1)
    sets = [m_sets[0:6], m_sets[6:12], m_sets[12:18]]
    start = (0, 0, 0, 0)
    plan = [
        (gb, (0, 192, 0, 256), sets[0], start, put_mlp(0)),
        (bm0, (0, 192, 0, 256), sets[1], start, put_mlp(1)),
        (bm1, (0, 192, 0, 256), sets[2], start, put_mlp(2)),
        (bm2, (0, 144, 0, 128), o_set, start, put_out),
        (gb, (0, 80, 0, 256), sets[0], start, put_pair),
        (gb, (80, 64, 0, 256), sets[0], (80, 48, 32, 0), put_pair_rest),
        (bm2, (0, 80, 128, 128), o_set, (0, 0, 0, 128), put_odd),
        (bm2, (80, 64, 128, 128), o_set, (80, 48, 32, 128), put_rest),
    ]
    scatters = [
        Scatter(
            f"scatter{k}", inner, b, block, slots, place,
            rs_send.at[k], rs_recv.at[k], credit.at[0], out,
        )
        for k, (b, block, slots, place, out) in enumerate(plan)
    ]
    m_sum, o_sum, qa_sum, qd_sum, qb_sum, qc_sum = scatters[0:3], *scatters[3:8]
    q_in, o_in, m_in = gathers[0:3], gathers[3], gathers[4:10]
    early = Total("early", inner, ar, ar_got, ar_send.at[0], ar_recv.at[0])
    late = Total("late", inner, br, br_got, ar_send.at[1], ar_recv.at[1])

    def after(t, last, *steps):
        @pl.when(t == last)
        def _():
            for step in steps:
                step()

    def rows_of(i, size):
        return pl.ds(pl.multiple_of(i * size, size), size)

    def weight(buf, t, r0, rows, columns):
        return buf[t // 2, t % 2, :, :, r0 : r0 + rows, columns].reshape(8 * rows, -1)

    def fold(columns):
        parts = columns.reshape(8, 96, 64)
        halves = [parts[:, 48 * n : 48 * n + 48].reshape(8 * 48, 64) for n in range(2)]
        return jnp.concatenate(halves, 1).astype(BF).reshape(4, 2, 48, 128)

    def cat(ref, s):
        return jnp.concatenate([ref[t, s, :] for t in range(4)], 1)

    def own_copies():
        copies = []
        for j in range(3):
            cols = pl.ds(256 * j, 256)
            copies.append((up_in.at[:, cols], bm[j].at[(*mine, pl.ds(0, 96))]))
            copies.append((down_in.at[:, cols], bm[j].at[(*mine, pl.ds(96, 96))]))
        copies += [(tok_in, tok), (cot_in, cot)]
        return [pltpu.make_async_copy(src, dst, own_sem.at[k]) for k, (src, dst) in enumerate(copies)]

    @phase
    def entry():
        for one in own_copies():
            one.start()
        greet(inner)
        q, k, v = (wq_in[n] for n in range(3))
        for n, one in enumerate((q, k, v)):
            bq[(*mine, slice(None), slice(128 * n, 128 * n + 128))] = one[:, 0:128]
        odd = [one[:, 128:192].astype(F32) for one in (q, k, v)]
        bq[(*mine, slice(None), slice(384, 512))] = jnp.concatenate(odd[0:2], 1).astype(BF)
        params = jnp.concatenate([one[...].astype(F32) for one in (par_a, par_b, par_c, par_d)] + [jnp.zeros((124, 96), F32)], 0).T[:, 0:64]
        bq[(*mine, slice(None), slice(512, 640))] = jnp.concatenate([odd[2], params], 1).astype(BF)
        met(inner)

    @phase
    def document_marks():
        me_t = lax.axis_index("tp")
        row = seg[pl.ds(me_t, 1), :].astype(F32)
        lane_id = lax.broadcasted_iota(jnp.int32, (128, length), 0)
        marks = jnp.where(row == lane_id.astype(F32), 1.0, 0.0)
        marks = jnp.where(lane_id < 8, marks, 0.0)
        low4 = lane_id % 16
        ones = (lane_id >= 8) & (lane_id < 56) & (low4 >= 8) & (low4 < 11)
        marks = jnp.where(ones, 1.0, marks)
        marks = jnp.where(lane_id == 64, valid[...].astype(F32), marks)
        columns = marks.T
        val[...] = columns[:, 64:65]
        kx[...] = jnp.where(lanes() < 64, columns, 0.0).astype(BF)
        ar[0] = jnp.zeros_like(ar.at[0])
        br[0] = jnp.zeros_like(br.at[0])
        g1[...] = jnp.zeros_like(g1)
        count = jnp.sum(valid[...].astype(F32), axis=1, keepdims=True)
        ar[0, 7:8, 0:128] = jnp.broadcast_to(count, (1, 128))
        wide = jnp.concatenate([wo_in[...].astype(F32), jnp.zeros((64, 96), F32)], 0).T
        third = wide[:, 128:192]
        bo[(*mine, slice(0, 96))] = wide[:, 0:128].astype(BF)
        bo[(*mine, slice(96, 144))] = jnp.concatenate([third[0:48], third[48:96]], 1).astype(BF)

    @phase
    def first_norm_statistics():
        @pl.loop(0, length // 256)
        def _(i):
            s = rows_of(i, 256)
            mid[s, :] = stats(tok[s, :].astype(F32))[0]

    @phase
    def first_norm():
        par[...] = bq[here.x, here.c, :, :, :, 512:640].reshape(width, 128).astype(F32).T

        @pl.loop(0, length // 256)
        def _(i):
            s = rows_of(i, 256)
            n1[s, :] = (mid[s, :] * par[64:65, :] + par[65:66, :]).astype(BF)

    @phase
    def attention():
        @pl.loop(0, 4)
        def _(n):
            x, c = (here.x + n // 2) % 2, (here.c + n % 2) % 2
            t = 2 * x + c
            w = bq[x, c].reshape(width, 640)

            @pl.loop(0, length // 512)
            def _(i):
                s = rows_of(i, 512)
                tt[t, s, :] = dot(n1[s, :], w).astype(BF)

            after(n, 1, m_in[1].s2, m_in[2].s1)
            after(n, 3, m_in[1].s3, m_in[2].s2, m_in[5].s1)
            attend(tt, ll, kx, k2, cc, t, length)
            after(n, 0, *[g.s4 for g in q_in], *[g.near for g in q_in], m_in[0].s2)
            after(n, 1, o_in.s3, m_in[3].s1)
            after(n, 2, m_in[0].s3, *[g.far for g in q_in], m_in[4].s1)
            after(n, 3, o_in.s4, m_in[3].s2, m_in[0].s4, o_in.s5)

    def out_weight(t):
        return jnp.concatenate([weight(bo, t, 0, 96, slice(0, 128)), wo[t]], 1)

    @phase
    def out_projection():
        for t in range(4):
            third = bo[t // 2, t % 2, :, :, 96:144, :].reshape(8, 48, 128)
            turned = pltpu.roll(third.astype(F32).reshape(8 * 48, 128), 64, 1).astype(BF)
            wo[t] = jnp.concatenate([third, turned.reshape(8, 48, 128)], 1).reshape(width, 128)

        @pl.loop(0, length // 256)
        def _(i):
            s = rows_of(i, 256)
            branch = jnp.zeros((256, width), F32)
            for t in range(4):
                branch = branch + dot(cc[t, s, :], out_weight(t), NT)
            v = tok[s, :].astype(F32) + branch
            mid[s, :] = v
            ar[0, 5:6, :] += jnp.sum(val[s, :] * (branch * branch), 0, keepdims=True)
            n, _ = stats(v)
            n2[s, :] = (n * par[66:67, :] + par[67:68, :]).astype(BF)

    def mlp_hidden(j, *steps):
        b = bm[j]

        @phase
        def hidden():
            @pl.loop(0, 4)
            def _(t):
                up = weight(b, t, 0, 96, slice(0, 256))
                down = weight(b, t, 96, 96, slice(0, 256))

                def finish(s, v, ga):
                    v2 = v * v
                    th = jnp.tanh(v * (C0 + C1 * v2))
                    h = 0.5 + 0.5 * th
                    act[t, s, :] = (v * h).astype(BF)
                    slope = h + (0.5 * v) * (1.0 - th * th) * (C0 + (3.0 * C1) * v2)
                    gu[t, s, :] = (ga * slope).astype(BF)

                waiting = None
                for i in range(length // 128):
                    s = slice(128 * i, 128 * i + 128)
                    now = (s, dot(n2[s, :], up), dot(cot[s, :], down))
                    if waiting is not None:
                        finish(*waiting)
                    waiting = now
                finish(*waiting)

                for k, step in enumerate(steps):
                    after(t, k, *step)

        hidden()

    def mlp_sums(j, *steps):
        b = bm[j]

        def wcat(r0):
            return jnp.concatenate([weight(b, t, r0, 96, slice(0, 256)) for t in range(4)], 1)

        @phase
        def sums():
            @pl.loop(0, length // 512)
            def _(i):
                s = rows_of(i, 512)
                one = dot(cat(act, s), wcat(96), NT)
                two = dot(cat(gu, s), wcat(0), NT)
                if j == 0:
                    acc[s, :] = one
                    gn[s, :] = two
                else:
                    acc[s, :] += one
                    gn[s, :] += two
                for k, step in enumerate(steps):
                    after(i, k, *step)

        sums()

    def mlp_weight_grads(j, *steps):
        b = grads[j]

        @phase
        def weight_grads():
            for t in range(4):
                gup = dot(n2[...], gu[t], TN).astype(BF)
                b[t // 2, t % 2, :, :, 0:96, :] = gup.reshape(4, 2, 96, 256)
                gdown = dot(cot[...], act[t], TN).astype(BF)
                b[t // 2, t % 2, :, :, 96:192, :] = gdown.reshape(4, 2, 96, 256)
                for step in steps[t : t + 1]:
                    step()

        weight_grads()

    def store_low():
        return [
            pltpu.make_async_copy(gu.at[k], lo_out.at[:, pl.ds(256 * k, 256)], local_sem.at[k])
            for k in range(width // 256)
        ]

    @phase
    def second_norm_back():
        @pl.loop(0, length // 256)
        def _(i):
            s = rows_of(i, 256)
            v = mid[s, :]
            mlp = acc[s, :]
            out = v + mlp
            weight_rows = val[s, :]
            ar[0, 4:5, :] += jnp.sum(weight_rows * (out * out), 0, keepdims=True)
            ar[0, 6:7, :] += jnp.sum(weight_rows * (mlp * mlp), 0, keepdims=True)
            low_out = out.astype(BF)
            for k in range(width // 256):
                gu[k, s, :] = low_out[:, 256 * k : 256 * k + 256]
            back, g_gain, g_bias = norm_back(v, gn[s, :], par[66:67, :])
            ar[0, 2:3, :] += g_gain
            ar[0, 3:4, :] += g_bias
            grad = cot[s, :].astype(F32) + back
            mid[s, :] = grad
            n2[s, :] = grad.astype(BF)

        for one in store_low():
            one.start()

    @phase
    def out_projection_back():
        @pl.loop(0, 4)
        def _(t):
            act[t] = dot(n2[...], out_weight(t)).astype(BF)
            grad = dot(n2[...], cc[t], TN)
            bm2[t // 2, t % 2, :, :, 0:96, 0:128] = grad[:, 0:128].astype(BF).reshape(4, 2, 96, 128)
            bm2[t // 2, t % 2, :, :, 96:144, 0:128] = fold(grad[:, 128:192])

    @phase
    def pair_attention_back():
        @pl.loop(0, 4)
        def _(t):
            attend_back(tt, ll, kx, k2, kt, cc, act, (dk, dv), (0, 1), t, length)
            after(t, 0, o_sum.s2)
            after(t, 1, m_sum[1].s4)

    def early_take_0():
        early.take(0)
        early.run(1)

    def early_take_1():
        early.take(1)
        early.left()

    @phase
    def pair_weight_grads():
        @pl.loop(0, 2)
        def _(x):
            both = jnp.concatenate([tt[2 * x, :, 0:384], tt[2 * x + 1, :, 0:384]], 1)
            grads = dot(n1[...], both, TN).astype(BF)
            for c in range(2):
                grad = grads[:, 384 * c : 384 * c + 384]
                gb[x, c, :, :, 0:96, :] = grad[:, 0:256].reshape(4, 2, 96, 256)
                third = grad[:, 256:384].reshape(4, 2, 96, 128)
                gb[x, c, :, :, 96:144, 0:128] = third[:, :, 0:48]
                gb[x, c, :, :, 96:144, 128:256] = third[:, :, 48:96]

    @phase
    def odd_weight_grads():
        @pl.loop(0, 4)
        def _(t):
            grad = dot(n1[...], tt[t, :, 384:640], TN)
            bm2[t // 2, t % 2, :, :, 0:96, 128:256] = grad[:, 0:128].astype(BF).reshape(4, 2, 96, 128)
            bm2[t // 2, t % 2, :, :, 96:144, 128:256] = fold(grad[:, 128:192])

    @phase
    def odd_attention_back():
        @pl.loop(0, 4)
        def _(t):
            attend_back(tt, ll, kx, k2, kt, cc, act, (dk, dv), (2,), t, length)
            after(t, 0, qa_sum.s2)
            after(t, 1, qd_sum.s2, m_sum[1].s5, early_take_0)
            after(t, 2, qa_sum.s3, o_sum.s4)
            after(t, 3, qd_sum.s3)

    def store_grad():
        return pltpu.make_async_copy(acc, gt_out, local_sem.at[4])

    @phase
    def first_norm_back():
        @pl.loop(0, length // 256)
        def _(i):
            s = rows_of(i, 256)
            w = jnp.concatenate([weight(bq, t, 0, 96, slice(0, 640)) for t in range(4)], 1)
            grad = dot(cat(tt, s), w, NT)
            after(i, 2, qb_sum.s3, qc_sum.s3)
            back, g_gain, g_bias = norm_back(tok[s, :].astype(F32), grad, par[64:65, :])
            g1[0:1, :] += g_gain
            g1[1:2, :] += g_bias
            acc[s, :] = mid[s, :] + back
            after(i, 0, qb_sum.s2, qc_sum.s2, qa_sum.s4)
            after(i, 1, qd_sum.s4)

        store_grad().start()
        for k in range(width // 128):
            for n in range(2):
                br[0, 6 * n + k : 6 * n + k + 1, :] = g1[n : n + 1, 128 * k : 128 * k + 128]

    @phase
    def small_results():
        rows = [jnp.concatenate([br[2, 6 * n + k : 6 * n + k + 1, :] for k in range(6)], 1) for n in range(2)]
        sums = jnp.concatenate(rows + [ar[2, 2:8, :]], 0)
        if inner > 1:
            small_out[...] = sums
            return
        share = width // 32
        owner = lax.axis_index("fsdp") * 4 + lax.axis_index("tp")
        moved = pltpu.roll(sums, width - owner * share, 1)
        square = jnp.sum(sums[4:7], axis=1, keepdims=True) / (sums[7:8, 0:1] * width)
        rms = jnp.sqrt(jnp.broadcast_to(square, (3, 128)))
        lane = lanes()
        row = jnp.where(lane == 0, rms[0:1], jnp.where(lane == 1, rms[1:2], rms[2:3]))
        small_out[0:4, :] = moved[0:4, 0:128]
        small_out[4:8, :] = jnp.broadcast_to(row, (4, 128))

    def give(k):
        held = (gq_out, go_out, gup_out, gdown_out, small_out)[k]
        return pltpu.make_async_copy(held, big_outs[k], give_sem.at[k])

    entry()
    q_in[0].s1()
    document_marks()
    for one in own_copies():
        one.wait()
    q_in[1].s1()
    first_norm_statistics()
    q_in[0].s2()
    q_in[2].s1()
    q_in[1].s2()
    q_in[0].s3()
    q_in[2].s2()
    o_in.s1()
    q_in[1].s3()
    m_in[0].s1()
    q_in[2].s3()
    first_norm()
    o_in.s2()
    m_in[1].s1()
    attention()
    out_projection()
    m_in[1].s4()
    m_in[0].s5()
    m_in[1].s5()

    mlp_hidden(0, (), (m_in[2].s3,), (), (m_in[3].s3,))
    m_in[4].s2()
    mlp_weight_grads(0)
    m_sum[0].s1()
    m_in[2].s4()
    m_in[5].s2()
    mlp_sums(0, (m_in[3].s4,))
    m_sum[0].s2()
    m_in[2].s5()
    m_in[3].s5()

    mlp_hidden(1, (), (m_in[4].s3,))
    m_in[0].s6()
    m_in[1].s6()
    mlp_weight_grads(1, lambda: None, m_in[5].s3)
    m_sum[1].s1()
    mlp_sums(1, (m_sum[0].s3,), (m_in[4].s4, m_in[5].s4))
    m_sum[1].s2()
    m_in[4].s5()
    m_in[5].s5()

    mlp_hidden(2)
    m_in[2].s6()
    m_in[3].s6()
    mlp_weight_grads(2)
    m_sum[2].s1()
    m_sum[0].s4()
    mlp_sums(2)
    m_sum[2].s2()
    m_sum[1].s3()
    m_in[4].s6()
    m_in[5].s6()

    second_norm_back()
    early.run(0)
    o_in.s6()
    out_projection_back()
    o_sum.s1()
    m_sum[2].s3()
    m_sum[0].s5()
    m_sum[0].give_credit()
    pair_attention_back()
    pair_weight_grads()
    m_sum[2].s4()
    o_sum.s3()
    m_sum[0].take_credit()
    qa_sum.s1()
    qd_sum.s1()
    odd_attention_back()
    odd_weight_grads()
    qb_sum.s1()
    qc_sum.s1()
    m_sum[2].s5()
    for g in q_in:
        g.s6()
    give(2).start()
    give(3).start()
    first_norm_back()
    late.run(0)
    early_take_1()
    o_sum.s5()
    give(1).start()
    qb_sum.s4()
    qc_sum.s4()
    late.take(0)
    late.run(1)
    qa_sum.s5()
    qd_sum.s5()
    late.take(1)
    late.left()
    small_results()
    give(4).start()
    qb_sum.s5()
    for one in store_low():
        one.wait()
    store_grad().wait()
    qc_sum.s5()
    give(0).start()
    for k in range(5):
        give(k).wait()


def scatter_slots(rows, columns):
    return [
        pltpu.VMEM((2, 4, 2, rows, columns), BF),
        pltpu.VMEM((4, (rows // 2 + 15) // 16 * 16, columns), BF),
        pltpu.VMEM((4, rows // 2, columns), BF),
        pltpu.VMEM((4, rows, columns), BF),
        pltpu.VMEM((4, rows, columns), BF),
        pltpu.VMEM((3, rows, columns), BF),
    ]


def layer(inner, tokens, cotangent, segments, valid, wq, wo, up, down, *params):
    length, width = tokens.shape
    block = lambda rows, columns: pltpu.VMEM((2, 2, 4, 2, rows, columns), BF)
    small = (8, width) if inner > 1 else (8, 128)
    shapes = [(3, 96, 3 * HD), (3 * HD, 96), (96, width), (96, width), small]
    scratch = [pltpu.VMEM(shape, F32) for shape in shapes]
    scratch += [
        block(96, 640), block(144, 128), block(192, 256), block(192, 256), block(192, 256), block(192, 256),
        pltpu.VMEM((length, width), BF),
        pltpu.VMEM((length, width), BF),
        pltpu.VMEM((length, width), BF),
        pltpu.VMEM((4, length, 640), BF),
        pltpu.VMEM((4, length, 256), BF),
        pltpu.VMEM((4, length, 128), BF),
        pltpu.VMEM((length, 128), BF),
        pltpu.VMEM((length, 128), BF),
        pltpu.VMEM((128, length), BF),
        pltpu.VMEM((4, width, 128), BF),
        pltpu.VMEM((length, width), F32),
        pltpu.VMEM((length, width), BF),
        pltpu.VMEM((length, width), F32),
        pltpu.VMEM((length, width), F32),
        pltpu.VMEM((4, length, 256), BF),
        pltpu.VMEM((4, length, 256), BF),
        pltpu.VMEM((length, 1), F32),
        pltpu.VMEM((128, width), F32),
    ]
    scratch += [pltpu.VMEM((length, 128), F32)] * 2
    scratch += [scatter_slots(192, 256) * 3, scatter_slots(144, 256)]
    scratch += [
        pltpu.VMEM((3, 8, width), F32),
        pltpu.VMEM((10, 8, width), F32),
        pltpu.VMEM((3, 16, 128), F32),
        pltpu.VMEM((10, 16, 128), F32),
        pltpu.VMEM((8, width), F32),
        pltpu.SemaphoreType.DMA((10, 3)),
        pltpu.SemaphoreType.DMA((10, 6)),
        pltpu.SemaphoreType.DMA((8, 3)),
        pltpu.SemaphoreType.DMA((8, 5)),
        pltpu.SemaphoreType.REGULAR((1, 6)),
        pltpu.SemaphoreType.DMA((2, 2)),
        pltpu.SemaphoreType.DMA((2, 2)),
        pltpu.SemaphoreType.DMA((5,)),
        pltpu.SemaphoreType.DMA((8,)),
        pltpu.SemaphoreType.DMA((5,)),
    ]
    vmem, anywhere = pl.BlockSpec(memory_space=pltpu.VMEM), pl.BlockSpec(memory_space=pl.ANY)
    return pl.pallas_call(
        partial(kernel, inner, length),
        out_shape=[
            jax.ShapeDtypeStruct((length, width), BF),
            jax.ShapeDtypeStruct((length, width), F32),
        ]
        + [jax.ShapeDtypeStruct(shape, F32) for shape in shapes],
        in_specs=[anywhere, anywhere, vmem, vmem, vmem, vmem, anywhere, anywhere] + [vmem] * 4,
        out_specs=[anywhere] * (2 + len(shapes)),
        scratch_shapes=scratch,
        compiler_params=pltpu.CompilerParams(
            collective_id=0, has_side_effects=True, vmem_limit_bytes=63 * 2**20
        ),
    )(tokens, cotangent, segments, valid, wq, wo, up, down, *params)


def hand_over(arrays, share):
    count = len(arrays)
    pieces = []
    for k, a in enumerate(arrays):
        step = 256 if a.ndim == 2 and a.shape[0] % 256 == 0 else a.shape[0]
        pieces += [(k, start, step) for start in range(0, a.shape[0], step)]
    small = [(share,)] * 4 + [(3,)] if share else []
    shapes = [(a.shape, a.dtype) for a in arrays[: count - 1 if small else count]] + [(cut, F32) for cut in small]
    whole = len(shapes) - len(small)

    def body(*refs):
        came, went = refs[:count], refs[count : count + len(shapes)]
        held = refs[count + len(shapes) : 2 * count + len(shapes)]
        cuts, sems = refs[2 * count + len(shapes) : -1], refs[-1]

        def part(ref, n):
            _, start, step = pieces[n]
            return ref.at[pl.ds(start, step)] if step < ref.shape[0] else ref

        def fetch(n):
            k = pieces[n][0]
            return pltpu.make_async_copy(part(came[k], n), part(held[k], n), sems.at[0, n])

        def put(n):
            k = pieces[n][0]
            return pltpu.make_async_copy(part(held[k], n), part(went[k], n), sems.at[1, n])

        def put_cut(k):
            return pltpu.make_async_copy(cuts[k], went[whole + k], sems.at[1, len(pieces) + k])

        for n in reversed(range(len(pieces))):
            fetch(n).start()
        for n in reversed(range(len(pieces))):
            fetch(n).wait()
            if pieces[n][0] < whole:
                put(n).start()
                continue
            for k, cut in enumerate(small):
                cuts[k][...] = held[whole][k, 0 : cut[0]]
                put_cut(k).start()
        for n in range(len(pieces)):
            if pieces[n][0] < whole:
                put(n).wait()
        for k in range(len(small)):
            put_cut(k).wait()

    anywhere = pl.BlockSpec(memory_space=pltpu.HBM)
    return pl.pallas_call(
        body,
        out_shape=[jax.ShapeDtypeStruct(shape, dtype) for shape, dtype in shapes],
        in_specs=[anywhere] * count,
        out_specs=[anywhere] * len(shapes),
        scratch_shapes=[pltpu.VMEM(a.shape, a.dtype) for a in arrays]
        + [pltpu.VMEM(cut, F32) for cut in small]
        + [pltpu.SemaphoreType.DMA((2, len(pieces) + 5))],
        compiler_params=pltpu.CompilerParams(vmem_limit_bytes=63 * 2**20),
    )(*arrays)


def local(
    tokens, segment_ids, valid, ln1_gain, ln1_bias, w_qkv, w_out, ln2_gain, ln2_bias, w_up, w_down, cotangent
):
    length, width = tokens.shape
    holders = lax.axis_size("fsdp")
    inner = holders // 8
    groups = [[g * inner + i for i in range(inner)] for g in range(8)]

    def widen(block, axis=0):
        if inner == 1:
            return block
        return lax.all_gather(block, "fsdp", axis_index_groups=groups, axis=axis, tiled=True)

    def narrow(block, axis=0):
        if inner == 1:
            return block
        return lax.psum_scatter(
            block, "fsdp", scatter_dimension=axis, axis_index_groups=groups, tiled=True
        )

    params = [widen(one.reshape(1, -1), 1) for one in (ln1_gain, ln1_bias, ln2_gain, ln2_bias)]
    results = layer(
        inner, tokens, cotangent, segment_ids, valid.reshape(1, length),
        widen(w_qkv.transpose(1, 0, 2), 1), widen(w_out, 1), widen(w_up), widen(w_down.T), *params,
    )
    low, grad_tokens, gq, go, gup, gdown, *small = hand_over(results, width // 32 if inner == 1 else 0)
    if inner > 1:
        sums = lax.psum(small[0], "fsdp", axis_index_groups=groups)
        share = width // (holders * lax.axis_size("tp"))
        owner = lax.axis_index("fsdp") * lax.axis_size("tp") + lax.axis_index("tp")
        mine = lax.dynamic_slice_in_dim(sums[0:4], owner * share, share, 1)
        spread = jnp.sqrt(jnp.sum(sums[4:7], axis=1) / (sums[7, 0] * width))
        small = (mine[0], mine[1], mine[2], mine[3], spread)
    return (
        low, grad_tokens, small[0], small[1], narrow(gq, 1).transpose(1, 0, 2), narrow(go, 1),
        small[2], small[3], narrow(gup), narrow(gdown).T, small[4],
    )


def solution(mesh):
    both = ("fsdp", "tp")
    return jax.shard_map(
        local,
        mesh=mesh,
        in_specs=(
            P(both, None), P("fsdp", None), P(both), P("fsdp"), P("fsdp"), P("fsdp", None, "tp"),
            P("tp", "fsdp"), P("fsdp"), P("fsdp"), P("fsdp", "tp"), P("tp", "fsdp"), P(both, None),
        ),
        out_specs=(
            P(both, None), P(both, None), P(both), P(both), P("fsdp", None, "tp"), P("tp", "fsdp"),
            P(both), P(both), P("fsdp", "tp"), P("tp", "fsdp"), P(),
        ),
        check_vma=False,
    )
```

```python
from functools import partial

import jax
import jax.numpy as jnp
from jax import lax
from jax.experimental import pallas as pl
from jax.experimental.pallas import tpu as pltpu
from jax.sharding import PartitionSpec as P

HD = 64
BQ = 256
EPS = 1e-05
BIG = -1e30
F32 = jnp.float32
BF = jnp.bfloat16
NN = (((1,), (0,)), ((), ()))
NT = (((1,), (1,)), ((), ()))
TN = (((0,), (0,)), ((), ()))
MESH = pl.DeviceIdType.MESH
C0 = 0.7978845608
C1 = 0.7978845608 * 0.044715


def dot(a, b, dims=NN):
    return lax.dot_general(a, b, dims, preferred_element_type=F32)


def phase(body):
    return body


def remote(src, dst, send, recv, device):
    return pltpu.make_async_remote_copy(
        src_ref=src, dst_ref=dst, send_sem=send, recv_sem=recv,
        device_id=device, device_id_type=MESH,
    )


class Place:
    def __init__(self, inner):
        f = lax.axis_index("fsdp")
        t = lax.axis_index("tp")
        g = f // inner
        self.low = f % inner
        self.inner = inner
        self.z, self.y, self.x, self.c = g // 2, g % 2, t // 2, t % 2

    def device(self, z, y, x, c):
        return ((z * 2 + y) * self.inner + self.low, x * 2 + c)

    def core(self):
        return self.device(self.z, self.y, self.x, 1 - self.c)

    def xn(self):
        return self.device(self.z, self.y, 1 - self.x, self.c)

    def yn(self):
        return self.device(self.z, 1 - self.y, self.x, self.c)

    def cube(self, n):
        y, x, c = (self.y + n // 4) % 2, (self.x + n // 2) % 2, (self.c + n) % 2
        return self.device(self.z, y, x, c)

    def zn(self, d):
        return self.device((self.z + d) % 4, self.y, self.x, self.c)

    def reach(self, k):
        upper = self.z // 2
        return (3 - k) * (1 - upper) + (1 + k) * upper

    def zp(self, d):
        return self.device((self.z - d + 4) % 4, self.y, self.x, self.c)


def greet(inner):
    p = Place(inner)
    sem = pltpu.get_barrier_semaphore()
    for dev in [p.cube(n) for n in range(1, 8)] + [p.zn(d) for d in range(1, 4)]:
        pl.semaphore_signal(sem, inc=1, device_id=dev, device_id_type=MESH)


def met(inner):
    pl.semaphore_wait(pltpu.get_barrier_semaphore(), 10)


class Gather:
    def __init__(self, name, inner, buf, row0, rows, send, recv):
        self.name = name
        self.inner, self.buf, self.row0, self.rows = inner, buf, row0, rows
        self.send, self.recv = send, recv

    def own(self, x, c, z, y):
        return self.buf.at[x, c, z, y, pl.ds(self.row0, self.rows)]

    def group(self, x, c, y, half=None):
        start, size = self.row0, self.rows
        if half is not None:
            cut = (size // 2 + 15) // 16 * 16
            start, size = (start + cut, size - cut) if half else (start, cut)
        return self.buf.at[x, c, :, y, pl.ds(start, size)]

    def parts(self, slot):
        p = Place(self.inner)
        x, c, z, y = p.x, p.c, p.z, p.y
        if slot < 3:
            mine = self.own(x, c, z, y)
            return mine, mine, p.zn(p.reach(slot))
        if slot == 3:
            return self.group(x, c, y), self.group(1 - x, c, y), p.xn()
        if slot == 4:
            return self.group(x, c, y), self.group(x, c, 1 - y), p.yn()
        if slot == 5:
            return self.group(1 - x, c, y, 0), self.group(1 - x, c, 1 - y, 0), p.yn()
        if slot == 6:
            return self.group(x, c, 1 - y, 1), self.group(1 - x, c, 1 - y, 1), p.xn()
        xx = x if slot in (7, 9) else 1 - x
        yy = y if slot in (7, 8) else 1 - y
        return self.group(xx, c, yy), self.group(xx, 1 - c, yy), p.core()

    SENT = (0, 0, 0, 1, 1, 2, 2, 1, 2, 2, 2)
    CAME = (0, 0, 0, 1, 2, 3, 3, 4, 5, 4, 5)

    def start(self, *slots):
        for slot in slots:
            mine, _, dev = self.parts(slot)
            remote(mine, mine, self.send.at[self.SENT[slot]], self.recv.at[self.CAME[slot]], dev).start()

    def bytes_of(self, blocks):
        rows = pl.ds(self.row0, self.rows)
        if blocks == 3:
            return self.buf.at[0, 0, 0:3, 0, rows]
        if blocks == 4:
            return self.buf.at[0, 0, :, 0, rows]
        if blocks == 8:
            return self.buf.at[0, 0, :, :, rows]
        if blocks == 12:
            return self.buf.at[:, :, 0:3, 0, rows]
        return self.buf.at[0, :, :, :, rows]

    def arrive(self, group):
        ref = self.bytes_of((3, 4, 4, 4, 8, 8)[group])
        dev = Place(self.inner).core()
        remote(ref, ref, self.send.at[0], self.recv.at[group], dev).wait_recv()

    def left(self):
        for group, blocks in enumerate((3, 12, 16)):
            ref = self.bytes_of(blocks)
            dev = Place(self.inner).core()
            remote(ref, ref, self.send.at[group], self.recv.at[0], dev).wait_send()

    def s1(self):
        self.start(0, 1, 2)

    def s2(self):
        self.arrive(0)
        self.start(3, 4, 7)

    def s3(self):
        self.arrive(2)
        self.start(6, 9)
        self.arrive(1)
        self.start(5, 8)

    def s4(self):
        self.arrive(3)
        self.start(10)

    def near(self):
        self.arrive(4)

    def far(self):
        self.arrive(5)

    def s5(self):
        self.near()
        self.far()

    def s6(self):
        self.left()


class Scatter:
    def __init__(self, name, inner, buf, block, slots, place, send, recv, credit, out):
        self.name = name
        self.inner, self.buf, self.slots = inner, buf, slots
        self.row0, self.rows, self.col0, columns = block
        self.half = (self.rows // 2 + 15) // 16 * 16
        row, upper, lower, col = place
        self.land = (
            slice(row, row + self.rows), slice(upper, upper + self.half),
            slice(lower, lower + self.rows - self.half), slice(col, col + columns),
        )
        self.cols = slice(self.col0, self.col0 + columns)
        self.send, self.recv = send, recv
        self.credit, self.out = credit, out

    def parts(self, slot):
        p = Place(self.inner)
        x, c, z, y = p.x, p.c, p.z, p.y
        buf, cols = self.buf, self.cols
        r1, ra, rb, rx, ry, rz = self.slots
        rows, upper, lower = self.spans()
        land, land_a, land_b, land_cols = self.land
        if slot == 0:
            return buf.at[:, 1 - c, :, :, rows, cols], r1.at[:, :, :, land, land_cols], p.core()
        if slot == 1:
            return buf.at[1 - x, c, :, 1 - y, upper, cols], ra.at[:, land_a, land_cols], p.yn()
        if slot == 2:
            return buf.at[1 - x, c, :, 1 - y, lower, cols], rb.at[:, land_b, land_cols], p.xn()
        if slot == 3:
            return buf.at[1 - x, c, :, y, rows, cols], rx.at[:, land, land_cols], p.xn()
        if slot == 4:
            return buf.at[x, c, :, 1 - y, rows, cols], ry.at[:, land, land_cols], p.yn()
        d = p.reach(slot - 5)
        return buf.at[x, c, (z + d) % 4, y, rows, cols], rz.at[d - 1, land, land_cols], p.zn(d)

    def spans(self):
        start, end = self.row0, self.row0 + self.rows
        return slice(start, end), slice(start, start + self.half), slice(start + self.half, end)

    SENT = (0, 1, 1, 1, 1, 2, 2, 2)
    CAME = (0, 1, 2, 3, 3, 4, 4, 4)

    def start(self, *slots):
        for slot in slots:
            src, dst, dev = self.parts(slot)
            remote(src, dst, self.send.at[self.SENT[slot]], self.recv.at[self.CAME[slot]], dev).start()

    def arrive(self, group):
        land, _, _, cols = self.land
        if group < 3:
            ref = self.parts(group)[1]
        elif group == 3:
            ref = self.slots[0].at[0, :, :, land, cols]
        else:
            ref = self.slots[5].at[:, land, cols]
        remote(ref, ref, self.send.at[0], self.recv.at[group], Place(self.inner).core()).wait_recv()

    def left(self):
        rows, cols = self.spans()[0], self.cols
        refs = (
            self.buf.at[:, 0, :, :, rows, cols], self.buf.at[:, :, 0:3, 0, rows, cols],
            self.buf.at[0, 0, 0:3, 0, rows, cols],
        )
        for group, ref in enumerate(refs):
            dev = Place(self.inner).core()
            remote(ref, ref, self.send.at[group], self.recv.at[0], dev).wait_send()

    def take_credit(self):
        for i in range(6):
            pl.semaphore_wait(self.credit.at[i], 1)

    def give_credit(self):
        p = Place(self.inner)
        for i, dev in enumerate((p.core(), p.xn(), p.yn(), p.zp(1), p.zp(2), p.zp(3))):
            pl.semaphore_signal(self.credit.at[i], inc=1, device_id=dev, device_id_type=MESH)

    def s1(self):
        self.start(0)

    def add(self, x, y, rows, *others):
        c = Place(self.inner).c

        @pl.loop(0, 4)
        def _(z):
            total = self.buf[x, c, z, y, rows, self.cols]
            if len(others) > 1:
                total = total.astype(F32)
            for other in others:
                total = total + other(z).astype(total.dtype)
            self.buf[x, c, z, y, rows, self.cols] = total.astype(BF)

    def s2(self):
        p = Place(self.inner)
        r1, (land, _, _, cols) = self.slots[0], self.land
        self.arrive(0)
        for x, y in ((1 - p.x, 1 - p.y), (1 - p.x, p.y), (p.x, 1 - p.y), (p.x, p.y)):
            self.add(x, y, self.spans()[0], lambda z: r1[x, z, y, land, cols])
            if x is not p.x and y is not p.y:
                self.start(1, 2)

    def s3(self):
        p = Place(self.inner)
        _, upper, lower = self.spans()
        _, land_a, land_b, cols = self.land
        ra, rb = self.slots[1:3]
        self.arrive(1)
        self.add(1 - p.x, p.y, upper, lambda z: ra[z, land_a, cols])
        self.start(3)
        self.arrive(2)
        self.add(p.x, 1 - p.y, lower, lambda z: rb[z, land_b, cols])
        self.start(4)

    def s4(self):
        p = Place(self.inner)
        land, _, _, cols = self.land
        rx, ry = self.slots[3:5]
        self.arrive(3)
        self.add(p.x, p.y, self.spans()[0], lambda z: rx[z, land, cols], lambda z: ry[z, land, cols])
        self.start(5, 6, 7)

    def s5(self):
        p = Place(self.inner)
        land, _, _, cols = self.land
        rz = self.slots[5]
        self.arrive(4)
        total = self.buf[p.x, p.c, p.z, p.y, self.spans()[0], self.cols].astype(F32)
        for d in range(3):
            total = total + rz[d, land, cols].astype(F32)
        self.out(total)
        self.left()


class Total:
    def __init__(self, name, inner, ref, got, send, recv):
        self.name = name
        self.inner, self.ref, self.got, self.send, self.recv = inner, ref, got, send, recv

    def copy(self, slot):
        p = Place(self.inner)
        dev = p.cube(slot + 1) if slot < 7 else p.zn(slot - 6)
        stage = 0 if slot < 7 else 1
        return remote(self.ref.at[stage], self.got.at[slot], self.send.at[stage], self.recv.at[stage], dev)

    def slots(self, stage):
        return range(7) if stage == 0 else range(7, 10)

    def all_of(self, stage):
        span = self.slots(stage)
        ref = self.got.at[span.start : span.stop]
        return remote(ref, ref, self.send.at[stage], self.recv.at[stage], Place(self.inner).core())

    def run(self, stage):
        for slot in self.slots(stage):
            self.copy(slot).start()

    def take(self, stage):
        self.all_of(stage).wait_recv()
        total = self.ref[stage]
        for slot in self.slots(stage):
            total = total + self.got[slot]
        self.ref[stage + 1] = total

    def left(self):
        for stage in range(2):
            self.all_of(stage).wait_send()


def head_parts(t_ref, k2_ref, t, h, qs, kr):
    if h < 2:
        return t_ref[t, qs, 0:128], t_ref[t, kr, 128:256], t_ref[t, kr, 256:384]
    return t_ref[t, qs, 384:512], k2_ref[kr, :], t_ref[t, kr, 512:640]


def lanes():
    return lax.broadcasted_iota(jnp.int32, (1, 128), 1)


def roll_key(t_ref, k2_ref, t):
    k2_ref[...] = pltpu.roll(t_ref[t, :, 384:512].astype(F32), 64, 1).astype(BF)


def below(transposed, size=BQ):
    r = lax.broadcasted_iota(jnp.int32, (size, size), 0)
    c = lax.broadcasted_iota(jnp.int32, (size, size), 1)
    return r <= c if transposed else r >= c


def attend(t_ref, l_ref, kx_ref, k2_ref, c_ref, t, length):
    lane = lanes()
    low = lane < 64
    roll_key(t_ref, k2_ref, t)
    for i in range(length // BQ):
        first = max(0, i * BQ - length // 2)
        width = (i + 1) * BQ - first
        qs, kr = slice(i * BQ, (i + 1) * BQ), slice(first, first + width)
        kx = kx_ref[kr, :]
        doc = kx_ref[qs, :].astype(F32)
        qx = jnp.where(lane < 8, BIG * (1.0 - doc), 0.0).astype(BF)
        marks = qx
        outs = []
        for h in range(3):
            q, k, v = head_parts(t_ref, k2_ref, t, h, qs, kr)
            keep = jnp.logical_not(low) if h == 1 else low
            q = jnp.where(keep, q * BF(HD ** -0.5), BF(0))
            s = dot(jnp.concatenate([q, qx], 1), jnp.concatenate([k, kx], 1), NT)
            edge = jnp.where(below(False), s[:, width - BQ :], BIG)
            s = edge if width == BQ else jnp.concatenate([s[:, : width - BQ], edge], 1)
            top = jnp.max(s, axis=1, keepdims=True)
            p = jnp.exp(s - top).astype(BF)
            both = dot(p, jnp.concatenate([v, jnp.ones((width, 128), BF)], 1))
            total = both[:, 128:256]
            outs.append(both[:, :128] / total)
            rest = -(top + jnp.log(total))
            for n in range(3):
                piece = rest.astype(BF)
                marks = jnp.where(lane == 8 + 16 * h + n, piece, marks)
                rest = rest - piece.astype(F32)
        l_ref[t, qs, :] = marks
        c_ref[t, qs, 0:128] = jnp.where(low, outs[0], outs[1]).astype(BF)
        c_ref[t, qs, 128:256] = jnp.where(low, outs[2], 0.0).astype(BF)


def attend_back(t_ref, l_ref, kx_ref, k2_ref, kt_ref, c_ref, do_ref, sums, heads, t, length):
    lane = lanes()
    low = lane < 64
    dk_ref, dv_ref = sums
    odd = heads == (2,)
    size = BQ
    if odd:
        roll_key(t_ref, k2_ref, t)
        kt_ref[...] = k2_ref[...].T
    else:
        kt_ref[...] = t_ref[t, :, 128:256].T
    for ref in sums:
        ref[...] = jnp.zeros_like(ref)
    for i in range(length // size):
        first = max(0, i * size - length // 2)
        width = (i + 1) * size - first
        qs, kr = slice(i * size, (i + 1) * size), slice(first, first + width)
        marks = l_ref[t, qs, :]
        side = slice(128, 256) if odd else slice(0, 128)
        qs_all, dos, left, right = [], [], [], []
        for h in heads:
            q, k, v = head_parts(t_ref, k2_ref, t, h, qs, kr)
            keep = jnp.logical_not(low) if h == 1 else low
            q = jnp.where(keep, q * BF(HD ** -0.5), BF(0))
            do = jnp.where(keep, do_ref[t, qs, side], BF(0))
            dd = (do.astype(F32) * c_ref[t, qs, side].astype(F32)).astype(BF)
            mine = (lane < 8) | ((lane >= 8 + 16 * h) & (lane < 24 + 16 * h))
            qs_all.append(q)
            dos.append(do)
            left.append(jnp.concatenate([q, jnp.where(mine, marks, BF(0))], 1))
            right.append(jnp.concatenate([do, dd], 1))
        s_all = dot(jnp.concatenate([k, kx_ref[kr, :]], 1), jnp.concatenate(left, 0), NT)
        minus = jnp.full((width, 128), -1.0, BF)
        dp_all = dot(jnp.concatenate([v, minus], 1), jnp.concatenate(right, 0), NT)
        ps, dss, grads = [], [], []
        for n in range(len(heads)):
            s = s_all[:, n * size : (n + 1) * size]
            edge = jnp.where(below(True, size), s[width - size :], BIG)
            s = edge if width == size else jnp.concatenate([s[: width - size], edge], 0)
            p = jnp.exp(s)
            ds = (p * dp_all[:, n * size : (n + 1) * size]).astype(BF)
            ps.append(p.astype(BF))
            dss.append(ds)
            grads.append(dot(kt_ref[64 * n : 64 * n + 64, kr], ds))
        if odd:
            grads.append(jnp.zeros((64, size), F32))
        grad = (jnp.concatenate(grads, 0).T * HD ** -0.5).astype(BF)
        dv_ref[kr, :] += dot(jnp.concatenate(ps, 1), jnp.concatenate(dos, 0))
        dk_ref[kr, :] += dot(jnp.concatenate(dss, 1), jnp.concatenate(qs_all, 0))
        if odd:
            t_ref[t, qs, 384:512] = jnp.where(low, grad, t_ref[t, qs, 384:512])
        else:
            t_ref[t, qs, 0:128] = grad
    if odd:
        moved = pltpu.roll(dk_ref[...], 64, 1).astype(BF)
        t_ref[t, :, 384:512] = jnp.where(low, t_ref[t, :, 384:512], moved)
        t_ref[t, :, 512:640] = dv_ref[...].astype(BF)
    else:
        t_ref[t, :, 128:256] = dk_ref[...].astype(BF)
        t_ref[t, :, 256:384] = dv_ref[...].astype(BF)


def stats(v):
    mean = jnp.mean(v, axis=-1, keepdims=True)
    center = v - mean
    scale = lax.rsqrt(jnp.mean(center * center, axis=-1, keepdims=True) + EPS)
    return center * scale, mean, scale


def norm_back(v, mean, scale, q, gain):
    n = (v - mean) * scale
    e = q * gain
    back = scale * (e - jnp.mean(e, -1, keepdims=True) - n * jnp.mean(e * n, -1, keepdims=True))
    return back, jnp.sum(q * n, 0, keepdims=True), jnp.sum(q, 0, keepdims=True)


def kernel(
    inner, length,
    tok_in, cot_in, seg, valid, wq_in, wo_in, up_in, down_in, par_a, par_b, par_c, par_d,
    lo_out, gt_out, *rest,
):
    big_outs = rest[0:5]
    (
        gq_out, go_out, gup_out, gdown_out, small_out,
        bq, bo, bm0, bm1, bm2, gb,
        tok, cot, n1, tt, cc, ll, kx, k2, kt, wo, mid, n2, acc, gn, act, gu, val, kept, par,
        dk, dv,
        m_sets, o_set, ar, ar_got, br, br_got, g1,
        ag_send, ag_recv, rs_send, rs_recv, credit, ar_send, ar_recv, local_sem, own_sem, give_sem,
    ) = rest[5:]
    width = tok.shape[1]
    bm = (bm0, bm1, bm2)
    blocks = [(bq, 0, 32), (bq, 32, 32), (bq, 64, 32), (bo, 0, 144)]
    blocks += [(b, r0, 96) for b in bm for r0 in (0, 96)]
    gathers = [
        Gather(f"gather{k}", inner, b, r0, rows, ag_send.at[k], ag_recv.at[k])
        for k, (b, r0, rows) in enumerate(blocks)
    ]
    here = Place(inner)
    mine = (here.x, here.c, here.z, here.y)

    def put_mlp(j):
        def put(total):
            gup_out[:, 256 * j : 256 * j + 256] = total[0:96]
            gdown_out[:, 256 * j : 256 * j + 256] = total[96:192]

        return put

    def put_out(total):
        go_out[0 : 2 * HD] = total[0:96].T
        third = total[96:144].T
        go_out[2 * HD : 3 * HD] = jnp.concatenate([third[0:64], third[64:128]], 1)

    def put_pair(total):
        gq_out[0, 0:80, 0:128] = total[:, 0:128]
        gq_out[1, 0:80, 0:128] = total[:, 128:256]

    def put_pair_rest(total):
        gq_out[0, 80:96, 0:128] = total[0:16, 0:128]
        gq_out[1, 80:96, 0:128] = total[0:16, 128:256]
        gq_out[2, 0:48, 0:128] = total[16:64, 0:128]
        gq_out[2, 48:96, 0:128] = total[16:64, 128:256]

    def put_odd(total):
        gq_out[0, 0:80, 128:192] = total[:, 0:64]
        gq_out[1, 0:80, 128:192] = total[:, 64:128]

    def put_rest(total):
        gq_out[0, 80:96, 128:192] = total[0:16, 0:64]
        gq_out[1, 80:96, 128:192] = total[0:16, 64:128]
        gq_out[2, 0:48, 128:192] = total[16:64, 0:64]
        gq_out[2, 48:96, 128:192] = total[16:64, 64:128]

    grads = (gb, bm0, bm1)
    sets = [m_sets[0:6], m_sets[6:12], m_sets[12:18]]
    start = (0, 0, 0, 0)
    plan = [
        (gb, (0, 192, 0, 256), sets[0], start, put_mlp(0)),
        (bm0, (0, 192, 0, 256), sets[1], start, put_mlp(1)),
        (bm1, (0, 192, 0, 256), sets[2], start, put_mlp(2)),
        (bm2, (0, 144, 0, 128), o_set, start, put_out),
        (gb, (0, 80, 0, 256), sets[0], start, put_pair),
        (gb, (80, 64, 0, 256), sets[0], (80, 48, 32, 0), put_pair_rest),
        (bm2, (0, 80, 128, 128), o_set, (0, 0, 0, 128), put_odd),
        (bm2, (80, 64, 128, 128), o_set, (80, 48, 32, 128), put_rest),
    ]
    scatters = [
        Scatter(
            f"scatter{k}", inner, b, block, slots, place,
            rs_send.at[k], rs_recv.at[k], credit.at[0], out,
        )
        for k, (b, block, slots, place, out) in enumerate(plan)
    ]
    m_sum, o_sum, qa_sum, qd_sum, qb_sum, qc_sum = scatters[0:3], *scatters[3:8]
    q_in, o_in, m_in = gathers[0:3], gathers[3], gathers[4:10]
    early = Total("early", inner, ar, ar_got, ar_send.at[0], ar_recv.at[0])
    late = Total("late", inner, br, br_got, ar_send.at[1], ar_recv.at[1])

    def after(t, last, *steps):
        @pl.when(t == last)
        def _():
            for step in steps:
                step()

    def rows_of(i, size):
        return pl.ds(pl.multiple_of(i * size, size), size)

    def weight(buf, t, r0, rows, columns):
        return buf[t // 2, t % 2, :, :, r0 : r0 + rows, columns].reshape(8 * rows, -1)

    def fold(columns):
        parts = columns.reshape(8, 96, 64)
        halves = [parts[:, 48 * n : 48 * n + 48].reshape(8 * 48, 64) for n in range(2)]
        return jnp.concatenate(halves, 1).astype(BF).reshape(4, 2, 48, 128)

    def cat(ref, s):
        return jnp.concatenate([ref[t, s, :] for t in range(4)], 1)

    def own_copies():
        copies = []
        for j in range(3):
            cols = pl.ds(256 * j, 256)
            copies.append((up_in.at[:, cols], bm[j].at[(*mine, pl.ds(0, 96))]))
            copies.append((down_in.at[:, cols], bm[j].at[(*mine, pl.ds(96, 96))]))
        copies += [(tok_in, tok), (cot_in, cot)]
        return [pltpu.make_async_copy(src, dst, own_sem.at[k]) for k, (src, dst) in enumerate(copies)]

    @phase
    def entry():
        for one in own_copies():
            one.start()
        greet(inner)
        q, k, v = (wq_in[n] for n in range(3))
        for n, one in enumerate((q, k, v)):
            bq[(*mine, slice(None), slice(128 * n, 128 * n + 128))] = one[:, 0:128]
        odd = [one[:, 128:192].astype(F32) for one in (q, k, v)]
        bq[(*mine, slice(None), slice(384, 512))] = jnp.concatenate(odd[0:2], 1).astype(BF)
        params = jnp.concatenate([one[...].astype(F32) for one in (par_a, par_b, par_c, par_d)] + [jnp.zeros((124, 96), F32)], 0).T[:, 0:64]
        bq[(*mine, slice(None), slice(512, 640))] = jnp.concatenate([odd[2], params], 1).astype(BF)
        met(inner)

    @phase
    def document_marks():
        me_t = lax.axis_index("tp")
        row = seg[pl.ds(me_t, 1), :].astype(F32)
        lane_id = lax.broadcasted_iota(jnp.int32, (128, length), 0)
        marks = jnp.where(row == lane_id.astype(F32), 1.0, 0.0)
        marks = jnp.where(lane_id < 8, marks, 0.0)
        low4 = lane_id % 16
        ones = (lane_id >= 8) & (lane_id < 56) & (low4 >= 8) & (low4 < 11)
        marks = jnp.where(ones, 1.0, marks)
        marks = jnp.where(lane_id == 64, valid[...].astype(F32), marks)
        columns = marks.T
        val[...] = columns[:, 64:65]
        kx[...] = jnp.where(lanes() < 64, columns, 0.0).astype(BF)
        ar[0] = jnp.zeros_like(ar.at[0])
        br[0] = jnp.zeros_like(br.at[0])
        g1[...] = jnp.zeros_like(g1)
        count = jnp.sum(valid[...].astype(F32), axis=1, keepdims=True)
        ar[0, 7:8, 0:128] = jnp.broadcast_to(count, (1, 128))
        wide = jnp.concatenate([wo_in[...].astype(F32), jnp.zeros((64, 96), F32)], 0).T
        third = wide[:, 128:192]
        bo[(*mine, slice(0, 96))] = wide[:, 0:128].astype(BF)
        bo[(*mine, slice(96, 144))] = jnp.concatenate([third[0:48], third[48:96]], 1).astype(BF)

    @phase
    def first_norm_statistics():
        @pl.loop(0, length // 256)
        def _(i):
            s = rows_of(i, 256)
            n, mean, scale = stats(tok[s, :].astype(F32))
            mid[s, :] = n
            kept[s, 0:1] = mean
            kept[s, 1:2] = scale

    @phase
    def first_norm():
        par[...] = bq[here.x, here.c, :, :, :, 512:640].reshape(width, 128).astype(F32).T

        @pl.loop(0, length // 256)
        def _(i):
            s = rows_of(i, 256)
            n1[s, :] = (mid[s, :] * par[64:65, :] + par[65:66, :]).astype(BF)

    @phase
    def attention():
        @pl.loop(0, 4)
        def _(n):
            x, c = (here.x + n // 2) % 2, (here.c + n % 2) % 2
            t = 2 * x + c
            w = bq[x, c].reshape(width, 640)

            @pl.loop(0, length // 512)
            def _(i):
                s = rows_of(i, 512)
                tt[t, s, :] = dot(n1[s, :], w).astype(BF)

            after(n, 1, m_in[1].s2, m_in[2].s1)
            after(n, 3, m_in[1].s3, m_in[2].s2, m_in[5].s1)
            attend(tt, ll, kx, k2, cc, t, length)
            after(n, 0, *[g.s4 for g in q_in], *[g.near for g in q_in], m_in[0].s2)
            after(n, 1, o_in.s3, m_in[3].s1)
            after(n, 2, m_in[0].s3, *[g.far for g in q_in], m_in[4].s1)
            after(n, 3, o_in.s4, m_in[3].s2, m_in[0].s4, o_in.s5)

    def out_weight(t):
        return jnp.concatenate([weight(bo, t, 0, 96, slice(0, 128)), wo[t]], 1)

    @phase
    def out_projection():
        for t in range(4):
            third = bo[t // 2, t % 2, :, :, 96:144, :].reshape(8, 48, 128)
            turned = pltpu.roll(third.astype(F32).reshape(8 * 48, 128), 64, 1).astype(BF)
            wo[t] = jnp.concatenate([third, turned.reshape(8, 48, 128)], 1).reshape(width, 128)

        @pl.loop(0, length // 256)
        def _(i):
            s = rows_of(i, 256)
            branch = jnp.zeros((256, width), F32)
            for t in range(4):
                branch = branch + dot(cc[t, s, :], out_weight(t), NT)
            v = tok[s, :].astype(F32) + branch
            mid[s, :] = v
            ar[0, 5:6, :] += jnp.sum(val[s, :] * (branch * branch), 0, keepdims=True)
            n, mean, scale = stats(v)
            kept[s, 2:3] = mean
            kept[s, 3:4] = scale
            n2[s, :] = (n * par[66:67, :] + par[67:68, :]).astype(BF)

    def mlp_hidden(j, *steps):
        b = bm[j]

        @phase
        def hidden():
            @pl.loop(0, 4)
            def _(t):
                up = weight(b, t, 0, 96, slice(0, 256))
                down = weight(b, t, 96, 96, slice(0, 256))

                def finish(s, v, ga):
                    v2 = v * v
                    th = jnp.tanh(v * (C0 + C1 * v2))
                    h = 0.5 + 0.5 * th
                    act[t, s, :] = (v * h).astype(BF)
                    slope = h + (0.5 * v) * (1.0 - th * th) * (C0 + (3.0 * C1) * v2)
                    gu[t, s, :] = (ga * slope).astype(BF)

                waiting = None
                for i in range(length // 128):
                    s = slice(128 * i, 128 * i + 128)
                    now = (s, dot(n2[s, :], up), dot(cot[s, :], down))
                    if waiting is not None:
                        finish(*waiting)
                    waiting = now
                finish(*waiting)

                for k, step in enumerate(steps):
                    after(t, k, *step)

        hidden()

    def mlp_sums(j, *steps):
        b = bm[j]

        def wcat(r0):
            return jnp.concatenate([weight(b, t, r0, 96, slice(0, 256)) for t in range(4)], 1)

        @phase
        def sums():
            @pl.loop(0, length // 512)
            def _(i):
                s = rows_of(i, 512)
                one = dot(cat(act, s), wcat(96), NT)
                two = dot(cat(gu, s), wcat(0), NT)
                if j == 0:
                    acc[s, :] = one
                    gn[s, :] = two
                else:
                    acc[s, :] += one
                    gn[s, :] += two
                for k, step in enumerate(steps):
                    after(i, k, *step)

        sums()

    def mlp_weight_grads(j, *steps):
        b = grads[j]

        @phase
        def weight_grads():
            for t in range(4):
                gup = dot(n2[...], gu[t], TN).astype(BF)
                b[t // 2, t % 2, :, :, 0:96, :] = gup.reshape(4, 2, 96, 256)
                gdown = dot(cot[...], act[t], TN).astype(BF)
                b[t // 2, t % 2, :, :, 96:192, :] = gdown.reshape(4, 2, 96, 256)
                for step in steps[t : t + 1]:
                    step()

        weight_grads()

    def store_low():
        return [
            pltpu.make_async_copy(gu.at[k], lo_out.at[:, pl.ds(256 * k, 256)], local_sem.at[k])
            for k in range(width // 256)
        ]

    @phase
    def second_norm_back():
        @pl.loop(0, length // 256)
        def _(i):
            s = rows_of(i, 256)
            v = mid[s, :]
            mlp = acc[s, :]
            out = v + mlp
            weight_rows = val[s, :]
            ar[0, 4:5, :] += jnp.sum(weight_rows * (out * out), 0, keepdims=True)
            ar[0, 6:7, :] += jnp.sum(weight_rows * (mlp * mlp), 0, keepdims=True)
            low_out = out.astype(BF)
            for k in range(width // 256):
                gu[k, s, :] = low_out[:, 256 * k : 256 * k + 256]
            back, g_gain, g_bias = norm_back(v, kept[s, 2:3], kept[s, 3:4], gn[s, :], par[66:67, :])
            ar[0, 2:3, :] += g_gain
            ar[0, 3:4, :] += g_bias
            grad = cot[s, :].astype(F32) + back
            mid[s, :] = grad
            n2[s, :] = grad.astype(BF)

        for one in store_low():
            one.start()

    @phase
    def out_projection_back():
        @pl.loop(0, 4)
        def _(t):
            act[t] = dot(n2[...], out_weight(t)).astype(BF)
            grad = dot(n2[...], cc[t], TN)
            bm2[t // 2, t % 2, :, :, 0:96, 0:128] = grad[:, 0:128].astype(BF).reshape(4, 2, 96, 128)
            bm2[t // 2, t % 2, :, :, 96:144, 0:128] = fold(grad[:, 128:192])

    @phase
    def pair_attention_back():
        @pl.loop(0, 4)
        def _(t):
            attend_back(tt, ll, kx, k2, kt, cc, act, (dk, dv), (0, 1), t, length)
            after(t, 0, o_sum.s2)
            after(t, 1, m_sum[1].s4)

    def early_take_0():
        early.take(0)
        early.run(1)

    def early_take_1():
        early.take(1)
        early.left()

    @phase
    def pair_weight_grads():
        @pl.loop(0, 2)
        def _(x):
            both = jnp.concatenate([tt[2 * x, :, 0:384], tt[2 * x + 1, :, 0:384]], 1)
            grads = dot(n1[...], both, TN).astype(BF)
            for c in range(2):
                grad = grads[:, 384 * c : 384 * c + 384]
                gb[x, c, :, :, 0:96, :] = grad[:, 0:256].reshape(4, 2, 96, 256)
                third = grad[:, 256:384].reshape(4, 2, 96, 128)
                gb[x, c, :, :, 96:144, 0:128] = third[:, :, 0:48]
                gb[x, c, :, :, 96:144, 128:256] = third[:, :, 48:96]

    @phase
    def odd_weight_grads():
        @pl.loop(0, 4)
        def _(t):
            grad = dot(n1[...], tt[t, :, 384:640], TN)
            bm2[t // 2, t % 2, :, :, 0:96, 128:256] = grad[:, 0:128].astype(BF).reshape(4, 2, 96, 128)
            bm2[t // 2, t % 2, :, :, 96:144, 128:256] = fold(grad[:, 128:192])

    @phase
    def odd_attention_back():
        @pl.loop(0, 4)
        def _(t):
            attend_back(tt, ll, kx, k2, kt, cc, act, (dk, dv), (2,), t, length)
            after(t, 0, qa_sum.s2, o_sum.s3)
            after(t, 1, qd_sum.s2, m_sum[1].s5, early_take_0)
            after(t, 2, qa_sum.s3)
            after(t, 3, o_sum.s4)

    def store_grad():
        return pltpu.make_async_copy(acc, gt_out, local_sem.at[4])

    @phase
    def first_norm_back():
        @pl.loop(0, length // 256)
        def _(i):
            s = rows_of(i, 256)
            w = jnp.concatenate([weight(bq, t, 0, 96, slice(0, 640)) for t in range(4)], 1)
            grad = dot(cat(tt, s), w, NT)
            after(i, 2, qb_sum.s3, qc_sum.s3)
            back, g_gain, g_bias = norm_back(tok[s, :].astype(F32), kept[s, 0:1], kept[s, 1:2], grad, par[64:65, :])
            g1[0:1, :] += g_gain
            g1[1:2, :] += g_bias
            acc[s, :] = mid[s, :] + back
            after(i, 0, qb_sum.s2, qc_sum.s2, qa_sum.s4)
            after(i, 2, qd_sum.s4)

        store_grad().start()
        for k in range(width // 128):
            for n in range(2):
                br[0, 6 * n + k : 6 * n + k + 1, :] = g1[n : n + 1, 128 * k : 128 * k + 128]

    @phase
    def small_results():
        rows = [jnp.concatenate([br[2, 6 * n + k : 6 * n + k + 1, :] for k in range(6)], 1) for n in range(2)]
        sums = jnp.concatenate(rows + [ar[2, 2:8, :]], 0)
        if inner > 1:
            small_out[...] = sums
            return
        share = width // 32
        owner = lax.axis_index("fsdp") * 4 + lax.axis_index("tp")
        moved = pltpu.roll(sums, width - owner * share, 1)
        square = jnp.sum(sums[4:7], axis=1, keepdims=True) / (sums[7:8, 0:1] * width)
        rms = jnp.sqrt(jnp.broadcast_to(square, (3, 128)))
        lane = lanes()
        row = jnp.where(lane == 0, rms[0:1], jnp.where(lane == 1, rms[1:2], rms[2:3]))
        small_out[0:4, :] = moved[0:4, 0:128]
        small_out[4:8, :] = jnp.broadcast_to(row, (4, 128))

    def give(k):
        held = (gq_out, go_out, gup_out, gdown_out, small_out)[k]
        return pltpu.make_async_copy(held, big_outs[k], give_sem.at[k])

    entry()
    q_in[0].s1()
    document_marks()
    for one in own_copies():
        one.wait()
    q_in[1].s1()
    first_norm_statistics()
    q_in[0].s2()
    q_in[2].s1()
    q_in[1].s2()
    q_in[0].s3()
    q_in[2].s2()
    o_in.s1()
    q_in[1].s3()
    m_in[0].s1()
    q_in[2].s3()
    first_norm()
    o_in.s2()
    m_in[1].s1()
    attention()
    out_projection()
    m_in[1].s4()
    m_in[0].s5()
    m_in[1].s5()

    mlp_hidden(0, (), (m_in[2].s3,), (), (m_in[3].s3,))
    m_in[4].s2()
    mlp_weight_grads(0)
    m_sum[0].s1()
    m_in[2].s4()
    m_in[5].s2()
    mlp_sums(0, (m_in[3].s4,))
    m_sum[0].s2()
    m_in[2].s5()
    m_in[3].s5()

    mlp_hidden(1, (), (m_in[4].s3,))
    m_in[0].s6()
    m_in[1].s6()
    mlp_weight_grads(1, lambda: None, m_in[5].s3)
    m_sum[1].s1()
    mlp_sums(1, (m_sum[0].s3,), (m_in[4].s4, m_in[5].s4))
    m_sum[1].s2()
    m_in[4].s5()
    m_in[5].s5()

    mlp_hidden(2)
    m_in[2].s6()
    m_in[3].s6()
    mlp_weight_grads(2)
    m_sum[2].s1()
    m_sum[0].s4()
    mlp_sums(2)
    m_sum[2].s2()
    m_sum[1].s3()
    m_in[4].s6()
    m_in[5].s6()

    second_norm_back()
    early.run(0)
    o_in.s6()
    out_projection_back()
    o_sum.s1()
    m_sum[2].s3()
    m_sum[0].s5()
    m_sum[0].give_credit()
    pair_attention_back()
    pair_weight_grads()
    m_sum[2].s4()
    m_sum[0].take_credit()
    qa_sum.s1()
    qd_sum.s1()
    odd_attention_back()
    odd_weight_grads()
    qb_sum.s1()
    qc_sum.s1()
    qd_sum.s3()
    m_sum[2].s5()
    for g in q_in:
        g.s6()
    give(2).start()
    give(3).start()
    first_norm_back()
    late.run(0)
    early_take_1()
    o_sum.s5()
    give(1).start()
    qb_sum.s4()
    qc_sum.s4()
    late.take(0)
    late.run(1)
    qa_sum.s5()
    qd_sum.s5()
    late.take(1)
    late.left()
    small_results()
    give(4).start()
    qb_sum.s5()
    for one in store_low():
        one.wait()
    store_grad().wait()
    qc_sum.s5()
    give(0).start()
    for k in range(5):
        give(k).wait()


def scatter_slots(rows, columns):
    return [
        pltpu.VMEM((2, 4, 2, rows, columns), BF),
        pltpu.VMEM((4, (rows // 2 + 15) // 16 * 16, columns), BF),
        pltpu.VMEM((4, rows // 2, columns), BF),
        pltpu.VMEM((4, rows, columns), BF),
        pltpu.VMEM((4, rows, columns), BF),
        pltpu.VMEM((3, rows, columns), BF),
    ]


def layer(inner, tokens, cotangent, segments, valid, wq, wo, up, down, *params):
    length, width = tokens.shape
    block = lambda rows, columns: pltpu.VMEM((2, 2, 4, 2, rows, columns), BF)
    small = (8, width) if inner > 1 else (8, 128)
    shapes = [(3, 96, 3 * HD), (3 * HD, 96), (96, width), (96, width), small]
    scratch = [pltpu.VMEM(shape, F32) for shape in shapes]
    scratch += [
        block(96, 640), block(144, 128), block(192, 256), block(192, 256), block(192, 256), block(192, 256),
        pltpu.VMEM((length, width), BF),
        pltpu.VMEM((length, width), BF),
        pltpu.VMEM((length, width), BF),
        pltpu.VMEM((4, length, 640), BF),
        pltpu.VMEM((4, length, 256), BF),
        pltpu.VMEM((4, length, 128), BF),
        pltpu.VMEM((length, 128), BF),
        pltpu.VMEM((length, 128), BF),
        pltpu.VMEM((128, length), BF),
        pltpu.VMEM((4, width, 128), BF),
        pltpu.VMEM((length, width), F32),
        pltpu.VMEM((length, width), BF),
        pltpu.VMEM((length, width), F32),
        pltpu.VMEM((length, width), F32),
        pltpu.VMEM((4, length, 256), BF),
        pltpu.VMEM((4, length, 256), BF),
        pltpu.VMEM((length, 1), F32),
        pltpu.VMEM((length, 4), F32),
        pltpu.VMEM((128, width), F32),
    ]
    scratch += [pltpu.VMEM((length, 128), F32)] * 2
    scratch += [scatter_slots(192, 256) * 3, scatter_slots(144, 256)]
    scratch += [
        pltpu.VMEM((3, 8, width), F32),
        pltpu.VMEM((10, 8, width), F32),
        pltpu.VMEM((3, 16, 128), F32),
        pltpu.VMEM((10, 16, 128), F32),
        pltpu.VMEM((8, width), F32),
        pltpu.SemaphoreType.DMA((10, 3)),
        pltpu.SemaphoreType.DMA((10, 6)),
        pltpu.SemaphoreType.DMA((8, 3)),
        pltpu.SemaphoreType.DMA((8, 5)),
        pltpu.SemaphoreType.REGULAR((1, 6)),
        pltpu.SemaphoreType.DMA((2, 2)),
        pltpu.SemaphoreType.DMA((2, 2)),
        pltpu.SemaphoreType.DMA((5,)),
        pltpu.SemaphoreType.DMA((8,)),
        pltpu.SemaphoreType.DMA((5,)),
    ]
    vmem, anywhere = pl.BlockSpec(memory_space=pltpu.VMEM), pl.BlockSpec(memory_space=pl.ANY)
    return pl.pallas_call(
        partial(kernel, inner, length),
        out_shape=[
            jax.ShapeDtypeStruct((length, width), BF),
            jax.ShapeDtypeStruct((length, width), F32),
        ]
        + [jax.ShapeDtypeStruct(shape, F32) for shape in shapes],
        in_specs=[anywhere, anywhere, vmem, vmem, vmem, vmem, anywhere, anywhere] + [vmem] * 4,
        out_specs=[anywhere] * (2 + len(shapes)),
        scratch_shapes=scratch,
        compiler_params=pltpu.CompilerParams(
            collective_id=0, has_side_effects=True, vmem_limit_bytes=63 * 2**20
        ),
    )(tokens, cotangent, segments, valid, wq, wo, up, down, *params)


def hand_over(arrays, share):
    count = len(arrays)
    pieces = []
    for k, a in enumerate(arrays):
        step = 256 if a.ndim == 2 and a.shape[0] % 256 == 0 else a.shape[0]
        pieces += [(k, start, step) for start in range(0, a.shape[0], step)]
    small = [(share,)] * 4 + [(3,)] if share else []
    shapes = [(a.shape, a.dtype) for a in arrays[: count - 1 if small else count]] + [(cut, F32) for cut in small]
    whole = len(shapes) - len(small)

    def body(*refs):
        came, went = refs[:count], refs[count : count + len(shapes)]
        held = refs[count + len(shapes) : 2 * count + len(shapes)]
        cuts, sems = refs[2 * count + len(shapes) : -1], refs[-1]

        def part(ref, n):
            _, start, step = pieces[n]
            return ref.at[pl.ds(start, step)] if step < ref.shape[0] else ref

        def fetch(n):
            k = pieces[n][0]
            return pltpu.make_async_copy(part(came[k], n), part(held[k], n), sems.at[0, n])

        def put(n):
            k = pieces[n][0]
            return pltpu.make_async_copy(part(held[k], n), part(went[k], n), sems.at[1, n])

        def put_cut(k):
            return pltpu.make_async_copy(cuts[k], went[whole + k], sems.at[1, len(pieces) + k])

        for n in reversed(range(len(pieces))):
            fetch(n).start()
        for n in reversed(range(len(pieces))):
            fetch(n).wait()
            if pieces[n][0] < whole:
                put(n).start()
                continue
            for k, cut in enumerate(small):
                cuts[k][...] = held[whole][k, 0 : cut[0]]
                put_cut(k).start()
        for n in range(len(pieces)):
            if pieces[n][0] < whole:
                put(n).wait()
        for k in range(len(small)):
            put_cut(k).wait()

    anywhere = pl.BlockSpec(memory_space=pltpu.HBM)
    return pl.pallas_call(
        body,
        out_shape=[jax.ShapeDtypeStruct(shape, dtype) for shape, dtype in shapes],
        in_specs=[anywhere] * count,
        out_specs=[anywhere] * len(shapes),
        scratch_shapes=[pltpu.VMEM(a.shape, a.dtype) for a in arrays]
        + [pltpu.VMEM(cut, F32) for cut in small]
        + [pltpu.SemaphoreType.DMA((2, len(pieces) + 5))],
        compiler_params=pltpu.CompilerParams(vmem_limit_bytes=63 * 2**20),
    )(*arrays)


def local(
    tokens, segment_ids, valid, ln1_gain, ln1_bias, w_qkv, w_out, ln2_gain, ln2_bias, w_up, w_down, cotangent
):
    length, width = tokens.shape
    holders = lax.axis_size("fsdp")
    inner = holders // 8
    groups = [[g * inner + i for i in range(inner)] for g in range(8)]

    def widen(block, axis=0):
        if inner == 1:
            return block
        return lax.all_gather(block, "fsdp", axis_index_groups=groups, axis=axis, tiled=True)

    def narrow(block, axis=0):
        if inner == 1:
            return block
        return lax.psum_scatter(
            block, "fsdp", scatter_dimension=axis, axis_index_groups=groups, tiled=True
        )

    params = [widen(one.reshape(1, -1), 1) for one in (ln1_gain, ln1_bias, ln2_gain, ln2_bias)]
    results = layer(
        inner, tokens, cotangent, segment_ids, valid.reshape(1, length),
        widen(w_qkv.transpose(1, 0, 2), 1), widen(w_out, 1), widen(w_up), widen(w_down.T), *params,
    )
    low, grad_tokens, gq, go, gup, gdown, *small = hand_over(results, width // 32 if inner == 1 else 0)
    if inner > 1:
        sums = lax.psum(small[0], "fsdp", axis_index_groups=groups)
        share = width // (holders * lax.axis_size("tp"))
        owner = lax.axis_index("fsdp") * lax.axis_size("tp") + lax.axis_index("tp")
        mine = lax.dynamic_slice_in_dim(sums[0:4], owner * share, share, 1)
        spread = jnp.sqrt(jnp.sum(sums[4:7], axis=1) / (sums[7, 0] * width))
        small = (mine[0], mine[1], mine[2], mine[3], spread)
    return (
        low, grad_tokens, small[0], small[1], narrow(gq, 1).transpose(1, 0, 2), narrow(go, 1),
        small[2], small[3], narrow(gup), narrow(gdown).T, small[4],
    )


def solution(mesh):
    both = ("fsdp", "tp")
    return jax.shard_map(
        local,
        mesh=mesh,
        in_specs=(
            P(both, None), P("fsdp", None), P(both), P("fsdp"), P("fsdp"), P("fsdp", None, "tp"),
            P("tp", "fsdp"), P("fsdp"), P("fsdp"), P("fsdp", "tp"), P("tp", "fsdp"), P(both, None),
        ),
        out_specs=(
            P(both, None), P(both, None), P(both), P(both), P("fsdp", None, "tp"), P("tp", "fsdp"),
            P(both), P(both), P("fsdp", "tp"), P("tp", "fsdp"), P(),
        ),
        check_vma=False,
    )
```

```python
from functools import partial

import jax
import jax.numpy as jnp
from jax import lax
from jax.experimental import pallas as pl
from jax.experimental.pallas import tpu as pltpu
from jax.sharding import PartitionSpec as P

HD = 64
BQ = 256
EPS = 1e-05
BIG = -1e30
F32 = jnp.float32
BF = jnp.bfloat16
NN = (((1,), (0,)), ((), ()))
NT = (((1,), (1,)), ((), ()))
TN = (((0,), (0,)), ((), ()))
MESH = pl.DeviceIdType.MESH
C0 = 0.7978845608
C1 = 0.7978845608 * 0.044715


def dot(a, b, dims=NN):
    return lax.dot_general(a, b, dims, preferred_element_type=F32)


def phase(body):
    return body


def remote(src, dst, send, recv, device):
    return pltpu.make_async_remote_copy(
        src_ref=src, dst_ref=dst, send_sem=send, recv_sem=recv,
        device_id=device, device_id_type=MESH,
    )


class Place:
    def __init__(self, inner):
        f = lax.axis_index("fsdp")
        t = lax.axis_index("tp")
        g = f // inner
        self.low = f % inner
        self.inner = inner
        self.z, self.y, self.x, self.c = g // 2, g % 2, t // 2, t % 2

    def device(self, z, y, x, c):
        return ((z * 2 + y) * self.inner + self.low, x * 2 + c)

    def core(self):
        return self.device(self.z, self.y, self.x, 1 - self.c)

    def xn(self):
        return self.device(self.z, self.y, 1 - self.x, self.c)

    def yn(self):
        return self.device(self.z, 1 - self.y, self.x, self.c)

    def cube(self, n):
        y, x, c = (self.y + n // 4) % 2, (self.x + n // 2) % 2, (self.c + n) % 2
        return self.device(self.z, y, x, c)

    def zn(self, d):
        return self.device((self.z + d) % 4, self.y, self.x, self.c)

    def reach(self, k):
        upper = self.z // 2
        return (3 - k) * (1 - upper) + (1 + k) * upper

    def zp(self, d):
        return self.device((self.z - d + 4) % 4, self.y, self.x, self.c)


def greet(inner):
    p = Place(inner)
    sem = pltpu.get_barrier_semaphore()
    for dev in [p.cube(n) for n in range(1, 8)] + [p.zn(d) for d in range(1, 4)]:
        pl.semaphore_signal(sem, inc=1, device_id=dev, device_id_type=MESH)


def met(inner):
    pl.semaphore_wait(pltpu.get_barrier_semaphore(), 10)


class Gather:
    def __init__(self, name, inner, buf, row0, rows, send, recv):
        self.name = name
        self.inner, self.buf, self.row0, self.rows = inner, buf, row0, rows
        self.send, self.recv = send, recv

    def own(self, x, c, z, y):
        return self.buf.at[x, c, z, y, pl.ds(self.row0, self.rows)]

    def group(self, x, c, y, half=None):
        start, size = self.row0, self.rows
        if half is not None:
            cut = (size // 2 + 15) // 16 * 16
            start, size = (start + cut, size - cut) if half else (start, cut)
        return self.buf.at[x, c, :, y, pl.ds(start, size)]

    def parts(self, slot):
        p = Place(self.inner)
        x, c, z, y = p.x, p.c, p.z, p.y
        if slot < 3:
            mine = self.own(x, c, z, y)
            return mine, mine, p.zn(p.reach(slot))
        if slot == 3:
            return self.group(x, c, y), self.group(1 - x, c, y), p.xn()
        if slot == 4:
            return self.group(x, c, y), self.group(x, c, 1 - y), p.yn()
        if slot == 5:
            return self.group(1 - x, c, y, 0), self.group(1 - x, c, 1 - y, 0), p.yn()
        if slot == 6:
            return self.group(x, c, 1 - y, 1), self.group(1 - x, c, 1 - y, 1), p.xn()
        xx = x if slot in (7, 9) else 1 - x
        yy = y if slot in (7, 8) else 1 - y
        return self.group(xx, c, yy), self.group(xx, 1 - c, yy), p.core()

    SENT = (0, 0, 0, 1, 1, 2, 2, 1, 2, 2, 2)
    CAME = (0, 0, 0, 1, 2, 3, 3, 4, 5, 4, 5)

    def start(self, *slots):
        for slot in slots:
            mine, _, dev = self.parts(slot)
            remote(mine, mine, self.send.at[self.SENT[slot]], self.recv.at[self.CAME[slot]], dev).start()

    def bytes_of(self, blocks):
        rows = pl.ds(self.row0, self.rows)
        if blocks == 3:
            return self.buf.at[0, 0, 0:3, 0, rows]
        if blocks == 4:
            return self.buf.at[0, 0, :, 0, rows]
        if blocks == 8:
            return self.buf.at[0, 0, :, :, rows]
        if blocks == 12:
            return self.buf.at[:, :, 0:3, 0, rows]
        return self.buf.at[0, :, :, :, rows]

    def arrive(self, group):
        ref = self.bytes_of((3, 4, 4, 4, 8, 8)[group])
        dev = Place(self.inner).core()
        remote(ref, ref, self.send.at[0], self.recv.at[group], dev).wait_recv()

    def left(self):
        for group, blocks in enumerate((3, 12, 16)):
            ref = self.bytes_of(blocks)
            dev = Place(self.inner).core()
            remote(ref, ref, self.send.at[group], self.recv.at[0], dev).wait_send()

    def s1(self):
        self.start(0, 1, 2)

    def s2(self):
        self.arrive(0)
        self.start(3, 4, 7)

    def s3(self):
        self.arrive(2)
        self.start(6, 9)
        self.arrive(1)
        self.start(5, 8)

    def s4(self):
        self.arrive(3)
        self.start(10)

    def near(self):
        self.arrive(4)

    def far(self):
        self.arrive(5)

    def s5(self):
        self.near()
        self.far()

    def s6(self):
        self.left()


class Scatter:
    def __init__(self, name, inner, buf, block, slots, place, send, recv, credit, out):
        self.name = name
        self.inner, self.buf, self.slots = inner, buf, slots
        self.row0, self.rows, self.col0, columns = block
        self.half = (self.rows // 2 + 15) // 16 * 16
        row, upper, lower, col = place
        self.land = (
            slice(row, row + self.rows), slice(upper, upper + self.half),
            slice(lower, lower + self.rows - self.half), slice(col, col + columns),
        )
        self.cols = slice(self.col0, self.col0 + columns)
        self.send, self.recv = send, recv
        self.credit, self.out = credit, out

    def parts(self, slot):
        p = Place(self.inner)
        x, c, z, y = p.x, p.c, p.z, p.y
        buf, cols = self.buf, self.cols
        r1, ra, rb, rx, ry, rz = self.slots
        rows, upper, lower = self.spans()
        land, land_a, land_b, land_cols = self.land
        if slot == 0:
            return buf.at[:, 1 - c, :, :, rows, cols], r1.at[:, :, :, land, land_cols], p.core()
        if slot == 1:
            return buf.at[1 - x, c, :, 1 - y, upper, cols], ra.at[:, land_a, land_cols], p.yn()
        if slot == 2:
            return buf.at[1 - x, c, :, 1 - y, lower, cols], rb.at[:, land_b, land_cols], p.xn()
        if slot == 3:
            return buf.at[1 - x, c, :, y, rows, cols], rx.at[:, land, land_cols], p.xn()
        if slot == 4:
            return buf.at[x, c, :, 1 - y, rows, cols], ry.at[:, land, land_cols], p.yn()
        d = p.reach(slot - 5)
        return buf.at[x, c, (z + d) % 4, y, rows, cols], rz.at[d - 1, land, land_cols], p.zn(d)

    def spans(self):
        start, end = self.row0, self.row0 + self.rows
        return slice(start, end), slice(start, start + self.half), slice(start + self.half, end)

    SENT = (0, 1, 1, 1, 1, 2, 2, 2)
    CAME = (0, 1, 2, 3, 3, 4, 4, 4)

    def start(self, *slots):
        for slot in slots:
            src, dst, dev = self.parts(slot)
            remote(src, dst, self.send.at[self.SENT[slot]], self.recv.at[self.CAME[slot]], dev).start()

    def arrive(self, group):
        land, _, _, cols = self.land
        if group < 3:
            ref = self.parts(group)[1]
        elif group == 3:
            ref = self.slots[0].at[0, :, :, land, cols]
        else:
            ref = self.slots[5].at[:, land, cols]
        remote(ref, ref, self.send.at[0], self.recv.at[group], Place(self.inner).core()).wait_recv()

    def left(self):
        rows, cols = self.spans()[0], self.cols
        refs = (
            self.buf.at[:, 0, :, :, rows, cols], self.buf.at[:, :, 0:3, 0, rows, cols],
            self.buf.at[0, 0, 0:3, 0, rows, cols],
        )
        for group, ref in enumerate(refs):
            dev = Place(self.inner).core()
            remote(ref, ref, self.send.at[group], self.recv.at[0], dev).wait_send()

    def take_credit(self):
        for i in range(6):
            pl.semaphore_wait(self.credit.at[i], 1)

    def give_credit(self):
        p = Place(self.inner)
        for i, dev in enumerate((p.core(), p.xn(), p.yn(), p.zp(1), p.zp(2), p.zp(3))):
            pl.semaphore_signal(self.credit.at[i], inc=1, device_id=dev, device_id_type=MESH)

    def s1(self):
        self.start(0)

    def add(self, x, y, rows, *others):
        c = Place(self.inner).c

        @pl.loop(0, 4)
        def _(z):
            total = self.buf[x, c, z, y, rows, self.cols]
            if len(others) > 1:
                total = total.astype(F32)
            for other in others:
                total = total + other(z).astype(total.dtype)
            self.buf[x, c, z, y, rows, self.cols] = total.astype(BF)

    def s2(self):
        p = Place(self.inner)
        r1, (land, _, _, cols) = self.slots[0], self.land
        self.arrive(0)
        for x, y in ((1 - p.x, 1 - p.y), (1 - p.x, p.y), (p.x, 1 - p.y), (p.x, p.y)):
            self.add(x, y, self.spans()[0], lambda z: r1[x, z, y, land, cols])
            if x is not p.x and y is not p.y:
                self.start(1, 2)

    def s3(self):
        p = Place(self.inner)
        _, upper, lower = self.spans()
        _, land_a, land_b, cols = self.land
        ra, rb = self.slots[1:3]
        self.arrive(1)
        self.add(1 - p.x, p.y, upper, lambda z: ra[z, land_a, cols])
        self.start(3)
        self.arrive(2)
        self.add(p.x, 1 - p.y, lower, lambda z: rb[z, land_b, cols])
        self.start(4)

    def s4(self):
        p = Place(self.inner)
        land, _, _, cols = self.land
        rx, ry = self.slots[3:5]
        self.arrive(3)
        self.add(p.x, p.y, self.spans()[0], lambda z: rx[z, land, cols], lambda z: ry[z, land, cols])
        self.start(5, 6, 7)

    def s5(self):
        p = Place(self.inner)
        land, _, _, cols = self.land
        rz = self.slots[5]
        self.arrive(4)
        total = self.buf[p.x, p.c, p.z, p.y, self.spans()[0], self.cols].astype(F32)
        for d in range(3):
            total = total + rz[d, land, cols].astype(F32)
        self.out(total)
        self.left()


class Total:
    def __init__(self, name, inner, ref, got, send, recv):
        self.name = name
        self.inner, self.ref, self.got, self.send, self.recv = inner, ref, got, send, recv

    def copy(self, slot):
        p = Place(self.inner)
        dev = p.cube(slot + 1) if slot < 7 else p.zn(slot - 6)
        stage = 0 if slot < 7 else 1
        return remote(self.ref.at[stage], self.got.at[slot], self.send.at[stage], self.recv.at[stage], dev)

    def slots(self, stage):
        return range(7) if stage == 0 else range(7, 10)

    def all_of(self, stage):
        span = self.slots(stage)
        ref = self.got.at[span.start : span.stop]
        return remote(ref, ref, self.send.at[stage], self.recv.at[stage], Place(self.inner).core())

    def run(self, stage):
        for slot in self.slots(stage):
            self.copy(slot).start()

    def take(self, stage):
        self.all_of(stage).wait_recv()
        total = self.ref[stage]
        for slot in self.slots(stage):
            total = total + self.got[slot]
        self.ref[stage + 1] = total

    def left(self):
        for stage in range(2):
            self.all_of(stage).wait_send()


def head_parts(t_ref, k2_ref, t, h, qs, kr):
    if h < 2:
        return t_ref[t, qs, 0:128], t_ref[t, kr, 128:256], t_ref[t, kr, 256:384]
    return t_ref[t, qs, 384:512], k2_ref[kr, :], t_ref[t, kr, 512:640]


def lanes():
    return lax.broadcasted_iota(jnp.int32, (1, 128), 1)


def roll_key(t_ref, k2_ref, t):
    k2_ref[...] = pltpu.roll(t_ref[t, :, 384:512].astype(F32), 64, 1).astype(BF)


def below(transposed, size=BQ):
    r = lax.broadcasted_iota(jnp.int32, (size, size), 0)
    c = lax.broadcasted_iota(jnp.int32, (size, size), 1)
    return r <= c if transposed else r >= c


def attend(t_ref, l_ref, kx_ref, k2_ref, c_ref, t, length):
    lane = lanes()
    low = lane < 64
    roll_key(t_ref, k2_ref, t)
    for i in range(length // BQ):
        first = max(0, i * BQ - length // 2)
        width = (i + 1) * BQ - first
        qs, kr = slice(i * BQ, (i + 1) * BQ), slice(first, first + width)
        kx = kx_ref[kr, :]
        doc = kx_ref[qs, :].astype(F32)
        qx = jnp.where(lane < 8, BIG * (1.0 - doc), 0.0).astype(BF)
        marks = qx
        outs = []
        for h in range(3):
            q, k, v = head_parts(t_ref, k2_ref, t, h, qs, kr)
            keep = jnp.logical_not(low) if h == 1 else low
            q = jnp.where(keep, q * BF(HD ** -0.5), BF(0))
            s = dot(jnp.concatenate([q, qx], 1), jnp.concatenate([k, kx], 1), NT)
            edge = jnp.where(below(False), s[:, width - BQ :], BIG)
            s = edge if width == BQ else jnp.concatenate([s[:, : width - BQ], edge], 1)
            top = jnp.max(s, axis=1, keepdims=True)
            p = jnp.exp(s - top).astype(BF)
            both = dot(p, jnp.concatenate([v, jnp.ones((width, 128), BF)], 1))
            total = both[:, 128:256]
            outs.append(both[:, :128] / total)
            rest = -(top + jnp.log(total))
            for n in range(3):
                piece = rest.astype(BF)
                marks = jnp.where(lane == 8 + 16 * h + n, piece, marks)
                rest = rest - piece.astype(F32)
        l_ref[t, qs, :] = marks
        c_ref[t, qs, 0:128] = jnp.where(low, outs[0], outs[1]).astype(BF)
        c_ref[t, qs, 128:256] = jnp.where(low, outs[2], 0.0).astype(BF)


def attend_back(t_ref, l_ref, kx_ref, k2_ref, kt_ref, c_ref, do_ref, sums, heads, t, length):
    lane = lanes()
    low = lane < 64
    dk_ref, dv_ref = sums
    odd = heads == (2,)
    size = BQ
    if odd:
        roll_key(t_ref, k2_ref, t)
        kt_ref[...] = k2_ref[...].T
    else:
        kt_ref[...] = t_ref[t, :, 128:256].T
    for ref in sums:
        ref[...] = jnp.zeros_like(ref)
    for i in range(length // size):
        first = max(0, i * size - length // 2)
        width = (i + 1) * size - first
        qs, kr = slice(i * size, (i + 1) * size), slice(first, first + width)
        marks = l_ref[t, qs, :]
        side = slice(128, 256) if odd else slice(0, 128)
        qs_all, dos, left, right = [], [], [], []
        for h in heads:
            q, k, v = head_parts(t_ref, k2_ref, t, h, qs, kr)
            keep = jnp.logical_not(low) if h == 1 else low
            q = jnp.where(keep, q * BF(HD ** -0.5), BF(0))
            do = jnp.where(keep, do_ref[t, qs, side], BF(0))
            dd = (do.astype(F32) * c_ref[t, qs, side].astype(F32)).astype(BF)
            mine = (lane < 8) | ((lane >= 8 + 16 * h) & (lane < 24 + 16 * h))
            qs_all.append(q)
            dos.append(do)
            left.append(jnp.concatenate([q, jnp.where(mine, marks, BF(0))], 1))
            right.append(jnp.concatenate([do, dd], 1))
        s_all = dot(jnp.concatenate([k, kx_ref[kr, :]], 1), jnp.concatenate(left, 0), NT)
        minus = jnp.full((width, 128), -1.0, BF)
        dp_all = dot(jnp.concatenate([v, minus], 1), jnp.concatenate(right, 0), NT)
        ps, dss, grads = [], [], []
        for n in range(len(heads)):
            s = s_all[:, n * size : (n + 1) * size]
            edge = jnp.where(below(True, size), s[width - size :], BIG)
            s = edge if width == size else jnp.concatenate([s[: width - size], edge], 0)
            p = jnp.exp(s)
            ds = (p * dp_all[:, n * size : (n + 1) * size]).astype(BF)
            ps.append(p.astype(BF))
            dss.append(ds)
            grads.append(dot(kt_ref[64 * n : 64 * n + 64, kr], ds))
        if odd:
            grads.append(jnp.zeros((64, size), F32))
        grad = (jnp.concatenate(grads, 0).T * HD ** -0.5).astype(BF)
        dv_ref[kr, :] += dot(jnp.concatenate(ps, 1), jnp.concatenate(dos, 0))
        dk_ref[kr, :] += dot(jnp.concatenate(dss, 1), jnp.concatenate(qs_all, 0))
        if odd:
            t_ref[t, qs, 384:512] = jnp.where(low, grad, t_ref[t, qs, 384:512])
        else:
            t_ref[t, qs, 0:128] = grad
    if odd:
        moved = pltpu.roll(dk_ref[...], 64, 1).astype(BF)
        t_ref[t, :, 384:512] = jnp.where(low, t_ref[t, :, 384:512], moved)
        t_ref[t, :, 512:640] = dv_ref[...].astype(BF)
    else:
        t_ref[t, :, 128:256] = dk_ref[...].astype(BF)
        t_ref[t, :, 256:384] = dv_ref[...].astype(BF)


def stats(v):
    mean = jnp.mean(v, axis=-1, keepdims=True)
    center = v - mean
    scale = lax.rsqrt(jnp.mean(center * center, axis=-1, keepdims=True) + EPS)
    return center * scale, mean, scale


def norm_back(v, mean, scale, q, gain):
    n = (v - mean) * scale
    e = q * gain
    back = scale * (e - jnp.mean(e, -1, keepdims=True) - n * jnp.mean(e * n, -1, keepdims=True))
    return back, jnp.sum(q * n, 0, keepdims=True), jnp.sum(q, 0, keepdims=True)


def kernel(
    inner, length,
    tok_in, cot_in, seg, valid, wq_in, wo_in, up_in, down_in, par_a, par_b, par_c, par_d,
    lo_out, gt_out, *rest,
):
    big_outs = rest[0:5]
    (
        gq_out, go_out, gup_out, gdown_out, small_out,
        bq, bo, bm0, bm1, bm2, gb,
        tok, cot, n1, tt, cc, ll, kx, k2, kt, wo, mid, n2, acc, gn, act, gu, val, kept, par,
        dk, dv,
        m_sets, o_set, ar, ar_got, br, br_got, g1,
        ag_send, ag_recv, rs_send, rs_recv, credit, ar_send, ar_recv, local_sem, own_sem, give_sem,
    ) = rest[5:]
    width = tok.shape[1]
    bm = (bm0, bm1, bm2)
    blocks = [(bq, 0, 32), (bq, 32, 32), (bq, 64, 32), (bo, 0, 144)]
    blocks += [(b, r0, 96) for b in bm for r0 in (0, 96)]
    gathers = [
        Gather(f"gather{k}", inner, b, r0, rows, ag_send.at[k], ag_recv.at[k])
        for k, (b, r0, rows) in enumerate(blocks)
    ]
    here = Place(inner)
    mine = (here.x, here.c, here.z, here.y)

    def put_mlp(j):
        def put(total):
            gup_out[:, 256 * j : 256 * j + 256] = total[0:96]
            gdown_out[:, 256 * j : 256 * j + 256] = total[96:192]

        return put

    def put_out(total):
        go_out[0 : 2 * HD] = total[0:96].T
        third = total[96:144].T
        go_out[2 * HD : 3 * HD] = jnp.concatenate([third[0:64], third[64:128]], 1)

    def put_pair(total):
        gq_out[0, 0:80, 0:128] = total[:, 0:128]
        gq_out[1, 0:80, 0:128] = total[:, 128:256]

    def put_pair_rest(total):
        gq_out[0, 80:96, 0:128] = total[0:16, 0:128]
        gq_out[1, 80:96, 0:128] = total[0:16, 128:256]
        gq_out[2, 0:48, 0:128] = total[16:64, 0:128]
        gq_out[2, 48:96, 0:128] = total[16:64, 128:256]

    def put_odd(total):
        gq_out[0, 0:80, 128:192] = total[:, 0:64]
        gq_out[1, 0:80, 128:192] = total[:, 64:128]

    def put_rest(total):
        gq_out[0, 80:96, 128:192] = total[0:16, 0:64]
        gq_out[1, 80:96, 128:192] = total[0:16, 64:128]
        gq_out[2, 0:48, 128:192] = total[16:64, 0:64]
        gq_out[2, 48:96, 128:192] = total[16:64, 64:128]

    grads = (gb, bm0, bm1)
    sets = [m_sets[0:6], m_sets[6:12], m_sets[12:18]]
    start = (0, 0, 0, 0)
    plan = [
        (gb, (0, 192, 0, 256), sets[0], start, put_mlp(0)),
        (bm0, (0, 192, 0, 256), sets[1], start, put_mlp(1)),
        (bm1, (0, 192, 0, 256), sets[2], start, put_mlp(2)),
        (bm2, (0, 144, 0, 128), o_set, start, put_out),
        (gb, (0, 80, 0, 256), sets[0], start, put_pair),
        (gb, (80, 64, 0, 256), sets[0], (80, 48, 32, 0), put_pair_rest),
        (bm2, (0, 80, 128, 128), o_set, (0, 0, 0, 128), put_odd),
        (bm2, (80, 64, 128, 128), o_set, (80, 48, 32, 128), put_rest),
    ]
    scatters = [
        Scatter(
            f"scatter{k}", inner, b, block, slots, place,
            rs_send.at[k], rs_recv.at[k], credit.at[0], out,
        )
        for k, (b, block, slots, place, out) in enumerate(plan)
    ]
    m_sum, o_sum, qa_sum, qd_sum, qb_sum, qc_sum = scatters[0:3], *scatters[3:8]
    q_in, o_in, m_in = gathers[0:3], gathers[3], gathers[4:10]
    early = Total("early", inner, ar, ar_got, ar_send.at[0], ar_recv.at[0])
    late = Total("late", inner, br, br_got, ar_send.at[1], ar_recv.at[1])

    def after(t, last, *steps):
        @pl.when(t == last)
        def _():
            for step in steps:
                step()

    def rows_of(i, size):
        return pl.ds(pl.multiple_of(i * size, size), size)

    def weight(buf, t, r0, rows, columns):
        return buf[t // 2, t % 2, :, :, r0 : r0 + rows, columns].reshape(8 * rows, -1)

    def fold(columns):
        parts = columns.reshape(8, 96, 64)
        halves = [parts[:, 48 * n : 48 * n + 48].reshape(8 * 48, 64) for n in range(2)]
        return jnp.concatenate(halves, 1).astype(BF).reshape(4, 2, 48, 128)

    def cat(ref, s):
        return jnp.concatenate([ref[t, s, :] for t in range(4)], 1)

    def own_copies():
        copies = []
        for j in range(3):
            cols = pl.ds(256 * j, 256)
            copies.append((up_in.at[:, cols], bm[j].at[(*mine, pl.ds(0, 96))]))
            copies.append((down_in.at[:, cols], bm[j].at[(*mine, pl.ds(96, 96))]))
        copies += [(tok_in, tok), (cot_in, cot)]
        return [pltpu.make_async_copy(src, dst, own_sem.at[k]) for k, (src, dst) in enumerate(copies)]

    @phase
    def entry():
        for one in own_copies():
            one.start()
        greet(inner)
        q, k, v = (wq_in[n] for n in range(3))
        for n, one in enumerate((q, k, v)):
            bq[(*mine, slice(None), slice(128 * n, 128 * n + 128))] = one[:, 0:128]
        odd = [one[:, 128:192].astype(F32) for one in (q, k, v)]
        bq[(*mine, slice(None), slice(384, 512))] = jnp.concatenate(odd[0:2], 1).astype(BF)
        params = jnp.concatenate([one[...].astype(F32) for one in (par_a, par_b, par_c, par_d)] + [jnp.zeros((124, 96), F32)], 0).T[:, 0:64]
        bq[(*mine, slice(None), slice(512, 640))] = jnp.concatenate([odd[2], params], 1).astype(BF)
        met(inner)

    @phase
    def document_marks():
        me_t = lax.axis_index("tp")
        row = seg[pl.ds(me_t, 1), :].astype(F32)
        lane_id = lax.broadcasted_iota(jnp.int32, (128, length), 0)
        marks = jnp.where(row == lane_id.astype(F32), 1.0, 0.0)
        marks = jnp.where(lane_id < 8, marks, 0.0)
        low4 = lane_id % 16
        ones = (lane_id >= 8) & (lane_id < 56) & (low4 >= 8) & (low4 < 11)
        marks = jnp.where(ones, 1.0, marks)
        marks = jnp.where(lane_id == 64, valid[...].astype(F32), marks)
        columns = marks.T
        val[...] = columns[:, 64:65]
        kx[...] = jnp.where(lanes() < 64, columns, 0.0).astype(BF)
        ar[0] = jnp.zeros_like(ar.at[0])
        br[0] = jnp.zeros_like(br.at[0])
        g1[...] = jnp.zeros_like(g1)
        count = jnp.sum(valid[...].astype(F32), axis=1, keepdims=True)
        ar[0, 7:8, 0:128] = jnp.broadcast_to(count, (1, 128))
        wide = jnp.concatenate([wo_in[...].astype(F32), jnp.zeros((64, 96), F32)], 0).T
        third = wide[:, 128:192]
        bo[(*mine, slice(0, 96))] = wide[:, 0:128].astype(BF)
        bo[(*mine, slice(96, 144))] = jnp.concatenate([third[0:48], third[48:96]], 1).astype(BF)

    @phase
    def first_norm_statistics():
        @pl.loop(0, length // 256)
        def _(i):
            s = rows_of(i, 256)
            n, mean, scale = stats(tok[s, :].astype(F32))
            mid[s, :] = n
            kept[s, 0:1] = mean
            kept[s, 1:2] = scale

    @phase
    def first_norm():
        par[...] = bq[here.x, here.c, :, :, :, 512:640].reshape(width, 128).astype(F32).T

        @pl.loop(0, length // 256)
        def _(i):
            s = rows_of(i, 256)
            n1[s, :] = (mid[s, :] * par[64:65, :] + par[65:66, :]).astype(BF)

    @phase
    def attention():
        @pl.loop(0, 4)
        def _(n):
            x, c = (here.x + n // 2) % 2, (here.c + n % 2) % 2
            t = 2 * x + c
            w = bq[x, c].reshape(width, 640)

            tt[t] = dot(n1[...], w).astype(BF)

            after(n, 1, m_in[1].s2, m_in[2].s1)
            after(n, 3, m_in[1].s3, m_in[2].s2, m_in[5].s1)
            attend(tt, ll, kx, k2, cc, t, length)
            after(n, 0, *[g.s4 for g in q_in], *[g.near for g in q_in], m_in[0].s2)
            after(n, 1, o_in.s3, m_in[3].s1)
            after(n, 2, m_in[0].s3, *[g.far for g in q_in], m_in[4].s1)
            after(n, 3, o_in.s4, m_in[3].s2, m_in[0].s4, o_in.s5)

    def out_weight(t):
        return jnp.concatenate([weight(bo, t, 0, 96, slice(0, 128)), wo[t]], 1)

    @phase
    def out_projection():
        for t in range(4):
            third = bo[t // 2, t % 2, :, :, 96:144, :].reshape(8, 48, 128)
            turned = pltpu.roll(third.astype(F32).reshape(8 * 48, 128), 64, 1).astype(BF)
            wo[t] = jnp.concatenate([third, turned.reshape(8, 48, 128)], 1).reshape(width, 128)

        @pl.loop(0, length // 256)
        def _(i):
            s = rows_of(i, 256)
            branch = jnp.zeros((256, width), F32)
            for t in range(4):
                branch = branch + dot(cc[t, s, :], out_weight(t), NT)
            v = tok[s, :].astype(F32) + branch
            mid[s, :] = v
            ar[0, 5:6, :] += jnp.sum(val[s, :] * (branch * branch), 0, keepdims=True)
            n, mean, scale = stats(v)
            kept[s, 2:3] = mean
            kept[s, 3:4] = scale
            n2[s, :] = (n * par[66:67, :] + par[67:68, :]).astype(BF)

    def mlp_hidden(j, *steps):
        b = bm[j]

        @phase
        def hidden():
            @pl.loop(0, 4)
            def _(t):
                up = weight(b, t, 0, 96, slice(0, 256))
                down = weight(b, t, 96, 96, slice(0, 256))

                def finish(s, v, ga):
                    v2 = v * v
                    th = jnp.tanh(v * (C0 + C1 * v2))
                    h = 0.5 + 0.5 * th
                    act[t, s, :] = (v * h).astype(BF)
                    slope = h + (0.5 * v) * (1.0 - th * th) * (C0 + (3.0 * C1) * v2)
                    gu[t, s, :] = (ga * slope).astype(BF)

                waiting = None
                for i in range(length // 128):
                    s = slice(128 * i, 128 * i + 128)
                    now = (s, dot(n2[s, :], up), dot(cot[s, :], down))
                    if waiting is not None:
                        finish(*waiting)
                    waiting = now
                finish(*waiting)

                for k, step in enumerate(steps):
                    after(t, k, *step)

        hidden()

    def mlp_sums(j, *steps):
        b = bm[j]

        def wcat(r0):
            return jnp.concatenate([weight(b, t, r0, 96, slice(0, 256)) for t in range(4)], 1)

        @phase
        def sums():
            @pl.loop(0, length // 512)
            def _(i):
                s = rows_of(i, 512)
                one = dot(cat(act, s), wcat(96), NT)
                two = dot(cat(gu, s), wcat(0), NT)
                if j == 0:
                    acc[s, :] = one
                    gn[s, :] = two
                else:
                    acc[s, :] += one
                    gn[s, :] += two
                for k, step in enumerate(steps):
                    after(i, k, *step)

        sums()

    def mlp_weight_grads(j, *steps):
        b = grads[j]

        @phase
        def weight_grads():
            for t in range(4):
                gup = dot(n2[...], gu[t], TN).astype(BF)
                b[t // 2, t % 2, :, :, 0:96, :] = gup.reshape(4, 2, 96, 256)
                gdown = dot(cot[...], act[t], TN).astype(BF)
                b[t // 2, t % 2, :, :, 96:192, :] = gdown.reshape(4, 2, 96, 256)
                for step in steps[t : t + 1]:
                    step()

        weight_grads()

    def store_low():
        return [
            pltpu.make_async_copy(gu.at[k], lo_out.at[:, pl.ds(256 * k, 256)], local_sem.at[k])
            for k in range(width // 256)
        ]

    @phase
    def second_norm_back():
        @pl.loop(0, length // 256)
        def _(i):
            s = rows_of(i, 256)
            v = mid[s, :]
            mlp = acc[s, :]
            out = v + mlp
            weight_rows = val[s, :]
            ar[0, 4:5, :] += jnp.sum(weight_rows * (out * out), 0, keepdims=True)
            ar[0, 6:7, :] += jnp.sum(weight_rows * (mlp * mlp), 0, keepdims=True)
            low_out = out.astype(BF)
            for k in range(width // 256):
                gu[k, s, :] = low_out[:, 256 * k : 256 * k + 256]
            back, g_gain, g_bias = norm_back(v, kept[s, 2:3], kept[s, 3:4], gn[s, :], par[66:67, :])
            ar[0, 2:3, :] += g_gain
            ar[0, 3:4, :] += g_bias
            grad = cot[s, :].astype(F32) + back
            mid[s, :] = grad
            n2[s, :] = grad.astype(BF)

        for one in store_low():
            one.start()

    @phase
    def out_projection_back():
        @pl.loop(0, 4)
        def _(t):
            act[t] = dot(n2[...], out_weight(t)).astype(BF)
            grad = dot(n2[...], cc[t], TN)
            bm2[t // 2, t % 2, :, :, 0:96, 0:128] = grad[:, 0:128].astype(BF).reshape(4, 2, 96, 128)
            bm2[t // 2, t % 2, :, :, 96:144, 0:128] = fold(grad[:, 128:192])

    @phase
    def pair_attention_back():
        @pl.loop(0, 4)
        def _(t):
            attend_back(tt, ll, kx, k2, kt, cc, act, (dk, dv), (0, 1), t, length)
            after(t, 0, o_sum.s2)
            after(t, 1, m_sum[1].s4)

    def early_take_0():
        early.take(0)
        early.run(1)

    def early_take_1():
        early.take(1)
        early.left()

    @phase
    def pair_weight_grads():
        @pl.loop(0, 2)
        def _(x):
            both = jnp.concatenate([tt[2 * x, :, 0:384], tt[2 * x + 1, :, 0:384]], 1)
            grads = dot(n1[...], both, TN).astype(BF)
            for c in range(2):
                grad = grads[:, 384 * c : 384 * c + 384]
                gb[x, c, :, :, 0:96, :] = grad[:, 0:256].reshape(4, 2, 96, 256)
                third = grad[:, 256:384].reshape(4, 2, 96, 128)
                gb[x, c, :, :, 96:144, 0:128] = third[:, :, 0:48]
                gb[x, c, :, :, 96:144, 128:256] = third[:, :, 48:96]

    @phase
    def odd_weight_grads():
        @pl.loop(0, 4)
        def _(t):
            grad = dot(n1[...], tt[t, :, 384:640], TN)
            bm2[t // 2, t % 2, :, :, 0:96, 128:256] = grad[:, 0:128].astype(BF).reshape(4, 2, 96, 128)
            bm2[t // 2, t % 2, :, :, 96:144, 128:256] = fold(grad[:, 128:192])

    @phase
    def odd_attention_back():
        @pl.loop(0, 4)
        def _(t):
            attend_back(tt, ll, kx, k2, kt, cc, act, (dk, dv), (2,), t, length)
            after(t, 0, qa_sum.s2, o_sum.s3, m_sum[2].s4)
            after(t, 1, qd_sum.s2, m_sum[1].s5, early_take_0)
            after(t, 2, qa_sum.s3)
            after(t, 3, o_sum.s4)

    def store_grad():
        return pltpu.make_async_copy(acc, gt_out, local_sem.at[4])

    @phase
    def first_norm_back():
        @pl.loop(0, length // 256)
        def _(i):
            s = rows_of(i, 256)
            w = jnp.concatenate([weight(bq, t, 0, 96, slice(0, 640)) for t in range(4)], 1)
            grad = dot(cat(tt, s), w, NT)
            after(i, 2, qb_sum.s3, qc_sum.s3)
            back, g_gain, g_bias = norm_back(tok[s, :].astype(F32), kept[s, 0:1], kept[s, 1:2], grad, par[64:65, :])
            g1[0:1, :] += g_gain
            g1[1:2, :] += g_bias
            acc[s, :] = mid[s, :] + back
            after(i, 0, qb_sum.s2, qc_sum.s2, qa_sum.s4)
            after(i, 2, qd_sum.s4)

        store_grad().start()
        for k in range(width // 128):
            for n in range(2):
                br[0, 6 * n + k : 6 * n + k + 1, :] = g1[n : n + 1, 128 * k : 128 * k + 128]

    @phase
    def small_results():
        rows = [jnp.concatenate([br[2, 6 * n + k : 6 * n + k + 1, :] for k in range(6)], 1) for n in range(2)]
        sums = jnp.concatenate(rows + [ar[2, 2:8, :]], 0)
        if inner > 1:
            small_out[...] = sums
            return
        share = width // 32
        owner = lax.axis_index("fsdp") * 4 + lax.axis_index("tp")
        moved = pltpu.roll(sums, width - owner * share, 1)
        square = jnp.sum(sums[4:7], axis=1, keepdims=True) / (sums[7:8, 0:1] * width)
        rms = jnp.sqrt(jnp.broadcast_to(square, (3, 128)))
        lane = lanes()
        row = jnp.where(lane == 0, rms[0:1], jnp.where(lane == 1, rms[1:2], rms[2:3]))
        small_out[0:4, :] = moved[0:4, 0:128]
        small_out[4:8, :] = jnp.broadcast_to(row, (4, 128))

    def give(k):
        held = (gq_out, go_out, gup_out, gdown_out, small_out)[k]
        return pltpu.make_async_copy(held, big_outs[k], give_sem.at[k])

    entry()
    q_in[0].s1()
    document_marks()
    for one in own_copies():
        one.wait()
    q_in[1].s1()
    first_norm_statistics()
    q_in[0].s2()
    q_in[2].s1()
    q_in[1].s2()
    q_in[0].s3()
    q_in[2].s2()
    o_in.s1()
    q_in[1].s3()
    m_in[0].s1()
    q_in[2].s3()
    first_norm()
    o_in.s2()
    m_in[1].s1()
    attention()
    out_projection()
    m_in[1].s4()
    m_in[0].s5()
    m_in[1].s5()

    mlp_hidden(0, (), (m_in[2].s3,), (), (m_in[3].s3,))
    m_in[4].s2()
    mlp_weight_grads(0)
    m_sum[0].s1()
    m_in[2].s4()
    m_in[5].s2()
    mlp_sums(0, (m_in[3].s4,))
    m_sum[0].s2()
    m_in[2].s5()
    m_in[3].s5()

    mlp_hidden(1, (), (m_in[4].s3,))
    m_in[0].s6()
    m_in[1].s6()
    mlp_weight_grads(1, lambda: None, m_in[5].s3)
    m_sum[1].s1()
    mlp_sums(1, (m_sum[0].s3,), (m_in[4].s4, m_in[5].s4))
    m_sum[1].s2()
    m_in[4].s5()
    m_in[5].s5()

    mlp_hidden(2)
    m_in[2].s6()
    m_in[3].s6()
    mlp_weight_grads(2)
    m_sum[2].s1()
    m_sum[0].s4()
    mlp_sums(2)
    m_sum[2].s2()
    m_sum[1].s3()
    m_in[4].s6()
    m_in[5].s6()

    second_norm_back()
    early.run(0)
    o_in.s6()
    out_projection_back()
    o_sum.s1()
    m_sum[2].s3()
    m_sum[0].s5()
    m_sum[0].give_credit()
    pair_attention_back()
    pair_weight_grads()
    m_sum[0].take_credit()
    qa_sum.s1()
    qd_sum.s1()
    odd_attention_back()
    odd_weight_grads()
    qb_sum.s1()
    qc_sum.s1()
    qd_sum.s3()
    m_sum[2].s5()
    for g in q_in:
        g.s6()
    give(2).start()
    give(3).start()
    first_norm_back()
    late.run(0)
    early_take_1()
    o_sum.s5()
    give(1).start()
    qb_sum.s4()
    qc_sum.s4()
    late.take(0)
    late.run(1)
    qa_sum.s5()
    qd_sum.s5()
    late.take(1)
    late.left()
    small_results()
    give(4).start()
    qb_sum.s5()
    for one in store_low():
        one.wait()
    store_grad().wait()
    qc_sum.s5()
    give(0).start()
    for k in range(5):
        give(k).wait()


def scatter_slots(rows, columns):
    return [
        pltpu.VMEM((2, 4, 2, rows, columns), BF),
        pltpu.VMEM((4, (rows // 2 + 15) // 16 * 16, columns), BF),
        pltpu.VMEM((4, rows // 2, columns), BF),
        pltpu.VMEM((4, rows, columns), BF),
        pltpu.VMEM((4, rows, columns), BF),
        pltpu.VMEM((3, rows, columns), BF),
    ]


def layer(inner, tokens, cotangent, segments, valid, wq, wo, up, down, *params):
    length, width = tokens.shape
    block = lambda rows, columns: pltpu.VMEM((2, 2, 4, 2, rows, columns), BF)
    small = (8, width) if inner > 1 else (8, 128)
    shapes = [(3, 96, 3 * HD), (3 * HD, 96), (96, width), (96, width), small]
    scratch = [pltpu.VMEM(shape, F32) for shape in shapes]
    scratch += [
        block(96, 640), block(144, 128), block(192, 256), block(192, 256), block(192, 256), block(192, 256),
        pltpu.VMEM((length, width), BF),
        pltpu.VMEM((length, width), BF),
        pltpu.VMEM((length, width), BF),
        pltpu.VMEM((4, length, 640), BF),
        pltpu.VMEM((4, length, 256), BF),
        pltpu.VMEM((4, length, 128), BF),
        pltpu.VMEM((length, 128), BF),
        pltpu.VMEM((length, 128), BF),
        pltpu.VMEM((128, length), BF),
        pltpu.VMEM((4, width, 128), BF),
        pltpu.VMEM((length, width), F32),
        pltpu.VMEM((length, width), BF),
        pltpu.VMEM((length, width), F32),
        pltpu.VMEM((length, width), F32),
        pltpu.VMEM((4, length, 256), BF),
        pltpu.VMEM((4, length, 256), BF),
        pltpu.VMEM((length, 1), F32),
        pltpu.VMEM((length, 4), F32),
        pltpu.VMEM((128, width), F32),
    ]
    scratch += [pltpu.VMEM((length, 128), F32)] * 2
    scratch += [scatter_slots(192, 256) * 3, scatter_slots(144, 256)]
    scratch += [
        pltpu.VMEM((3, 8, width), F32),
        pltpu.VMEM((10, 8, width), F32),
        pltpu.VMEM((3, 16, 128), F32),
        pltpu.VMEM((10, 16, 128), F32),
        pltpu.VMEM((8, width), F32),
        pltpu.SemaphoreType.DMA((10, 3)),
        pltpu.SemaphoreType.DMA((10, 6)),
        pltpu.SemaphoreType.DMA((8, 3)),
        pltpu.SemaphoreType.DMA((8, 5)),
        pltpu.SemaphoreType.REGULAR((1, 6)),
        pltpu.SemaphoreType.DMA((2, 2)),
        pltpu.SemaphoreType.DMA((2, 2)),
        pltpu.SemaphoreType.DMA((5,)),
        pltpu.SemaphoreType.DMA((8,)),
        pltpu.SemaphoreType.DMA((5,)),
    ]
    vmem, anywhere = pl.BlockSpec(memory_space=pltpu.VMEM), pl.BlockSpec(memory_space=pl.ANY)
    return pl.pallas_call(
        partial(kernel, inner, length),
        out_shape=[
            jax.ShapeDtypeStruct((length, width), BF),
            jax.ShapeDtypeStruct((length, width), F32),
        ]
        + [jax.ShapeDtypeStruct(shape, F32) for shape in shapes],
        in_specs=[anywhere, anywhere, vmem, vmem, vmem, vmem, anywhere, anywhere] + [vmem] * 4,
        out_specs=[anywhere] * (2 + len(shapes)),
        scratch_shapes=scratch,
        compiler_params=pltpu.CompilerParams(
            collective_id=0, has_side_effects=True, vmem_limit_bytes=63 * 2**20
        ),
    )(tokens, cotangent, segments, valid, wq, wo, up, down, *params)


def hand_over(arrays, share):
    count = len(arrays)
    pieces = []
    for k, a in enumerate(arrays):
        step = 256 if a.ndim == 2 and a.shape[0] % 256 == 0 else a.shape[0]
        pieces += [(k, start, step) for start in range(0, a.shape[0], step)]
    small = [(share,)] * 4 + [(3,)] if share else []
    shapes = [(a.shape, a.dtype) for a in arrays[: count - 1 if small else count]] + [(cut, F32) for cut in small]
    whole = len(shapes) - len(small)

    def body(*refs):
        came, went = refs[:count], refs[count : count + len(shapes)]
        held = refs[count + len(shapes) : 2 * count + len(shapes)]
        cuts, sems = refs[2 * count + len(shapes) : -1], refs[-1]

        def part(ref, n):
            _, start, step = pieces[n]
            return ref.at[pl.ds(start, step)] if step < ref.shape[0] else ref

        def fetch(n):
            k = pieces[n][0]
            return pltpu.make_async_copy(part(came[k], n), part(held[k], n), sems.at[0, n])

        def put(n):
            k = pieces[n][0]
            return pltpu.make_async_copy(part(held[k], n), part(went[k], n), sems.at[1, n])

        def put_cut(k):
            return pltpu.make_async_copy(cuts[k], went[whole + k], sems.at[1, len(pieces) + k])

        for n in reversed(range(len(pieces))):
            fetch(n).start()
        for n in reversed(range(len(pieces))):
            fetch(n).wait()
            if pieces[n][0] < whole:
                put(n).start()
                continue
            for k, cut in enumerate(small):
                cuts[k][...] = held[whole][k, 0 : cut[0]]
                put_cut(k).start()
        for n in range(len(pieces)):
            if pieces[n][0] < whole:
                put(n).wait()
        for k in range(len(small)):
            put_cut(k).wait()

    anywhere = pl.BlockSpec(memory_space=pltpu.HBM)
    return pl.pallas_call(
        body,
        out_shape=[jax.ShapeDtypeStruct(shape, dtype) for shape, dtype in shapes],
        in_specs=[anywhere] * count,
        out_specs=[anywhere] * len(shapes),
        scratch_shapes=[pltpu.VMEM(a.shape, a.dtype) for a in arrays]
        + [pltpu.VMEM(cut, F32) for cut in small]
        + [pltpu.SemaphoreType.DMA((2, len(pieces) + 5))],
        compiler_params=pltpu.CompilerParams(vmem_limit_bytes=63 * 2**20),
    )(*arrays)


def local(
    tokens, segment_ids, valid, ln1_gain, ln1_bias, w_qkv, w_out, ln2_gain, ln2_bias, w_up, w_down, cotangent
):
    length, width = tokens.shape
    holders = lax.axis_size("fsdp")
    inner = holders // 8
    groups = [[g * inner + i for i in range(inner)] for g in range(8)]

    def widen(block, axis=0):
        if inner == 1:
            return block
        return lax.all_gather(block, "fsdp", axis_index_groups=groups, axis=axis, tiled=True)

    def narrow(block, axis=0):
        if inner == 1:
            return block
        return lax.psum_scatter(
            block, "fsdp", scatter_dimension=axis, axis_index_groups=groups, tiled=True
        )

    params = [widen(one.reshape(1, -1), 1) for one in (ln1_gain, ln1_bias, ln2_gain, ln2_bias)]
    results = layer(
        inner, tokens, cotangent, segment_ids, valid.reshape(1, length),
        widen(w_qkv.transpose(1, 0, 2), 1), widen(w_out, 1), widen(w_up), widen(w_down.T), *params,
    )
    low, grad_tokens, gq, go, gup, gdown, *small = hand_over(results, width // 32 if inner == 1 else 0)
    if inner > 1:
        sums = lax.psum(small[0], "fsdp", axis_index_groups=groups)
        share = width // (holders * lax.axis_size("tp"))
        owner = lax.axis_index("fsdp") * lax.axis_size("tp") + lax.axis_index("tp")
        mine = lax.dynamic_slice_in_dim(sums[0:4], owner * share, share, 1)
        spread = jnp.sqrt(jnp.sum(sums[4:7], axis=1) / (sums[7, 0] * width))
        small = (mine[0], mine[1], mine[2], mine[3], spread)
    return (
        low, grad_tokens, small[0], small[1], narrow(gq, 1).transpose(1, 0, 2), narrow(go, 1),
        small[2], small[3], narrow(gup), narrow(gdown).T, small[4],
    )


def solution(mesh):
    both = ("fsdp", "tp")
    return jax.shard_map(
        local,
        mesh=mesh,
        in_specs=(
            P(both, None), P("fsdp", None), P(both), P("fsdp"), P("fsdp"), P("fsdp", None, "tp"),
            P("tp", "fsdp"), P("fsdp"), P("fsdp"), P("fsdp", "tp"), P("tp", "fsdp"), P(both, None),
        ),
        out_specs=(
            P(both, None), P(both, None), P(both), P(both), P("fsdp", None, "tp"), P("tp", "fsdp"),
            P(both), P(both), P("fsdp", "tp"), P("tp", "fsdp"), P(),
        ),
        check_vma=False,
    )
```
